32 devices in a mesh: groups: 2 (over x), gz: 16 (over z, y, core).
Axes of the slice: x: 2, y: 2, z: 4, core: 2. Of those that a mesh axis runs over, the one named last changes fastest.
Arguments:
- estimate: float32 [16, 512, 256], P(None, 'gz', 'groups'), parts along dimension 2, may hold values from 0 to 2
- frames: int32 [3, 5, 16, 512, 256], P(None, None, 'gz', None, 'groups'), parts along dimension 4, may hold values from 0 to 4095
- phase_index: int32 [3, 5], replicated, may hold values from 0 to 4, each once within a row
- axial_otf: float32 [3, 2, 16], replicated, may hold values from -4 to 4
- row_blur: float32 [3, 128, 128], replicated, may hold values from -0.5 to 0.5
- column_taps: float32 [3, 7], replicated, may hold values from 0.1 to 1
Outputs:
- gradient: float32 [16, 512, 256], P(None, 'gz', 'groups'), parts along dimension 2
The draws below stay inside these ranges and needn't reach their ends.
There are 2 independent parts, one for each index of `groups`. The reference program is written for one: setup_inputs(seed, part) draws one part's arguments, and reference() takes and returns one part's arrays. A program takes and returns all parts, laid end to end along the dimension named above; an argument that names none is the same for every part. Nothing has to cross between parts.
Inputs may be any that keep to these rules, and one draw needn't show every extreme that they name: `phase_index`: for each orientation the 5 frames take every phase step once.
All inputs are finite; a program needn't handle non-finite values.
Results may differ from the reference program's by a relative error of at most 0.0001.
Values sent between devices are 32-bit elements; how exact they have to be, the bound alone decides.
No kernel may reach another device: no remote copies, remote signals or barrier semaphores. Data moves between devices by JAX's collectives and lax.ppermute only.
A program may use at most 64 MiB of HBM per device.

```python
import math
import jax
import jax.numpy as jnp
from jax import lax

TILE_Y = 128
REACH = 3
ORIENT = 3
NPH = 5
NZ = 16
WIDTH_X = 512
COUNT_MAX = 4095


def touch_ends(values, stream_key, low, largest):
    extent = values.shape
    place = [jax.random.randint(jax.random.fold_in(stream_key, axis), (), 0, extent[axis]) for axis in range(len(extent))]
    values = values.at[tuple(place)].set(low)
    longest = extent.index(max(extent))
    place[longest] = (place[longest] + 1) % extent[longest]
    return values.at[tuple(place)].set(largest)


def levels(own_key, dims, pieces, low, largest):
    def one(position, parts):
        draws = jax.random.uniform(jax.random.fold_in(jax.random.fold_in(own_key, 6), position), (parts,), jnp.float32, low / len(pieces), largest / len(pieces))
        return jnp.repeat(jnp.exp(draws), dims[position] // parts).reshape((-1,) + (1,) * (len(dims) - position - 1))

    level = one(*pieces[0])
    for cut in pieces[1:]:
        level = level * one(*cut)
    return level


def scatter_about(key, extent, deviation, most, kind=jnp.bfloat16):
    return jnp.clip(deviation * jax.random.normal(key, extent, jnp.float32), -most, most).astype(kind)


def setup_inputs(seed: int = 0, part: int = 0) -> dict:
    key_list = jax.random.split(jax.random.key(seed), 7)
    part_splits = jax.random.split(jax.random.fold_in(key_list[6], part), 7)
    estimate = jnp.clip(2.0 * jax.random.uniform(part_splits[0], (NZ, WIDTH_X, TILE_Y), jnp.float32) ** levels(part_splits[0], (NZ, WIDTH_X, TILE_Y), ((1, 16),), -0.2, 0.2), 0.0, 2.0)
    frames = touch_ends(jax.random.randint(part_splits[1], (ORIENT, NPH, NZ, WIDTH_X, TILE_Y), 0, COUNT_MAX + 1), jax.random.fold_in(part_splits[1], 1), 0, COUNT_MAX).astype(jnp.int32)
    phase_index = jax.vmap(lambda own: jax.random.permutation(own, NPH))(jax.random.split(key_list[2], ORIENT)).reshape((ORIENT, NPH)).astype(jnp.int32)
    axial_otf = scatter_about(key_list[3], (3, 2, NZ), 0.7, 4.0, jnp.float32)
    row_blur = scatter_about(key_list[4], (3, TILE_Y, TILE_Y), TILE_Y ** -0.5, 0.5, jnp.float32)
    column_taps = jnp.clip(jax.random.uniform(key_list[5], (3, 2 * REACH + 1), jnp.float32, 0.1, 1.0), 0.1, 1.0)
    return dict(estimate=estimate, frames=frames, phase_index=phase_index, axial_otf=axial_otf, row_blur=row_blur, column_taps=column_taps)


pattern_period = 3.7
orient_base = 0.3
data_scale = 1.0 / 1024.0


def matmul(left_side, right_side):
    return jnp.dot(left_side, right_side, preferred_element_type=jnp.float32, precision=lax.Precision.HIGHEST)


def tables(plane_count):
    positions = jnp.arange(plane_count, dtype=jnp.int32)
    wrapped = (positions[:, None] * positions[None, :]) % plane_count
    phase_angle = wrapped.astype(jnp.float32) * (2.0 * math.pi / plane_count)
    return jnp.cos(phase_angle), jnp.sin(phase_angle)


def pattern(orient, harmonic, columns, row_index):
    direction = orient_base + 2.0 * math.pi * orient / 3.0
    lateral_phase = (columns.astype(jnp.float32)[:, None] * math.cos(direction) + row_index.astype(jnp.float32)[None, :] * math.sin(direction)) * (2.0 * math.pi / pattern_period)
    return jnp.cos(harmonic * lateral_phase), jnp.sin(harmonic * lateral_phase)


def axial_forward(flattened, axial_otf, cosine_table, sine_table):
    plane_count = flattened.shape[0]
    cos_part = matmul(cosine_table, flattened)
    sin_part = matmul(sine_table, flattened)
    otf_real = jnp.transpose(axial_otf[:, 0])[:, :, None]
    otf_imag = jnp.transpose(axial_otf[:, 1])[:, :, None]
    real_parts = (otf_real * cos_part[:, None, :] + otf_imag * sin_part[:, None, :]).reshape(plane_count, -1)
    imag_parts = (otf_imag * cos_part[:, None, :] - otf_real * sin_part[:, None, :]).reshape(plane_count, -1)
    return (matmul(cosine_table, real_parts) - matmul(sine_table, imag_parts)) / plane_count


def axial_adjoint(stacked, axial_otf, cosine_table, sine_table):
    plane_count = stacked.shape[0]
    flattened = stacked.reshape(plane_count, -1)
    cos_part = matmul(cosine_table, flattened).reshape(plane_count, 3, -1)
    sin_part = matmul(sine_table, flattened).reshape(plane_count, 3, -1)
    otf_real = jnp.transpose(axial_otf[:, 0])[:, :, None]
    otf_imag = jnp.transpose(axial_otf[:, 1])[:, :, None]
    real_sum = jnp.sum(otf_real * cos_part - otf_imag * sin_part, axis=1)
    imag_sum = -jnp.sum(otf_real * sin_part + otf_imag * cos_part, axis=1)
    return (matmul(cosine_table, real_sum) - matmul(sine_table, imag_sum)) / plane_count


def blur_plane(image_in, harmonic, row_blur, column_taps):
    blur_reach = (column_taps.shape[1] - 1) // 2
    summed = jnp.zeros(image_in.shape, jnp.float32)
    for offset in range(-blur_reach, blur_reach + 1):
        summed = summed + column_taps[harmonic, offset + blur_reach] * jnp.roll(image_in, -offset, axis=1)
    row_count = image_in.shape[2]
    return matmul(summed.reshape(-1, row_count), jnp.transpose(row_blur[harmonic])).reshape(image_in.shape)


def blur_plane_adjoint(image_in, harmonic, row_blur, column_taps):
    blur_reach = (column_taps.shape[1] - 1) // 2
    row_count = image_in.shape[2]
    blurred = matmul(image_in.reshape(-1, row_count), row_blur[harmonic]).reshape(image_in.shape)
    summed = jnp.zeros(image_in.shape, jnp.float32)
    for offset in range(-blur_reach, blur_reach + 1):
        summed = summed + column_taps[harmonic, offset + blur_reach] * jnp.roll(blurred, offset, axis=1)
    return summed


def residual_sums(base_image, cos_images, sin_images, frames, phase_index):
    orients, phases = frames.shape[0], frames.shape[1]
    frame_weight = 1.0 / (orients * phases)
    overall = jnp.zeros(base_image.shape, jnp.float32)
    cos_sums = []
    sin_sums = []
    for orient in range(orients):
        row_cos = [jnp.zeros(base_image.shape, jnp.float32) for pair_index in range(2)]
        row_sin = [jnp.zeros(base_image.shape, jnp.float32) for pair_index in range(2)]
        for phase_step in range(phases):
            phase_angle = phase_index[orient, phase_step].astype(jnp.float32) * (2.0 * math.pi / phases)
            predicted = base_image
            for pair_index in range(2):
                harmonic = pair_index + 1
                predicted = predicted + jnp.cos(harmonic * phase_angle) * cos_images[orient][pair_index] - jnp.sin(harmonic * phase_angle) * sin_images[orient][pair_index]
            measured = frames[orient, phase_step].astype(jnp.float32) * data_scale - 2.0
            residual = (predicted - measured) * frame_weight
            overall = overall + residual
            for pair_index in range(2):
                harmonic = pair_index + 1
                row_cos[pair_index] = row_cos[pair_index] + jnp.cos(harmonic * phase_angle) * residual
                row_sin[pair_index] = row_sin[pair_index] - jnp.sin(harmonic * phase_angle) * residual
        cos_sums.append(row_cos)
        sin_sums.append(row_sin)
    return overall, cos_sums, sin_sums


def reference(estimate, frames, phase_index, axial_otf, row_blur, column_taps):
    plane_count, loop_width, row_count = estimate.shape
    cosine_table, sine_table = tables(plane_count)
    merged = axial_forward(estimate.reshape(plane_count, -1), axial_otf, cosine_table, sine_table)
    band_stack = merged.reshape(plane_count, 3, loop_width, row_count)
    columns = jnp.arange(loop_width, dtype=jnp.int32)
    row_index = jnp.arange(row_count, dtype=jnp.int32)
    base_image = blur_plane(band_stack[:, 0], 0, row_blur, column_taps)
    cos_images = []
    sin_images = []
    patterns = []
    for orient in range(frames.shape[0]):
        row_c = []
        row_s = []
        row_p = []
        for pair_index in range(2):
            harmonic = pair_index + 1
            cos_pattern, sin_pattern = pattern(orient, harmonic, columns, row_index)
            row_p.append((cos_pattern, sin_pattern))
            row_c.append(blur_plane(cos_pattern * band_stack[:, harmonic], harmonic, row_blur, column_taps))
            row_s.append(blur_plane(sin_pattern * band_stack[:, harmonic], harmonic, row_blur, column_taps))
        cos_images.append(row_c)
        sin_images.append(row_s)
        patterns.append(row_p)
    overall, cos_sums, sin_sums = residual_sums(base_image, cos_images, sin_images, frames, phase_index)
    back_list = [blur_plane_adjoint(overall, 0, row_blur, column_taps)]
    for pair_index in range(2):
        harmonic = pair_index + 1
        summed = jnp.zeros(estimate.shape, jnp.float32)
        for orient in range(frames.shape[0]):
            cos_pattern, sin_pattern = patterns[orient][pair_index]
            summed = summed + cos_pattern * blur_plane_adjoint(cos_sums[orient][pair_index], harmonic, row_blur, column_taps)
            summed = summed + sin_pattern * blur_plane_adjoint(sin_sums[orient][pair_index], harmonic, row_blur, column_taps)
        back_list.append(summed)
    stacked = jnp.stack(back_list, axis=1)
    return axial_adjoint(stacked, axial_otf, cosine_table, sine_table).reshape(estimate.shape)
```

```python
import functools
import math

import jax
import jax.numpy as jnp
import numpy as np
from jax import lax
from jax.experimental import pallas as pl
from jax.experimental.pallas import tpu as pltpu
from jax.sharding import PartitionSpec as P

pattern_period = 3.7
orient_base = 0.3
data_scale = 1.0 / 1024.0
PAD = 8


def exact_dot(left_side, right_side):
    return jnp.dot(
        left_side, right_side, preferred_element_type=jnp.float32, precision=lax.Precision.HIGHEST
    )


def split(values):
    high = values.astype(jnp.bfloat16)
    low = (values - high.astype(jnp.float32)).astype(jnp.bfloat16)
    return high, low


def wide(values):
    high, low = split(values)
    return jnp.concatenate([high, low], axis=1)


def weights(matrix):
    row = wide(matrix)
    return jnp.concatenate([row, row], axis=0)


def narrow(product):
    half = product.shape[1] // 2
    return product[:, :half] + product[:, half:]


def wide_dot(left_side, right_side):
    return jnp.dot(left_side, right_side, preferred_element_type=jnp.float32)


def pattern_table(orients, loop_width, row_count):
    columns = np.arange(-PAD, loop_width + PAD) % loop_width
    rows = np.arange(row_count)
    images = []
    for orient in range(orients):
        direction = orient_base + 2.0 * math.pi * orient / 3.0
        phase = (
            columns.astype(np.float32)[:, None] * np.float32(math.cos(direction))
            + rows.astype(np.float32)[None, :] * np.float32(math.sin(direction))
        ) * np.float32(2.0 * math.pi / pattern_period)
        images += [np.cos(phase.astype(np.float64)), np.sin(phase.astype(np.float64))]
    return np.stack(images).astype(np.float32)


def harmonic_of(cos_one, sin_one, harmonic):
    if harmonic == 1:
        return cos_one, sin_one
    return cos_one * cos_one - sin_one * sin_one, 2.0 * (sin_one * cos_one)


def data_kernel(
    phase_ref, taps_ref, frames_hbm, blur_ref, table_hbm, out_ref,
    raw, mixed, left, product, weight, table, sems, table_sem,
):
    orients, phases = frames_hbm.shape[0], frames_hbm.shape[1]
    loop_width = raw.shape[2]
    chunks, bands, width, _ = out_ref.shape
    reach = (taps_ref.shape[1] - 1) // 2
    copies = []
    for orient in range(orients):
        row = []
        for index in range(phases):
            copy = pltpu.make_async_copy(
                frames_hbm.at[orient, index, 0],
                raw.at[orient, phase_ref[orient, index]],
                sems.at[orient, index],
            )
            copy.start()
            row.append(copy)
        copies.append(row)
    table_copy = pltpu.make_async_copy(table_hbm, table, table_sem)
    table_copy.start()
    for band in range(bands):
        weight[band] = weights(blur_ref[band])
    total = bands * 0 + 4 * orients
    c1, c2 = math.cos(2 * math.pi / 5), math.cos(4 * math.pi / 5)
    s1, s2 = math.sin(2 * math.pi / 5), math.sin(4 * math.pi / 5)
    step = 32
    for orient in range(orients):
        for copy in copies[orient]:
            copy.wait()

        def mix(index, carry):
            rows = pl.ds(pl.multiple_of(index * step, step), step)
            at = pl.ds(pl.multiple_of(index * step + PAD, 8), step)
            f0, f1, f2, f3, f4 = [raw[orient, k, rows, :] for k in range(5)]
            zero = f0.astype(jnp.float32) * data_scale - 2.0
            near = (f1 + f4).astype(jnp.float32) * data_scale - 4.0
            far = (f2 + f3).astype(jnp.float32) * data_scale - 4.0
            near_odd = (f1 - f4).astype(jnp.float32) * data_scale
            far_odd = (f2 - f3).astype(jnp.float32) * data_scale
            mixed[4 * orient, at, :] = zero + c1 * near + c2 * far
            mixed[4 * orient + 1, at, :] = s1 * near_odd + s2 * far_odd
            mixed[4 * orient + 2, at, :] = zero + c2 * near + c1 * far
            mixed[4 * orient + 3, at, :] = s2 * near_odd - s1 * far_odd
            plain = zero + near + far
            if orient:
                plain = plain + mixed[total, at, :]
            mixed[total, at, :] = plain
            return carry

        lax.fori_loop(0, loop_width // step, mix, 0)
    for image in range(total + 1):
        mixed[image, PAD - reach : PAD, :] = mixed[
            image, loop_width + PAD - reach : loop_width + PAD, :
        ]
        mixed[image, loop_width + PAD : loop_width + PAD + reach, :] = mixed[
            image, PAD : PAD + reach, :
        ]
    table_copy.wait()

    def blur(image, band, slot):
        scaled = [
            taps_ref[band, offset + reach] * (1.0 / (orients * phases))
            for offset in range(-reach, reach + 1)
        ]

        def one(index, carry):
            begin = index * step + PAD
            acc = None
            for offset in range(-reach, reach + 1):
                term = scaled[offset + reach] * mixed[image, pl.ds(begin - offset, step), :]
                acc = term if acc is None else acc + term
            to = pl.multiple_of(index * step + slot * loop_width, step)
            left[pl.ds(to, step), :] = wide(acc)
            return carry

        lax.fori_loop(0, loop_width // step, one, 0)

    blur(total, 0, 0)
    product[0:loop_width, :] = wide_dot(left[0:loop_width, :], weight[0])

    block = max(width, 8)
    shares = block // width

    def store(index, band, values):
        for share in range(shares):
            out_ref[index * shares + share, band] = values[share * width : (share + 1) * width]

    def plain_out(index, carry):
        begin = pl.multiple_of(index * block, block)
        store(index, 0, narrow(product[pl.ds(begin, block), :]))
        return carry

    lax.fori_loop(0, loop_width // block, plain_out, 0)
    for band in range(1, bands):
        for orient in range(orients):
            blur(4 * orient + 2 * band - 2, band, 2 * orient)
            blur(4 * orient + 2 * band - 1, band, 2 * orient + 1)
        rows = 2 * orients * loop_width
        product[0:rows, :] = wide_dot(left[0:rows, :], weight[band])

        def band_out(index, carry):
            begin = pl.multiple_of(index * block, block)
            at = pl.ds(begin + PAD, block)
            acc = None
            for orient in range(orients):
                cos_pattern, sin_pattern = harmonic_of(
                    table[2 * orient, at, :], table[2 * orient + 1, at, :], band
                )
                even = narrow(product[pl.ds(begin + 2 * orient * loop_width, block), :])
                odd = narrow(product[pl.ds(begin + (2 * orient + 1) * loop_width, block), :])
                term = cos_pattern * even - sin_pattern * odd
                acc = term if acc is None else acc + term
            store(index, band, acc)
            return carry

        lax.fori_loop(0, loop_width // block, band_out, 0)


def data_sums(frames, phase_index, row_blur, column_taps, table, chunks):
    orients, phases, _, loop_width, row_count = frames.shape
    bands = row_blur.shape[0]
    width = loop_width // chunks
    smem = pl.BlockSpec(memory_space=pltpu.SMEM)
    vmem = pl.BlockSpec(memory_space=pltpu.VMEM)
    anywhere = pl.BlockSpec(memory_space=pltpu.HBM)
    images = 4 * orients + 1
    return pl.pallas_call(
        data_kernel,
        out_shape=jax.ShapeDtypeStruct((chunks, bands, width, row_count), jnp.float32),
        in_specs=[smem, smem, anywhere, vmem, anywhere],
        out_specs=vmem,
        scratch_shapes=[
            pltpu.VMEM((orients, phases, loop_width, row_count), jnp.int32),
            pltpu.VMEM((images, loop_width + 2 * PAD, row_count), jnp.float32),
            pltpu.VMEM((2 * orients * loop_width, 2 * row_count), jnp.bfloat16),
            pltpu.VMEM((2 * orients * loop_width, 2 * row_count), jnp.float32),
            pltpu.VMEM((bands, 2 * row_count, 2 * row_count), jnp.bfloat16),
            pltpu.VMEM(table.shape, jnp.float32),
            pltpu.SemaphoreType.DMA((orients, phases)),
            pltpu.SemaphoreType.DMA,
        ],
        cost_estimate=pl.CostEstimate(
            flops=13 * loop_width * 2 * 256 * 256, bytes_accessed=frames.size * 4, transcendentals=0
        ),
        compiler_params=pltpu.CompilerParams(vmem_limit_bytes=40 << 20),
        name="data_sums",
    )(phase_index, column_taps, frames, row_blur, table)


def estimate_kernel(taps_ref, axial_ref, table_ref, blur_ref, out_ref, mod, left, product):
    bands, extended, planes, row_count = axial_ref.shape
    width = out_ref.shape[0]
    orients = table_ref.shape[0] // 2
    reach = (taps_ref.shape[1] - 1) // 2
    span = 2 * reach
    assert extended == width + 2 * span
    step = 4
    gain = (0.5 / orients, 0.5 / orients)

    def chain(band, scale):
        return [
            scale
            * sum(
                taps_ref[band, d] * taps_ref[band, d + shift]
                for d in range(0, 2 * reach + 1 - shift)
            )
            for shift in range(span + 1)
        ]

    def filtered(source, lags, slot):
        def one(index, carry):
            begin = index * step
            loaded = [source[begin + i] for i in range(step + 2 * span)]
            for i in range(step):
                acc = lags[0] * loaded[i + span]
                for shift in range(1, span + 1):
                    acc = acc + lags[shift] * (loaded[i + span - shift] + loaded[i + span + shift])
                to = pl.multiple_of(slot * width * planes + (begin + i) * planes, 16)
                left[pl.ds(to, planes), :] = wide(acc)
            return carry

        lax.fori_loop(0, width // step, one, 0)

    def weight_of(band):
        matrix = blur_ref[band]
        return weights(
            lax.dot_general(
                matrix,
                matrix,
                (((0,), (0,)), ((), ())),
                preferred_element_type=jnp.float32,
                precision=lax.Precision.HIGHEST,
            )
        )

    count = width * planes
    filtered(axial_ref.at[0], chain(0, 1.0), 0)
    product[0:count, :] = wide_dot(left[0:count, :], weight_of(0))

    def first(index, carry):
        out_ref[index] = narrow(
            product[pl.ds(pl.multiple_of(index * planes, planes), planes), :]
        )
        return carry

    lax.fori_loop(0, width, first, 0)
    for band in range(1, bands):
        lags = chain(band, gain[band - 1])
        for orient in range(orients):
            for part in range(2):

                def modulate(index, carry):
                    patterns = harmonic_of(
                        table_ref[2 * orient, pl.ds(index, 1), :],
                        table_ref[2 * orient + 1, pl.ds(index, 1), :],
                        band,
                    )
                    mod[index] = patterns[part] * axial_ref[band, index]
                    return carry

                lax.fori_loop(0, extended, modulate, 0, unroll=4)
                filtered(mod, lags, 2 * orient + part)
        rows = 2 * orients * count
        product[0:rows, :] = wide_dot(left[0:rows, :], weight_of(band))

        def collect(index, carry):
            acc = out_ref[index]
            for orient in range(orients):
                patterns = harmonic_of(
                    table_ref[2 * orient, pl.ds(index + span, 1), :],
                    table_ref[2 * orient + 1, pl.ds(index + span, 1), :],
                    band,
                )
                for part in range(2):
                    begin = (2 * orient + part) * count + index * planes
                    acc = acc + patterns[part] * narrow(
                        product[pl.ds(pl.multiple_of(begin, planes), planes), :]
                    )
            out_ref[index] = acc
            return carry

        lax.fori_loop(0, width, collect, 0)


def estimate_part(axial, table, row_blur, column_taps, width):
    bands, _, planes, row_count = axial.shape
    orients = table.shape[0] // 2
    smem = pl.BlockSpec(memory_space=pltpu.SMEM)
    vmem = pl.BlockSpec(memory_space=pltpu.VMEM)
    rows = 2 * orients * width * planes
    return pl.pallas_call(
        estimate_kernel,
        out_shape=jax.ShapeDtypeStruct((width, planes, row_count), jnp.float32),
        in_specs=[smem, vmem, vmem, vmem],
        out_specs=vmem,
        scratch_shapes=[
            pltpu.VMEM(axial.shape[1:], jnp.float32),
            pltpu.VMEM((rows, 2 * row_count), jnp.bfloat16),
            pltpu.VMEM((rows, 2 * row_count), jnp.float32),
        ],
        cost_estimate=pl.CostEstimate(
            flops=40 * rows * 2 * 256 * 256, bytes_accessed=axial.size * 4, transcendentals=0
        ),
        compiler_params=pltpu.CompilerParams(vmem_limit_bytes=40 << 20),
        name="estimate_part",
    )(column_taps, axial, table, row_blur)


def halo(estimate, span):
    ring = lax.axis_size("gz")
    width = estimate.shape[1]
    lefts, rights = [], []
    hop, missing = 1, span
    while missing > 0:
        take = min(missing, width)
        lefts.insert(
            0,
            lax.ppermute(
                estimate[:, width - take :], "gz", [(s, (s + hop) % ring) for s in range(ring)]
            ),
        )
        rights.append(
            lax.ppermute(estimate[:, :take], "gz", [(s, (s - hop) % ring) for s in range(ring)])
        )
        missing -= take
        hop += 1
    return jnp.concatenate(lefts + [estimate] + rights, axis=1)


def axial_matrices(axial_otf, planes):
    wrapped = np.arange(planes)[:, None] * np.arange(planes)[None, :] % planes
    angle = wrapped * (2.0 * math.pi / planes)
    cosine = np.cos(angle).astype(np.float32)
    sine = np.sin(angle).astype(np.float32)
    real = axial_otf[:, 0, :, None]
    imag = axial_otf[:, 1, :, None]
    inner = jnp.concatenate(
        [real * cosine + imag * sine, real * sine - imag * cosine], axis=1
    )
    both = np.concatenate([cosine, sine], axis=1) / planes
    return jnp.einsum(
        "zk,mkw->mzw", both, inner, precision=lax.Precision.HIGHEST,
        preferred_element_type=jnp.float32,
    )


def shards(estimate, frames, phase_index, axial_otf, row_blur, column_taps):
    planes, width, row_count = estimate.shape
    ring = lax.axis_size("gz")
    orients = frames.shape[0]
    bands = row_blur.shape[0]
    span = column_taps.shape[1] - 1
    table = jnp.asarray(pattern_table(orients, width * ring, row_count))
    extended = halo(estimate, span)
    sums = data_sums(frames, phase_index, row_blur, column_taps, table, ring)
    received = lax.all_to_all(sums, "gz", 0, 0, tiled=True)
    forward = axial_matrices(axial_otf, planes)
    squared = jnp.einsum("mzw,mzv->mwv", forward, forward, precision=lax.Precision.HIGHEST)
    axial = exact_dot(squared.reshape(bands * planes, planes), extended.reshape(planes, -1))
    axial = axial.reshape(bands, planes, width + 2 * span, row_count).transpose(0, 2, 1, 3)
    begin = lax.axis_index("gz") * width + (PAD - span)
    near = lax.dynamic_slice_in_dim(table, begin, width + 2 * span, axis=1)
    from_estimate = estimate_part(axial, near, row_blur, column_taps, width)
    adjoint = forward.transpose(2, 1, 0).reshape(planes, planes * bands)
    from_data = exact_dot(adjoint, received.reshape(planes * bands, width * row_count))
    return from_estimate.transpose(1, 0, 2) - from_data.reshape(estimate.shape)


def solution(mesh):
    placed = (P(None, "gz", "groups"), P(None, None, "gz", None, "groups"), P(), P(), P(), P())
    return jax.shard_map(
        shards, mesh=mesh, in_specs=placed, out_specs=P(None, "gz", "groups"), check_vma=False
    )
```

```python
import functools
import math

import jax
import jax.numpy as jnp
import numpy as np
from jax import lax
from jax.experimental import pallas as pl
from jax.experimental.pallas import tpu as pltpu
from jax.sharding import PartitionSpec as P

pattern_period = 3.7
orient_base = 0.3
data_scale = 1.0 / 1024.0
PAD = 8


def exact_dot(left_side, right_side):
    return jnp.dot(
        left_side, right_side, preferred_element_type=jnp.float32, precision=lax.Precision.HIGHEST
    )


def split(values):
    high = values.astype(jnp.bfloat16)
    low = (values - high.astype(jnp.float32)).astype(jnp.bfloat16)
    return high, low


def wide(values):
    high, low = split(values)
    return jnp.concatenate([high, low], axis=1)


def weights(matrix):
    row = wide(matrix)
    return jnp.concatenate([row, row], axis=0)


def narrow(product):
    half = product.shape[1] // 2
    return product[:, :half] + product[:, half:]


def wide_dot(left_side, right_side):
    return jnp.dot(left_side, right_side, preferred_element_type=jnp.float32)


def pattern_table(orients, loop_width, row_count):
    columns = np.arange(-PAD, loop_width + PAD) % loop_width
    rows = np.arange(row_count)
    images = []
    for orient in range(orients):
        direction = orient_base + 2.0 * math.pi * orient / 3.0
        phase = (
            columns.astype(np.float32)[:, None] * np.float32(math.cos(direction))
            + rows.astype(np.float32)[None, :] * np.float32(math.sin(direction))
        ) * np.float32(2.0 * math.pi / pattern_period)
        images += [np.cos(phase.astype(np.float64)), np.sin(phase.astype(np.float64))]
    return np.stack(images).astype(np.float32)


def harmonic_of(cos_one, sin_one, harmonic):
    if harmonic == 1:
        return cos_one, sin_one
    return cos_one * cos_one - sin_one * sin_one, 2.0 * (sin_one * cos_one)


def data_kernel(
    phase_ref, taps_ref, frames_hbm, blur_hbm, table_hbm, out_ref,
    raw, mixed, left, product, weight, table, blur_rows, sems, side_sems,
):
    orients, phases = frames_hbm.shape[0], frames_hbm.shape[1]
    loop_width = raw.shape[2]
    chunks, bands, width, _ = out_ref.shape
    reach = (taps_ref.shape[1] - 1) // 2
    copies = []
    for orient in range(orients):
        row = []
        for index in range(phases):
            copy = pltpu.make_async_copy(
                frames_hbm.at[orient, index, 0],
                raw.at[orient, index],
                sems.at[orient, index],
            )
            copy.start()
            row.append(copy)
        copies.append(row)
    blur_copy = pltpu.make_async_copy(blur_hbm, blur_rows, side_sems.at[0])
    blur_copy.start()
    table_copy = pltpu.make_async_copy(table_hbm, table, side_sems.at[1])
    table_copy.start()
    total = bands * 0 + 4 * orients
    c1, c2 = math.cos(2 * math.pi / 5), math.cos(4 * math.pi / 5)
    s1, s2 = math.sin(2 * math.pi / 5), math.sin(4 * math.pi / 5)
    step = 32
    for orient in range(orients):
        holder = []
        for step_index in range(phases):
            at_step = 0
            for index in range(1, phases):
                at_step = jnp.where(phase_ref[orient, index] == step_index, index, at_step)
            holder.append(at_step)
        for copy in copies[orient]:
            copy.wait()

        def mix(index, carry):
            rows = pl.ds(pl.multiple_of(index * step, step), step)
            at = pl.ds(pl.multiple_of(index * step + PAD, 8), step)
            f0, f1, f2, f3, f4 = [raw[orient, k, rows, :] for k in holder]
            zero = f0.astype(jnp.float32) * data_scale - 2.0
            near = (f1 + f4).astype(jnp.float32) * data_scale - 4.0
            far = (f2 + f3).astype(jnp.float32) * data_scale - 4.0
            near_odd = (f1 - f4).astype(jnp.float32) * data_scale
            far_odd = (f2 - f3).astype(jnp.float32) * data_scale
            mixed[4 * orient, at, :] = zero + c1 * near + c2 * far
            mixed[4 * orient + 1, at, :] = s1 * near_odd + s2 * far_odd
            mixed[4 * orient + 2, at, :] = zero + c2 * near + c1 * far
            mixed[4 * orient + 3, at, :] = s2 * near_odd - s1 * far_odd
            plain = zero + near + far
            if orient:
                plain = plain + mixed[total, at, :]
            mixed[total, at, :] = plain
            return carry

        lax.fori_loop(0, loop_width // step, mix, 0)
    for image in range(total + 1):
        mixed[image, PAD - reach : PAD, :] = mixed[
            image, loop_width + PAD - reach : loop_width + PAD, :
        ]
        mixed[image, loop_width + PAD : loop_width + PAD + reach, :] = mixed[
            image, PAD : PAD + reach, :
        ]
    blur_copy.wait()
    for band in range(bands):
        weight[band] = weights(blur_rows[band])
    table_copy.wait()

    def blur(image, band, slot):
        scaled = [
            taps_ref[band, offset + reach] * (1.0 / (orients * phases))
            for offset in range(-reach, reach + 1)
        ]

        def one(index, carry):
            begin = index * step + PAD
            acc = None
            for offset in range(-reach, reach + 1):
                term = scaled[offset + reach] * mixed[image, pl.ds(begin - offset, step), :]
                acc = term if acc is None else acc + term
            to = pl.multiple_of(index * step + slot * loop_width, step)
            left[pl.ds(to, step), :] = wide(acc)
            return carry

        lax.fori_loop(0, loop_width // step, one, 0)

    blur(total, 0, 0)
    product[0:loop_width, :] = wide_dot(left[0:loop_width, :], weight[0])

    block = max(width, 8)
    shares = block // width

    def store(index, band, values):
        for share in range(shares):
            out_ref[index * shares + share, band] = values[share * width : (share + 1) * width]

    def plain_out(index, carry):
        begin = pl.multiple_of(index * block, block)
        store(index, 0, narrow(product[pl.ds(begin, block), :]))
        return carry

    lax.fori_loop(0, loop_width // block, plain_out, 0)
    for band in range(1, bands):
        for orient in range(orients):
            blur(4 * orient + 2 * band - 2, band, 2 * orient)
            blur(4 * orient + 2 * band - 1, band, 2 * orient + 1)
        rows = 2 * orients * loop_width
        product[0:rows, :] = wide_dot(left[0:rows, :], weight[band])

        def band_out(index, carry):
            begin = pl.multiple_of(index * block, block)
            at = pl.ds(begin + PAD, block)
            acc = None
            for orient in range(orients):
                cos_pattern, sin_pattern = harmonic_of(
                    table[2 * orient, at, :], table[2 * orient + 1, at, :], band
                )
                even = narrow(product[pl.ds(begin + 2 * orient * loop_width, block), :])
                odd = narrow(product[pl.ds(begin + (2 * orient + 1) * loop_width, block), :])
                term = cos_pattern * even - sin_pattern * odd
                acc = term if acc is None else acc + term
            store(index, band, acc)
            return carry

        lax.fori_loop(0, loop_width // block, band_out, 0)


def data_sums(frames, phase_index, row_blur, column_taps, table, chunks):
    orients, phases, _, loop_width, row_count = frames.shape
    bands = row_blur.shape[0]
    width = loop_width // chunks
    smem = pl.BlockSpec(memory_space=pltpu.SMEM)
    vmem = pl.BlockSpec(memory_space=pltpu.VMEM)
    anywhere = pl.BlockSpec(memory_space=pltpu.HBM)
    images = 4 * orients + 1
    return pl.pallas_call(
        data_kernel,
        out_shape=jax.ShapeDtypeStruct((chunks, bands, width, row_count), jnp.float32),
        in_specs=[smem, smem, anywhere, anywhere, anywhere],
        out_specs=vmem,
        scratch_shapes=[
            pltpu.VMEM((orients, phases, loop_width, row_count), jnp.int32),
            pltpu.VMEM((images, loop_width + 2 * PAD, row_count), jnp.float32),
            pltpu.VMEM((2 * orients * loop_width, 2 * row_count), jnp.bfloat16),
            pltpu.VMEM((2 * orients * loop_width, 2 * row_count), jnp.float32),
            pltpu.VMEM((bands, 2 * row_count, 2 * row_count), jnp.bfloat16),
            pltpu.VMEM(table.shape, jnp.float32),
            pltpu.VMEM(row_blur.shape, jnp.float32),
            pltpu.SemaphoreType.DMA((orients, phases)),
            pltpu.SemaphoreType.DMA((2,)),
        ],
        cost_estimate=pl.CostEstimate(
            flops=13 * loop_width * 2 * 256 * 256, bytes_accessed=frames.size * 4, transcendentals=0
        ),
        compiler_params=pltpu.CompilerParams(vmem_limit_bytes=63 << 20),
        name="data_sums",
    )(phase_index, column_taps, frames, row_blur, table)


def estimate_kernel(taps_ref, axial_ref, table_ref, blur_ref, out_ref, mod, left, product):
    bands, extended, planes, row_count = axial_ref.shape
    width = out_ref.shape[0] // planes
    orients = table_ref.shape[0] // 2
    reach = (taps_ref.shape[1] - 1) // 2
    span = 2 * reach
    assert extended == width + 2 * span
    step = 4
    gain = (0.5 / orients, 0.5 / orients)

    def chain(band, scale):
        return [
            scale
            * sum(
                taps_ref[band, d] * taps_ref[band, d + shift]
                for d in range(0, 2 * reach + 1 - shift)
            )
            for shift in range(span + 1)
        ]

    def filtered(source, lags, slot):
        def one(index, carry):
            begin = index * step
            loaded = [source[begin + i] for i in range(step + 2 * span)]
            for i in range(step):
                acc = lags[0] * loaded[i + span]
                for shift in range(1, span + 1):
                    acc = acc + lags[shift] * (loaded[i + span - shift] + loaded[i + span + shift])
                to = pl.multiple_of(slot * width * planes + (begin + i) * planes, 16)
                left[pl.ds(to, planes), :] = wide(acc)
            return carry

        lax.fori_loop(0, width // step, one, 0)

    def weight_of(band):
        matrix = blur_ref[band]
        return weights(
            lax.dot_general(
                matrix,
                matrix,
                (((0,), (0,)), ((), ())),
                preferred_element_type=jnp.float32,
                precision=lax.Precision.HIGHEST,
            )
        )

    count = width * planes
    filtered(axial_ref.at[0], chain(0, 1.0), 0)
    product[0:count, :] = wide_dot(left[0:count, :], weight_of(0))

    def first(index, carry):
        out_ref[pl.ds(index, planes, stride=width), :] = narrow(
            product[pl.ds(pl.multiple_of(index * planes, planes), planes), :]
        )
        return carry

    lax.fori_loop(0, width, first, 0)
    for band in range(1, bands):
        lags = chain(band, gain[band - 1])
        for orient in range(orients):
            for part in range(2):

                def modulate(index, carry):
                    patterns = harmonic_of(
                        table_ref[2 * orient, pl.ds(index, 1), :],
                        table_ref[2 * orient + 1, pl.ds(index, 1), :],
                        band,
                    )
                    mod[index] = patterns[part] * axial_ref[band, index]
                    return carry

                lax.fori_loop(0, extended, modulate, 0, unroll=4)
                filtered(mod, lags, 2 * orient + part)
        rows = 2 * orients * count
        product[0:rows, :] = wide_dot(left[0:rows, :], weight_of(band))

        def collect(index, carry):
            acc = out_ref[pl.ds(index, planes, stride=width), :]
            for orient in range(orients):
                patterns = harmonic_of(
                    table_ref[2 * orient, pl.ds(index + span, 1), :],
                    table_ref[2 * orient + 1, pl.ds(index + span, 1), :],
                    band,
                )
                for part in range(2):
                    begin = (2 * orient + part) * count + index * planes
                    acc = acc + patterns[part] * narrow(
                        product[pl.ds(pl.multiple_of(begin, planes), planes), :]
                    )
            out_ref[pl.ds(index, planes, stride=width), :] = acc
            return carry

        lax.fori_loop(0, width, collect, 0)


def estimate_part(axial, table, row_blur, column_taps, width):
    bands, _, planes, row_count = axial.shape
    orients = table.shape[0] // 2
    smem = pl.BlockSpec(memory_space=pltpu.SMEM)
    vmem = pl.BlockSpec(memory_space=pltpu.VMEM)
    rows = 2 * orients * width * planes
    return pl.pallas_call(
        estimate_kernel,
        out_shape=jax.ShapeDtypeStruct((planes * width, row_count), jnp.float32),
        in_specs=[smem, vmem, vmem, vmem],
        out_specs=vmem,
        scratch_shapes=[
            pltpu.VMEM(axial.shape[1:], jnp.float32),
            pltpu.VMEM((rows, 2 * row_count), jnp.bfloat16),
            pltpu.VMEM((rows, 2 * row_count), jnp.float32),
        ],
        cost_estimate=pl.CostEstimate(
            flops=40 * rows * 2 * 256 * 256, bytes_accessed=axial.size * 4, transcendentals=0
        ),
        compiler_params=pltpu.CompilerParams(vmem_limit_bytes=40 << 20),
        name="estimate_part",
    )(column_taps, axial, table, row_blur)


def halo(estimate, span):
    ring = lax.axis_size("gz")
    width = estimate.shape[1]
    lefts, rights = [], []
    hop, missing = 1, span
    while missing > 0:
        take = min(missing, width)
        lefts.insert(
            0,
            lax.ppermute(
                estimate[:, width - take :], "gz", [(s, (s + hop) % ring) for s in range(ring)]
            ),
        )
        rights.append(
            lax.ppermute(estimate[:, :take], "gz", [(s, (s - hop) % ring) for s in range(ring)])
        )
        missing -= take
        hop += 1
    return jnp.concatenate(lefts + [estimate] + rights, axis=1)


def axial_matrices(axial_otf, planes):
    wrapped = np.arange(planes)[:, None] * np.arange(planes)[None, :] % planes
    angle = wrapped * (2.0 * math.pi / planes)
    cosine = np.cos(angle).astype(np.float32)
    sine = np.sin(angle).astype(np.float32)
    real = axial_otf[:, 0, :, None]
    imag = axial_otf[:, 1, :, None]
    inner = jnp.concatenate(
        [real * cosine + imag * sine, real * sine - imag * cosine], axis=1
    )
    both = np.concatenate([cosine, sine], axis=1) / planes
    return jnp.einsum(
        "zk,mkw->mzw", both, inner, precision=lax.Precision.HIGHEST,
        preferred_element_type=jnp.float32,
    )


def shards(estimate, frames, phase_index, axial_otf, row_blur, column_taps):
    planes, width, row_count = estimate.shape
    ring = lax.axis_size("gz")
    orients = frames.shape[0]
    bands = row_blur.shape[0]
    span = column_taps.shape[1] - 1
    table = jnp.asarray(pattern_table(orients, width * ring, row_count))
    extended = halo(estimate, span)
    sums = data_sums(frames, phase_index, row_blur, column_taps, table, ring)
    received = lax.all_to_all(sums, "gz", 0, 0, tiled=True)
    forward = axial_matrices(axial_otf, planes)
    squared = jnp.einsum("mzw,mzv->mwv", forward, forward, precision=lax.Precision.HIGHEST)
    axial = exact_dot(squared.reshape(bands * planes, planes), extended.reshape(planes, -1))
    axial = axial.reshape(bands, planes, width + 2 * span, row_count).transpose(0, 2, 1, 3)
    begin = lax.axis_index("gz") * width + (PAD - span)
    near = lax.dynamic_slice_in_dim(table, begin, width + 2 * span, axis=1)
    from_estimate = estimate_part(axial, near, row_blur, column_taps, width)
    adjoint = forward.transpose(2, 1, 0).reshape(planes, planes * bands)
    from_data = exact_dot(adjoint, received.reshape(planes * bands, width * row_count))
    return from_estimate.reshape(estimate.shape) - from_data.reshape(estimate.shape)


def solution(mesh):
    placed = (P(None, "gz", "groups"), P(None, None, "gz", None, "groups"), P(), P(), P(), P())
    return jax.shard_map(
        shards, mesh=mesh, in_specs=placed, out_specs=P(None, "gz", "groups"), check_vma=False
    )
```

```python
import math

import jax
import jax.numpy as jnp
import numpy as np
from jax import lax
from jax.experimental import pallas as pl
from jax.experimental.pallas import tpu as pltpu
from jax.sharding import PartitionSpec as P


pattern_period = 3.7
orient_base = 0.3
data_scale = 1.0 / 1024.0
PAD = 8


def exact_dot(left_side, right_side):
    return jnp.dot(
        left_side, right_side, preferred_element_type=jnp.float32, precision=lax.Precision.HIGHEST
    )


def split(values):
    high = values.astype(jnp.bfloat16)
    low = (values - high.astype(jnp.float32)).astype(jnp.bfloat16)
    return high, low


def wide(values):
    high, low = split(values)
    return jnp.concatenate([high, low], axis=1)


def weights(matrix):
    row = wide(matrix)
    return jnp.concatenate([row, row], axis=0)


def narrow(product):
    half = product.shape[1] // 2
    return product[:, :half] + product[:, half:]


def wide_dot(left_side, right_side):
    return jnp.dot(left_side, right_side, preferred_element_type=jnp.float32)


def pattern_table(orients, loop_width, row_count):
    columns = np.arange(-PAD, loop_width + PAD) % loop_width
    rows = np.arange(row_count)
    images = []
    for orient in range(orients):
        direction = orient_base + 2.0 * math.pi * orient / 3.0
        phase = (
            columns.astype(np.float32)[:, None] * np.float32(math.cos(direction))
            + rows.astype(np.float32)[None, :] * np.float32(math.sin(direction))
        ) * np.float32(2.0 * math.pi / pattern_period)
        images += [np.cos(phase.astype(np.float64)), np.sin(phase.astype(np.float64))]
    return np.stack(images).astype(np.float32)


def harmonic_of(cos_one, sin_one, harmonic):
    if harmonic == 1:
        return cos_one, sin_one
    return cos_one * cos_one - sin_one * sin_one, 2.0 * (sin_one * cos_one)


def data_kernel(
    phase_ref, taps_ref, frames_hbm, blur_hbm, table_hbm, out_ref,
    raw, mixed, weight, table, blur_rows, sems, side_sems,
):
    orients, phases = frames_hbm.shape[0], frames_hbm.shape[1]
    loop_width = raw.shape[2]
    _, bands, width, _ = out_ref.shape
    reach = (taps_ref.shape[1] - 1) // 2
    copies = []
    for orient in range(orients):
        row = []
        for index in range(phases):
            copy = pltpu.make_async_copy(
                frames_hbm.at[orient, index, 0],
                raw.at[orient, index],
                sems.at[orient, index],
            )
            copy.start()
            row.append(copy)
        copies.append(row)
    blur_copy = pltpu.make_async_copy(blur_hbm, blur_rows, side_sems.at[0])
    blur_copy.start()
    table_copy = pltpu.make_async_copy(table_hbm, table, side_sems.at[1])
    table_copy.start()
    total = bands * 0 + 4 * orients
    c1, c2 = math.cos(2 * math.pi / 5), math.cos(4 * math.pi / 5)
    s1, s2 = math.sin(2 * math.pi / 5), math.sin(4 * math.pi / 5)
    step = max(64, width)
    for orient in range(orients):
        holder = []
        for step_index in range(phases):
            at_step = 0
            for index in range(1, phases):
                at_step = jnp.where(phase_ref[orient, index] == step_index, index, at_step)
            holder.append(at_step)
        for copy in copies[orient]:
            copy.wait()

        def mix(index, carry):
            rows = pl.ds(pl.multiple_of(index * step, step), step)
            at = pl.ds(pl.multiple_of(index * step + PAD, 8), step)
            f0, f1, f2, f3, f4 = [raw[orient, k, rows, :] for k in holder]
            zero = f0.astype(jnp.float32) * data_scale - 2.0
            near = (f1 + f4).astype(jnp.float32) * data_scale - 4.0
            far = (f2 + f3).astype(jnp.float32) * data_scale - 4.0
            near_odd = (f1 - f4).astype(jnp.float32) * data_scale
            far_odd = (f2 - f3).astype(jnp.float32) * data_scale
            mixed[4 * orient, at, :] = zero + c1 * near + c2 * far
            mixed[4 * orient + 1, at, :] = s1 * near_odd + s2 * far_odd
            mixed[4 * orient + 2, at, :] = zero + c2 * near + c1 * far
            mixed[4 * orient + 3, at, :] = s2 * near_odd - s1 * far_odd
            plain = zero + near + far
            if orient:
                plain = plain + mixed[total, at, :]
            mixed[total, at, :] = plain
            return carry

        lax.fori_loop(0, loop_width // step, mix, 0)
    for image in range(total + 1):
        mixed[image, PAD - reach : PAD, :] = mixed[
            image, loop_width + PAD - reach : loop_width + PAD, :
        ]
        mixed[image, loop_width + PAD : loop_width + PAD + reach, :] = mixed[
            image, PAD : PAD + reach, :
        ]
    blur_copy.wait()
    for band in range(bands):
        weight[band] = weights(blur_rows[band])
    table_copy.wait()

    def blur(image, band, begin):
        acc = None
        for offset in range(-reach, reach + 1):
            tap = taps_ref[band, offset + reach] * (1.0 / (orients * phases))
            term = tap * mixed[image, pl.ds(begin + PAD - offset, step), :]
            acc = term if acc is None else acc + term
        return acc

    shares = step // width

    def store(index, band, values):
        for share in range(shares):
            out_ref[index * shares + share, band] = values[share * width : (share + 1) * width]

    def plain_out(index, carry):
        begin = pl.multiple_of(index * step, step)
        store(index, 0, narrow(wide_dot(wide(blur(total, 0, begin)), weight[0])))
        return carry

    lax.fori_loop(0, loop_width // step, plain_out, 0)
    for band in range(1, bands):

        def band_out(index, carry):
            begin = pl.multiple_of(index * step, step)
            at = pl.ds(begin + PAD, step)
            parts = []
            for orient in range(orients):
                for part in range(2):
                    parts.append(wide(blur(4 * orient + 2 * band - 2 + part, band, begin)))
            product = narrow(wide_dot(jnp.concatenate(parts, axis=0), weight[band]))
            acc = None
            for orient in range(orients):
                cos_pattern, sin_pattern = harmonic_of(
                    table[2 * orient, at, :], table[2 * orient + 1, at, :], band
                )
                even = product[2 * orient * step : (2 * orient + 1) * step]
                odd = product[(2 * orient + 1) * step : (2 * orient + 2) * step]
                term = cos_pattern * even - sin_pattern * odd
                acc = term if acc is None else acc + term
            store(index, band, acc)
            return carry

        lax.fori_loop(0, loop_width // step, band_out, 0)


def data_sums(frames, phase_index, row_blur, column_taps, table, chunks):
    orients, phases, _, loop_width, row_count = frames.shape
    bands = row_blur.shape[0]
    width = loop_width // chunks
    smem = pl.BlockSpec(memory_space=pltpu.SMEM)
    vmem = pl.BlockSpec(memory_space=pltpu.VMEM)
    anywhere = pl.BlockSpec(memory_space=pltpu.HBM)
    images = 4 * orients + 1
    return pl.pallas_call(
        data_kernel,
        out_shape=jax.ShapeDtypeStruct((chunks, bands, width, row_count), jnp.float32),
        in_specs=[smem, smem, anywhere, anywhere, anywhere],
        out_specs=vmem,
        scratch_shapes=[
            pltpu.VMEM((orients, phases, loop_width, row_count), jnp.int32),
            pltpu.VMEM((images, loop_width + 2 * PAD, row_count), jnp.float32),
            pltpu.VMEM((bands, 2 * row_count, 2 * row_count), jnp.bfloat16),
            pltpu.VMEM(table.shape, jnp.float32),
            pltpu.VMEM(row_blur.shape, jnp.float32),
            pltpu.SemaphoreType.DMA((orients, phases)),
            pltpu.SemaphoreType.DMA((2,)),
        ],
        cost_estimate=pl.CostEstimate(
            flops=13 * loop_width * 2 * 256 * 256, bytes_accessed=frames.size * 4, transcendentals=0
        ),
        compiler_params=pltpu.CompilerParams(vmem_limit_bytes=63 << 20),
        name="data_sums",
    )(phase_index, column_taps, frames, row_blur, table)


def estimate_kernel(taps_ref, axial_ref, table_ref, blur_ref, out_ref):
    bands, _, planes, _ = axial_ref.shape
    width = out_ref.shape[0]
    orients = table_ref.shape[0] // 2
    reach = (taps_ref.shape[1] - 1) // 2
    span = 2 * reach
    step = 4

    def lags_of(band, scale):
        return [
            scale
            * sum(
                taps_ref[band, d] * taps_ref[band, d + shift]
                for d in range(0, 2 * reach + 1 - shift)
            )
            for shift in range(span + 1)
        ]

    def filtered(columns, lags):
        rows = []
        for i in range(step):
            acc = lags[0] * columns[i + span]
            for shift in range(1, span + 1):
                acc = acc + lags[shift] * (columns[i + span - shift] + columns[i + span + shift])
            rows.append(wide(acc))
        return rows

    def weight_of(band):
        matrix = blur_ref[band]
        return weights(
            lax.dot_general(
                matrix,
                matrix,
                (((0,), (0,)), ((), ())),
                preferred_element_type=jnp.float32,
                precision=lax.Precision.HIGHEST,
            )
        )

    weight = [weight_of(band) for band in range(bands)]
    lags = [lags_of(0, 1.0)] + [lags_of(band, 0.5 / orients) for band in range(1, bands)]

    def chunk(index, carry):
        begin = index * step
        rows = filtered([axial_ref[0, begin + i] for i in range(step + 2 * span)], lags[0])
        product = narrow(wide_dot(jnp.concatenate(rows, axis=0), weight[0]))
        acc = [product[i * planes : (i + 1) * planes] for i in range(step)]
        for band in range(1, bands):
            rows = []
            patterns = []
            for orient in range(orients):
                pairs = [
                    harmonic_of(
                        table_ref[2 * orient, pl.ds(begin + i, 1), :],
                        table_ref[2 * orient + 1, pl.ds(begin + i, 1), :],
                        band,
                    )
                    for i in range(step + 2 * span)
                ]
                for part in range(2):
                    columns = [
                        pairs[i][part] * axial_ref[band, begin + i]
                        for i in range(step + 2 * span)
                    ]
                    rows += filtered(columns, lags[band])
                    patterns.append([pairs[i + span][part] for i in range(step)])
            product = narrow(wide_dot(jnp.concatenate(rows, axis=0), weight[band]))
            for which, pattern in enumerate(patterns):
                for i in range(step):
                    at = (which * step + i) * planes
                    acc[i] = acc[i] + pattern[i] * product[at : at + planes]
        for i in range(step):
            out_ref[begin + i] = acc[i]
        return carry

    lax.fori_loop(0, width // step, chunk, 0)


def estimate_part(axial, table, row_blur, column_taps, width):
    _, _, planes, row_count = axial.shape
    orients = table.shape[0] // 2
    smem = pl.BlockSpec(memory_space=pltpu.SMEM)
    vmem = pl.BlockSpec(memory_space=pltpu.VMEM)
    rows = 2 * orients * width * planes
    return pl.pallas_call(
        estimate_kernel,
        out_shape=jax.ShapeDtypeStruct((width, planes, row_count), jnp.float32),
        in_specs=[smem, vmem, vmem, vmem],
        out_specs=vmem,
        cost_estimate=pl.CostEstimate(
            flops=40 * rows * 2 * 256 * 256, bytes_accessed=axial.size * 4, transcendentals=0
        ),
        compiler_params=pltpu.CompilerParams(vmem_limit_bytes=40 << 20),
        name="estimate_part",
    )(column_taps, axial, table, row_blur)


def combine_kernel(adjoint_ref, estimate_ref, received_ref, out_ref):
    width, planes, _ = estimate_ref.shape
    high, low = split(adjoint_ref[...])
    left_side = jnp.concatenate([high, high, low], axis=1)
    depth = adjoint_ref.shape[1]
    for index in range(width):
        high, low = split(received_ref[pl.ds(index, depth, stride=width), :])
        right_side = jnp.concatenate([high, low, high], axis=0)
        out_ref[pl.ds(index, planes, stride=width), :] = estimate_ref[index] - wide_dot(
            left_side, right_side
        )


def combine(adjoint, from_estimate, received):
    width, planes, row_count = from_estimate.shape
    depth = adjoint.shape[1]
    vmem = pl.BlockSpec(memory_space=pltpu.VMEM)
    return pl.pallas_call(
        combine_kernel,
        out_shape=jax.ShapeDtypeStruct((planes * width, row_count), jnp.float32),
        in_specs=[vmem, vmem, vmem],
        out_specs=vmem,
        cost_estimate=pl.CostEstimate(
            flops=2 * received.size * planes, bytes_accessed=received.size * 4, transcendentals=0
        ),
        compiler_params=pltpu.CompilerParams(vmem_limit_bytes=24 << 20),
        name="combine",
    )(adjoint, from_estimate, received.reshape(depth * width, row_count)).reshape(
        planes, width, row_count
    )


def halo(estimate, span):
    ring = lax.axis_size("gz")
    width = estimate.shape[1]
    lefts, rights = [], []
    hop, missing = 1, span
    while missing > 0:
        take = min(missing, width)
        lefts.insert(
            0,
            lax.ppermute(
                estimate[:, width - take :], "gz", [(s, (s + hop) % ring) for s in range(ring)]
            ),
        )
        rights.append(
            lax.ppermute(estimate[:, :take], "gz", [(s, (s - hop) % ring) for s in range(ring)])
        )
        missing -= take
        hop += 1
    return jnp.concatenate(lefts + [estimate] + rights, axis=1)


def axial_matrices(axial_otf, planes):
    wrapped = np.arange(planes)[:, None] * np.arange(planes)[None, :] % planes
    angle = wrapped * (2.0 * math.pi / planes)
    cosine = np.cos(angle).astype(np.float32)
    sine = np.sin(angle).astype(np.float32)
    real = axial_otf[:, 0, :, None]
    imag = axial_otf[:, 1, :, None]
    inner = jnp.concatenate(
        [real * cosine + imag * sine, real * sine - imag * cosine], axis=1
    )
    both = np.concatenate([cosine, sine], axis=1) / planes
    return jnp.einsum(
        "zk,mkw->mzw", both, inner, precision=lax.Precision.HIGHEST,
        preferred_element_type=jnp.float32,
    )


def shards(estimate, frames, phase_index, axial_otf, row_blur, column_taps):
    planes, width, row_count = estimate.shape
    ring = lax.axis_size("gz")
    orients = frames.shape[0]
    bands = row_blur.shape[0]
    span = column_taps.shape[1] - 1
    table = jnp.asarray(pattern_table(orients, width * ring, row_count))
    sums = data_sums(frames, phase_index, row_blur, column_taps, table, ring)
    estimate, sums = lax.optimization_barrier((estimate, sums))
    extended = halo(estimate, span)
    received = lax.all_to_all(sums, "gz", 0, 0, tiled=True)
    forward = axial_matrices(axial_otf, planes)
    squared = jnp.einsum("mzw,mzv->mwv", forward, forward, precision=lax.Precision.HIGHEST)
    axial = exact_dot(squared.reshape(bands * planes, planes), extended.reshape(planes, -1))
    axial = axial.reshape(bands, planes, width + 2 * span, row_count).transpose(0, 2, 1, 3)
    begin = lax.axis_index("gz") * width + (PAD - span)
    near = lax.dynamic_slice_in_dim(table, begin, width + 2 * span, axis=1)
    from_estimate = estimate_part(axial, near, row_blur, column_taps, width)
    adjoint = forward.transpose(2, 1, 0).reshape(planes, planes * bands)
    return combine(adjoint, from_estimate, received)


def solution(mesh):
    placed = (P(None, "gz", "groups"), P(None, None, "gz", None, "groups"), P(), P(), P(), P())
    return jax.shard_map(
        shards, mesh=mesh, in_specs=placed, out_specs=P(None, "gz", "groups"), check_vma=False
    )
```

```python
import math

import jax
import jax.numpy as jnp
import numpy as np
from jax import lax
from jax.experimental import pallas as pl
from jax.experimental.pallas import tpu as pltpu
from jax.sharding import PartitionSpec as P


pattern_period = 3.7
orient_base = 0.3
data_scale = 1.0 / 1024.0
PAD = 8


def exact_dot(left_side, right_side):
    return jnp.dot(
        left_side, right_side, preferred_element_type=jnp.float32, precision=lax.Precision.HIGHEST
    )


def split(values):
    high = values.astype(jnp.bfloat16)
    low = (values - high.astype(jnp.float32)).astype(jnp.bfloat16)
    return high, low


def wide(values):
    high, low = split(values)
    return jnp.concatenate([high, low], axis=1)


def weights(matrix):
    row = wide(matrix)
    return jnp.concatenate([row, row], axis=0)


def narrow(product):
    half = product.shape[1] // 2
    return product[:, :half] + product[:, half:]


def wide_dot(left_side, right_side):
    return jnp.dot(left_side, right_side, preferred_element_type=jnp.float32)


def pattern_table(orients, loop_width, row_count):
    columns = np.arange(-PAD, loop_width + PAD) % loop_width
    rows = np.arange(row_count)
    images = []
    for orient in range(orients):
        direction = orient_base + 2.0 * math.pi * orient / 3.0
        phase = (
            columns.astype(np.float32)[:, None] * np.float32(math.cos(direction))
            + rows.astype(np.float32)[None, :] * np.float32(math.sin(direction))
        ) * np.float32(2.0 * math.pi / pattern_period)
        images += [np.cos(phase.astype(np.float64)), np.sin(phase.astype(np.float64))]
    return np.stack(images).astype(np.float32)


def harmonic_of(cos_one, sin_one, harmonic):
    if harmonic == 1:
        return cos_one, sin_one
    return cos_one * cos_one - sin_one * sin_one, 2.0 * (sin_one * cos_one)


def blurred(mixed, image, taps, begin, step):
    reach = (len(taps) - 1) // 2
    acc = None
    for offset in range(-reach, reach + 1):
        term = taps[offset + reach] * mixed[image, pl.ds(begin + PAD - offset, step), :]
        acc = term if acc is None else acc + term
    return acc


def band_rows(mixed, images, taps, table, weight, band, begin, step):
    at = pl.ds(begin + PAD, step)
    parts = [wide(blurred(mixed, image, taps, begin, step)) for image in images]
    product = narrow(wide_dot(jnp.concatenate(parts, axis=0), weight))
    acc = None
    for orient in range(len(images) // 2):
        cos_pattern, sin_pattern = harmonic_of(
            table[2 * orient, at, :], table[2 * orient + 1, at, :], band
        )
        even = product[2 * orient * step : (2 * orient + 1) * step]
        odd = product[(2 * orient + 1) * step : (2 * orient + 2) * step]
        term = cos_pattern * even - sin_pattern * odd
        acc = term if acc is None else acc + term
    return acc


def put(out, index, band, values):
    width = out.shape[2]
    shares = values.shape[0] // width
    for share in range(shares):
        out[index * shares + share, band] = values[share * width : (share + 1) * width]


def scaled_taps(taps_ref, band, count):
    return [taps_ref[band, at] * (1.0 / count) for at in range(taps_ref.shape[1])]


def data_kernel(
    phase_hbm, taps_hbm, frames_hbm, blur_hbm, table_hbm, out_hbm,
    raw, mixed, weight, table, blur_rows, out, phase_ref, taps_ref,
    frame_sems, side_sems, out_sems,
):
    orients, phases = raw.shape[0], raw.shape[1]
    loop_width = raw.shape[2]
    bands, width = out.shape[1], out.shape[2]
    phase_copy = pltpu.make_async_copy(phase_hbm, phase_ref, side_sems.at[0])
    phase_copy.start()
    copies = []
    for orient in range(orients):
        row = []
        for index in range(phases):
            copy = pltpu.make_async_copy(
                frames_hbm.at[orient, index, 0],
                raw.at[orient, index],
                frame_sems.at[orient, index],
            )
            copy.start()
            row.append(copy)
        copies.append(row)
    taps_copy = pltpu.make_async_copy(taps_hbm, taps_ref, side_sems.at[1])
    taps_copy.start()
    blur_copy = pltpu.make_async_copy(blur_hbm, blur_rows, side_sems.at[2])
    blur_copy.start()
    table_copy = pltpu.make_async_copy(table_hbm, table, side_sems.at[3])
    table_copy.start()
    c1, c2 = math.cos(2 * math.pi / 5), math.cos(4 * math.pi / 5)
    s1, s2 = math.sin(2 * math.pi / 5), math.sin(4 * math.pi / 5)
    step = max(64, width)
    reach = (taps_ref.shape[1] - 1) // 2
    total = 4 * orients
    phase_copy.wait()
    for orient in range(orients):
        holder = []
        for step_index in range(phases):
            at_step = 0
            for index in range(1, phases):
                at_step = jnp.where(phase_ref[orient, index] == step_index, index, at_step)
            holder.append(at_step)
        for copy in copies[orient]:
            copy.wait()

        def mix(index, carry):
            rows = pl.ds(pl.multiple_of(index * step, step), step)
            at = pl.ds(pl.multiple_of(index * step + PAD, 8), step)
            f0, f1, f2, f3, f4 = [raw[orient, k, rows, :] for k in holder]
            zero = f0.astype(jnp.float32) * data_scale - 2.0
            near = (f1 + f4).astype(jnp.float32) * data_scale - 4.0
            far = (f2 + f3).astype(jnp.float32) * data_scale - 4.0
            near_odd = (f1 - f4).astype(jnp.float32) * data_scale
            far_odd = (f2 - f3).astype(jnp.float32) * data_scale
            mixed[2 * orient, at, :] = zero + c1 * near + c2 * far
            mixed[2 * orient + 1, at, :] = s1 * near_odd + s2 * far_odd
            mixed[2 * (orients + orient), at, :] = zero + c2 * near + c1 * far
            mixed[2 * (orients + orient) + 1, at, :] = s2 * near_odd - s1 * far_odd
            plain = zero + near + far
            if orient:
                plain = plain + mixed[total, at, :]
            mixed[total, at, :] = plain
            return carry

        lax.fori_loop(0, loop_width // step, mix, 0)
    for image in range(total + 1):
        mixed[image, PAD - reach : PAD, :] = mixed[
            image, loop_width + PAD - reach : loop_width + PAD, :
        ]
        mixed[image, loop_width + PAD : loop_width + PAD + reach, :] = mixed[
            image, PAD : PAD + reach, :
        ]
    taps_copy.wait()
    blur_copy.wait()
    for band in range(bands):
        weight[band] = weights(blur_rows[band])
    taps = [scaled_taps(taps_ref, band, orients * phases) for band in range(bands)]

    def plain_out(index, carry):
        begin = pl.multiple_of(index * step, step)
        rows = blurred(mixed, total, taps[0], begin, step)
        put(out, index, 0, narrow(wide_dot(wide(rows), weight[0])))
        return carry

    lax.fori_loop(0, loop_width // step, plain_out, 0)
    out_copies = [pltpu.make_async_copy(out.at[:, 0], out_hbm.at[:, 0], out_sems.at[0])]
    out_copies[0].start()
    table_copy.wait()
    for band in range(1, bands):
        images = list(range(2 * orients * (band - 1), 2 * orients * band))

        def band_out(index, carry):
            begin = pl.multiple_of(index * step, step)
            put(
                out,
                index,
                band,
                band_rows(mixed, images, taps[band], table, weight[band], band, begin, step),
            )
            return carry

        lax.fori_loop(0, loop_width // step, band_out, 0)
        out_copies.append(
            pltpu.make_async_copy(out.at[:, band], out_hbm.at[:, band], out_sems.at[band])
        )
        out_copies[band].start()
    for copy in out_copies:
        copy.wait()


def data_sums(frames, phase_index, row_blur, column_taps, table, chunks):
    orients, phases, _, loop_width, row_count = frames.shape
    bands = row_blur.shape[0]
    width = loop_width // chunks
    anywhere = pl.BlockSpec(memory_space=pltpu.HBM)
    return pl.pallas_call(
        data_kernel,
        out_shape=jax.ShapeDtypeStruct((chunks, bands, width, row_count), jnp.float32),
        in_specs=[anywhere] * 5,
        out_specs=anywhere,
        scratch_shapes=[
            pltpu.VMEM((orients, phases, loop_width, row_count), jnp.int32),
            pltpu.VMEM((4 * orients + 1, loop_width + 2 * PAD, row_count), jnp.float32),
            pltpu.VMEM((bands, 2 * row_count, 2 * row_count), jnp.bfloat16),
            pltpu.VMEM(table.shape, jnp.float32),
            pltpu.VMEM(row_blur.shape, jnp.float32),
            pltpu.VMEM((chunks, bands, width, row_count), jnp.float32),
            pltpu.SMEM(phase_index.shape, jnp.int32),
            pltpu.SMEM(column_taps.shape, jnp.float32),
            pltpu.SemaphoreType.DMA((orients, phases)),
            pltpu.SemaphoreType.DMA((4,)),
            pltpu.SemaphoreType.DMA((bands,)),
        ],
        cost_estimate=pl.CostEstimate(
            flops=13 * loop_width * 2 * 256 * 256, bytes_accessed=frames.size * 4, transcendentals=0
        ),
        compiler_params=pltpu.CompilerParams(vmem_limit_bytes=63 << 20),
        name="data_sums",
    )(phase_index, column_taps, frames, row_blur, table)


def estimate_kernel(taps_ref, axial_ref, table_ref, blur_ref, out_ref):
    bands, _, planes, _ = axial_ref.shape
    width = out_ref.shape[0]
    orients = table_ref.shape[0] // 2
    reach = (taps_ref.shape[1] - 1) // 2
    span = 2 * reach
    step = 4

    def lags_of(band, scale):
        return [
            scale
            * sum(
                taps_ref[band, d] * taps_ref[band, d + shift]
                for d in range(0, 2 * reach + 1 - shift)
            )
            for shift in range(span + 1)
        ]

    def filtered(columns, lags):
        rows = []
        for i in range(step):
            acc = lags[0] * columns[i + span]
            for shift in range(1, span + 1):
                acc = acc + lags[shift] * (columns[i + span - shift] + columns[i + span + shift])
            rows.append(wide(acc))
        return rows

    def weight_of(band):
        matrix = blur_ref[band]
        return weights(
            lax.dot_general(
                matrix,
                matrix,
                (((0,), (0,)), ((), ())),
                preferred_element_type=jnp.float32,
                precision=lax.Precision.HIGHEST,
            )
        )

    weight = [weight_of(band) for band in range(bands)]
    lags = [lags_of(0, 1.0)] + [lags_of(band, 0.5 / orients) for band in range(1, bands)]

    def chunk(index, carry):
        begin = index * step
        rows = filtered([axial_ref[0, begin + i] for i in range(step + 2 * span)], lags[0])
        product = narrow(wide_dot(jnp.concatenate(rows, axis=0), weight[0]))
        acc = [product[i * planes : (i + 1) * planes] for i in range(step)]
        for band in range(1, bands):
            rows = []
            patterns = []
            for orient in range(orients):
                pairs = [
                    harmonic_of(
                        table_ref[2 * orient, pl.ds(begin + i, 1), :],
                        table_ref[2 * orient + 1, pl.ds(begin + i, 1), :],
                        band,
                    )
                    for i in range(step + 2 * span)
                ]
                for part in range(2):
                    columns = [
                        pairs[i][part] * axial_ref[band, begin + i]
                        for i in range(step + 2 * span)
                    ]
                    rows += filtered(columns, lags[band])
                    patterns.append([pairs[i + span][part] for i in range(step)])
            product = narrow(wide_dot(jnp.concatenate(rows, axis=0), weight[band]))
            for which, pattern in enumerate(patterns):
                for i in range(step):
                    at = (which * step + i) * planes
                    acc[i] = acc[i] + pattern[i] * product[at : at + planes]
        for i in range(step):
            out_ref[begin + i] = acc[i]
        return carry

    lax.fori_loop(0, width // step, chunk, 0)


def estimate_part(axial, table, row_blur, column_taps, width):
    _, _, planes, row_count = axial.shape
    orients = table.shape[0] // 2
    smem = pl.BlockSpec(memory_space=pltpu.SMEM)
    vmem = pl.BlockSpec(memory_space=pltpu.VMEM)
    rows = 2 * orients * width * planes
    return pl.pallas_call(
        estimate_kernel,
        out_shape=jax.ShapeDtypeStruct((width, planes, row_count), jnp.float32),
        in_specs=[smem, vmem, vmem, vmem],
        out_specs=vmem,
        cost_estimate=pl.CostEstimate(
            flops=40 * rows * 2 * 256 * 256, bytes_accessed=axial.size * 4, transcendentals=0
        ),
        compiler_params=pltpu.CompilerParams(vmem_limit_bytes=40 << 20),
        name="estimate_part",
    )(column_taps, axial, table, row_blur)


def combine_kernel(adjoint_ref, estimate_ref, received_ref, out_ref):
    width, planes, _ = estimate_ref.shape
    depth = adjoint_ref.shape[1]
    high, low = split(adjoint_ref[...])
    left_side = jnp.concatenate([high, high, low], axis=1)
    for index in range(width):
        high, low = split(received_ref[pl.ds(index, depth, stride=width), :])
        right_side = jnp.concatenate([high, low, high], axis=0)
        out_ref[pl.ds(index, planes, stride=width), :] = estimate_ref[index] - wide_dot(
            left_side, right_side
        )


def combine(forward, from_estimate, received):
    width, planes, row_count = from_estimate.shape
    depth = forward.shape[0] * planes
    adjoint = forward.transpose(2, 1, 0).reshape(planes, depth)
    vmem = pl.BlockSpec(memory_space=pltpu.VMEM)
    return pl.pallas_call(
        combine_kernel,
        out_shape=jax.ShapeDtypeStruct((planes * width, row_count), jnp.float32),
        in_specs=[vmem] * 3,
        out_specs=vmem,
        cost_estimate=pl.CostEstimate(
            flops=2 * received.size * planes, bytes_accessed=received.size * 4, transcendentals=0
        ),
        compiler_params=pltpu.CompilerParams(vmem_limit_bytes=24 << 20),
        name="combine",
    )(adjoint, from_estimate, received.reshape(depth * width, row_count)).reshape(
        planes, width, row_count
    )


def halo(estimate, span):
    ring = lax.axis_size("gz")
    width = estimate.shape[1]
    lefts, rights = [], []
    hop, missing = 1, span
    while missing > 0:
        take = min(missing, width)
        lefts.insert(
            0,
            lax.ppermute(
                estimate[:, width - take :], "gz", [(s, (s + hop) % ring) for s in range(ring)]
            ),
        )
        rights.append(
            lax.ppermute(estimate[:, :take], "gz", [(s, (s - hop) % ring) for s in range(ring)])
        )
        missing -= take
        hop += 1
    return jnp.concatenate(lefts + [estimate] + rights, axis=1)


def axial_matrices(axial_otf, planes):
    wrapped = np.arange(planes)[:, None] * np.arange(planes)[None, :] % planes
    angle = wrapped * (2.0 * math.pi / planes)
    cosine = np.cos(angle).astype(np.float32)
    sine = np.sin(angle).astype(np.float32)
    real = axial_otf[:, 0, :, None]
    imag = axial_otf[:, 1, :, None]
    inner = jnp.concatenate(
        [real * cosine + imag * sine, real * sine - imag * cosine], axis=1
    )
    both = np.concatenate([cosine, sine], axis=1) / planes
    return jnp.einsum(
        "zk,mkw->mzw", both, inner, precision=lax.Precision.HIGHEST,
        preferred_element_type=jnp.float32,
    )


def shards(estimate, frames, phase_index, axial_otf, row_blur, column_taps):
    planes, width, row_count = estimate.shape
    ring = lax.axis_size("gz")
    orients = frames.shape[0]
    bands = row_blur.shape[0]
    span = column_taps.shape[1] - 1
    table = jnp.asarray(pattern_table(orients, width * ring, row_count))
    sums = data_sums(frames, phase_index, row_blur, column_taps, table, ring)
    estimate, sums = lax.optimization_barrier((estimate, sums))
    extended = halo(estimate, span)
    received = lax.all_to_all(sums, "gz", 0, 0, tiled=True)
    forward = axial_matrices(axial_otf, planes)
    squared = jnp.einsum("mzw,mzv->mwv", forward, forward, precision=lax.Precision.HIGHEST)
    axial = exact_dot(squared.reshape(bands * planes, planes), extended.reshape(planes, -1))
    axial = axial.reshape(bands, planes, width + 2 * span, row_count).transpose(0, 2, 1, 3)
    begin = lax.axis_index("gz") * width + (PAD - span)
    near = lax.dynamic_slice_in_dim(table, begin, width + 2 * span, axis=1)
    from_estimate = estimate_part(axial, near, row_blur, column_taps, width)
    return combine(forward, from_estimate, received)


def solution(mesh):
    placed = (P(None, "gz", "groups"), P(None, None, "gz", None, "groups"), P(), P(), P(), P())
    return jax.shard_map(
        shards, mesh=mesh, in_specs=placed, out_specs=P(None, "gz", "groups"), check_vma=False
    )
```

```python
import functools
import math

import jax
import jax.numpy as jnp
import numpy as np
from jax import lax
from jax.experimental import pallas as pl
from jax.experimental.pallas import tpu as pltpu
from jax.sharding import PartitionSpec as P


pattern_period = 3.7
orient_base = 0.3
data_scale = 1.0 / 1024.0
PAD = 8


def exact_dot(left_side, right_side):
    return jnp.dot(
        left_side, right_side, preferred_element_type=jnp.float32, precision=lax.Precision.HIGHEST
    )


def split(values):
    high = values.astype(jnp.bfloat16)
    low = (values - high.astype(jnp.float32)).astype(jnp.bfloat16)
    return high, low


def wide(values):
    high, low = split(values)
    return jnp.concatenate([high, low], axis=1)


def weights(matrix):
    row = wide(matrix)
    return jnp.concatenate([row, row], axis=0)


def narrow(product):
    half = product.shape[1] // 2
    return product[:, :half] + product[:, half:]


def wide_dot(left_side, right_side):
    return jnp.dot(left_side, right_side, preferred_element_type=jnp.float32)


def pattern_table(orients, loop_width, row_count, pad):
    columns = np.arange(-pad, loop_width + pad) % loop_width
    rows = np.arange(row_count)
    images = []
    for orient in range(orients):
        direction = orient_base + 2.0 * math.pi * orient / 3.0
        phase = (
            columns.astype(np.float32)[:, None] * np.float32(math.cos(direction))
            + rows.astype(np.float32)[None, :] * np.float32(math.sin(direction))
        ) * np.float32(2.0 * math.pi / pattern_period)
        images += [np.cos(phase.astype(np.float64)), np.sin(phase.astype(np.float64))]
    return np.stack(images).astype(np.float32)


def harmonic_of(cos_one, sin_one, harmonic):
    if harmonic == 1:
        return cos_one, sin_one
    return cos_one * cos_one - sin_one * sin_one, 2.0 * (sin_one * cos_one)


def blurred(mixed, image, taps, begin, step):
    reach = (len(taps) - 1) // 2
    acc = None
    for offset in range(-reach, reach + 1):
        term = taps[offset + reach] * mixed[image, pl.ds(begin + PAD - offset, step), :]
        acc = term if acc is None else acc + term
    return acc


def band_rows(mixed, images, taps, table, weight, band, begin, step):
    at = pl.ds(begin + (table.shape[1] - mixed.shape[1]) // 2 + PAD, step)
    parts = [wide(blurred(mixed, image, cut, begin, step)) for image, cut in zip(images, taps)]
    product = narrow(wide_dot(jnp.concatenate(parts, axis=0), weight))
    acc = None
    for orient in range(len(images) // 2):
        cos_pattern, sin_pattern = harmonic_of(
            table[2 * orient, at, :], table[2 * orient + 1, at, :], band
        )
        even = product[2 * orient * step : (2 * orient + 1) * step]
        odd = product[(2 * orient + 1) * step : (2 * orient + 2) * step]
        term = cos_pattern * even - sin_pattern * odd
        acc = term if acc is None else acc + term
    return acc


def put(out, index, band, values):
    width = out.shape[2]
    shares = values.shape[0] // width
    for share in range(shares):
        out[index * shares + share, band] = values[share * width : (share + 1) * width]


def scaled_taps(taps_ref, band, scale):
    return [taps_ref[band, at] * scale for at in range(taps_ref.shape[1])]


def data_kernel(
    phase_hbm, taps_hbm, frames_hbm, blur_hbm, table_hbm, out_hbm,
    raw, summed, mixed, weight, table, blur_rows, out, phase_ref, taps_ref,
    frame_sems, side_sems, out_sems,
):
    orients, phases = raw.shape[0], raw.shape[1]
    loop_width = raw.shape[2]
    bands = out.shape[1]
    phase_copy = pltpu.make_async_copy(phase_hbm, phase_ref, side_sems.at[0])
    phase_copy.start()
    copies = []
    for orient in range(orients):
        row = []
        for index in range(phases):
            copy = pltpu.make_async_copy(
                frames_hbm.at[orient, index, 0],
                raw.at[orient, index],
                frame_sems.at[orient, index],
            )
            copy.start()
            row.append(copy)
        copies.append(row)
    taps_copy = pltpu.make_async_copy(taps_hbm, taps_ref, side_sems.at[1])
    taps_copy.start()
    blur_copy = pltpu.make_async_copy(blur_hbm, blur_rows, side_sems.at[2])
    blur_copy.start()
    table_copy = pltpu.make_async_copy(table_hbm, table, side_sems.at[3])
    table_copy.start()
    step = loop_width // 2
    reach = (taps_ref.shape[1] - 1) // 2
    total = 4 * orients
    count = orients * phases
    first_sine, second_sine = math.sin(2 * math.pi / 5), math.sin(4 * math.pi / 5)
    ratio = second_sine / first_sine
    phase_copy.wait()
    for orient in range(orients):
        holder = []
        for step_index in range(phases):
            at_step = 0
            for index in range(1, phases):
                at_step = jnp.where(phase_ref[orient, index] == step_index, index, at_step)
            holder.append(at_step)
        for copy in copies[orient]:
            copy.wait()

        def mix(index, carry):
            rows = pl.ds(pl.multiple_of(index * step, step), step)
            at = pl.ds(pl.multiple_of(index * step + PAD, 8), step)
            f0, f1, f2, f3, f4 = [raw[orient, k, rows, :] for k in holder]
            near, far, near_odd, far_odd = f1 + f4, f2 + f3, f1 - f4, f2 - f3
            both = near + far
            even = (4 * f0 - both).astype(jnp.float32)
            swing = (near - far).astype(jnp.float32) * math.sqrt(5.0)
            near_odd = near_odd.astype(jnp.float32)
            far_odd = far_odd.astype(jnp.float32)
            mixed[2 * orient, at, :] = even + swing
            mixed[2 * orient + 1, at, :] = near_odd + ratio * far_odd
            mixed[2 * (orients + orient), at, :] = even - swing
            mixed[2 * (orients + orient) + 1, at, :] = ratio * near_odd - far_odd
            plain = f0 + both
            if orient:
                plain = plain + summed[rows, :]
            if orient < orients - 1:
                summed[rows, :] = plain
            else:
                mixed[total, at, :] = plain.astype(jnp.float32) * data_scale - 2.0 * count
            return carry

        lax.fori_loop(0, loop_width // step, mix, 0)
    for image in range(total + 1):
        mixed[image, PAD - reach : PAD, :] = mixed[
            image, loop_width + PAD - reach : loop_width + PAD, :
        ]
        mixed[image, loop_width + PAD : loop_width + PAD + reach, :] = mixed[
            image, PAD : PAD + reach, :
        ]
    taps_copy.wait()
    blur_copy.wait()
    for band in range(bands):
        weight[band] = weights(blur_rows[band])
    even_scale, odd_scale = data_scale / (4.0 * count), data_scale * first_sine / count
    taps = [scaled_taps(taps_ref, 0, 1.0 / count)]
    for band in range(1, bands):
        taps.append(
            [scaled_taps(taps_ref, band, even_scale), scaled_taps(taps_ref, band, odd_scale)]
            * orients
        )

    def plain_out(index, carry):
        begin = pl.multiple_of(index * step, step)
        rows = blurred(mixed, total, taps[0], begin, step)
        put(out, index, 0, narrow(wide_dot(wide(rows), weight[0])))
        return carry

    lax.fori_loop(0, loop_width // step, plain_out, 0)
    out_copies = [pltpu.make_async_copy(out.at[:, 0], out_hbm.at[:, 0], out_sems.at[0])]
    out_copies[0].start()
    table_copy.wait()
    for band in range(1, bands):
        images = list(range(2 * orients * (band - 1), 2 * orients * band))

        def band_out(index, carry):
            begin = pl.multiple_of(index * step, step)
            put(
                out,
                index,
                band,
                band_rows(mixed, images, taps[band], table, weight[band], band, begin, step),
            )
            return carry

        lax.fori_loop(0, loop_width // step, band_out, 0)
        out_copies.append(
            pltpu.make_async_copy(out.at[:, band], out_hbm.at[:, band], out_sems.at[band])
        )
        out_copies[band].start()
    for copy in out_copies:
        copy.wait()


def data_sums(frames, phase_index, row_blur, column_taps, table, chunks):
    orients, phases, _, loop_width, row_count = frames.shape
    bands = row_blur.shape[0]
    width = loop_width // chunks
    anywhere = pl.BlockSpec(memory_space=pltpu.HBM)
    return pl.pallas_call(
        data_kernel,
        out_shape=jax.ShapeDtypeStruct((chunks, bands, width, row_count), jnp.float32),
        in_specs=[anywhere] * 5,
        out_specs=anywhere,
        scratch_shapes=[
            pltpu.VMEM((orients, phases, loop_width, row_count), jnp.int32),
            pltpu.VMEM((loop_width, row_count), jnp.int32),
            pltpu.VMEM((4 * orients + 1, loop_width + 2 * PAD, row_count), jnp.float32),
            pltpu.VMEM((bands, 2 * row_count, 2 * row_count), jnp.bfloat16),
            pltpu.VMEM(table.shape, jnp.float32),
            pltpu.VMEM(row_blur.shape, jnp.float32),
            pltpu.VMEM((chunks, bands, width, row_count), jnp.float32),
            pltpu.SMEM(phase_index.shape, jnp.int32),
            pltpu.SMEM(column_taps.shape, jnp.float32),
            pltpu.SemaphoreType.DMA((orients, phases)),
            pltpu.SemaphoreType.DMA((4,)),
            pltpu.SemaphoreType.DMA((bands,)),
        ],
        cost_estimate=pl.CostEstimate(
            flops=13 * loop_width * 2 * 256 * 256, bytes_accessed=frames.size * 4, transcendentals=0
        ),
        compiler_params=pltpu.CompilerParams(vmem_limit_bytes=63 << 20),
        name="data_sums",
    )(phase_index, column_taps, frames, row_blur, table)


def estimate_kernel(taps_ref, axial_ref, table_ref, blur_ref, out_ref):
    bands, _, planes, _ = axial_ref.shape
    orients = table_ref.shape[0] // 2
    reach = (taps_ref.shape[1] - 1) // 2
    span = 2 * reach
    step = 4

    def lags_of(band, scale):
        return [
            scale
            * sum(
                taps_ref[band, d] * taps_ref[band, d + shift]
                for d in range(0, 2 * reach + 1 - shift)
            )
            for shift in range(span + 1)
        ]

    def filtered(columns, lags):
        rows = []
        for i in range(step):
            acc = lags[0] * columns[i + span]
            for shift in range(1, span + 1):
                acc = acc + lags[shift] * (columns[i + span - shift] + columns[i + span + shift])
            rows.append(wide(acc))
        return rows

    def weight_of(band):
        matrix = blur_ref[band]
        return weights(
            lax.dot_general(
                matrix,
                matrix,
                (((0,), (0,)), ((), ())),
                preferred_element_type=jnp.float32,
                precision=lax.Precision.HIGHEST,
            )
        )

    weight = [weight_of(band) for band in range(bands)]
    lags = [lags_of(0, 1.0)] + [lags_of(band, 0.5 / orients) for band in range(1, bands)]

    def chunk(index, carry):
        begin = index * step
        rows = filtered([axial_ref[0, begin + i] for i in range(step + 2 * span)], lags[0])
        product = narrow(wide_dot(jnp.concatenate(rows, axis=0), weight[0]))
        acc = [product[i * planes : (i + 1) * planes] for i in range(step)]
        for band in range(1, bands):
            rows = []
            patterns = []
            for orient in range(orients):
                pairs = [
                    harmonic_of(
                        table_ref[2 * orient, pl.ds(begin + i, 1), :],
                        table_ref[2 * orient + 1, pl.ds(begin + i, 1), :],
                        band,
                    )
                    for i in range(step + 2 * span)
                ]
                for part in range(2):
                    columns = [
                        pairs[i][part] * axial_ref[band, begin + i]
                        for i in range(step + 2 * span)
                    ]
                    rows += filtered(columns, lags[band])
                    patterns.append([pairs[i + span][part] for i in range(step)])
            product = narrow(wide_dot(jnp.concatenate(rows, axis=0), weight[band]))
            for which, pattern in enumerate(patterns):
                for i in range(step):
                    at = (which * step + i) * planes
                    acc[i] = acc[i] + pattern[i] * product[at : at + planes]
        for i in range(step):
            out_ref[begin + i] = acc[i]
        return carry

    lax.fori_loop(0, out_ref.shape[0] // step, chunk, 0)


def estimate_part(axial, table, row_blur, column_taps):
    _, padded, planes, row_count = axial.shape
    orients = table.shape[0] // 2
    width = padded - 2 * (column_taps.shape[1] - 1)
    smem = pl.BlockSpec(memory_space=pltpu.SMEM)
    vmem = pl.BlockSpec(memory_space=pltpu.VMEM)
    rows = 2 * orients * width * planes
    return pl.pallas_call(
        estimate_kernel,
        out_shape=jax.ShapeDtypeStruct((width, planes, row_count), jnp.float32),
        in_specs=[smem, vmem, vmem, vmem],
        out_specs=vmem,
        cost_estimate=pl.CostEstimate(
            flops=40 * rows * 2 * 256 * 256, bytes_accessed=axial.size * 4, transcendentals=0
        ),
        compiler_params=pltpu.CompilerParams(vmem_limit_bytes=40 << 20),
        name="estimate_part",
    )(column_taps, axial, table, row_blur)


def combine_kernel(adjoint_ref, estimate_ref, received_ref, *refs, places):
    out_ref = refs[-1]
    planes, _ = estimate_ref.shape[1:]
    depth = adjoint_ref.shape[1]
    width = received_ref.shape[0] // depth
    span = (estimate_ref.shape[0] - width) // 2
    high, low = split(adjoint_ref[...])
    left_side = jnp.concatenate([high, high, low], axis=1)
    for index in range(width):
        high, low = split(received_ref[pl.ds(index, depth, stride=width), :])
        right_side = jnp.concatenate([high, low, high], axis=0)
        acc = estimate_ref[span + index]
        for ref, (begin, count) in zip(refs, places):
            if begin <= index < begin + count:
                acc = acc + ref[index - begin]
        out_ref[pl.ds(index, planes, stride=width), :] = acc - wide_dot(left_side, right_side)


def combine(forward, from_estimate, pieces, places, received):
    planes, row_count = from_estimate.shape[1:]
    depth = forward.shape[0] * planes
    width = received.size // (depth * row_count)
    adjoint = forward.transpose(2, 1, 0).reshape(planes, depth)
    vmem = pl.BlockSpec(memory_space=pltpu.VMEM)
    return pl.pallas_call(
        functools.partial(combine_kernel, places=places),
        out_shape=jax.ShapeDtypeStruct((planes * width, row_count), jnp.float32),
        in_specs=[vmem] * (3 + len(pieces)),
        out_specs=vmem,
        cost_estimate=pl.CostEstimate(
            flops=2 * received.size * planes, bytes_accessed=received.size * 4, transcendentals=0
        ),
        compiler_params=pltpu.CompilerParams(vmem_limit_bytes=24 << 20),
        name="combine",
    )(adjoint, from_estimate, received.reshape(depth * width, row_count), *pieces).reshape(
        planes, width, row_count
    )


def spread(from_estimate, span):
    ring = lax.axis_size("gz")
    width = from_estimate.shape[0] - 2 * span
    pieces, places = [], []
    hop, missing = 1, span
    while missing > 0:
        take = min(missing, width)
        piece = from_estimate[missing - take : missing]
        pieces.append(lax.ppermute(piece, "gz", [(s, (s - hop) % ring) for s in range(ring)]))
        places.append((width - take, take))
        begin = span + width * hop
        piece = from_estimate[begin : begin + take]
        pieces.append(lax.ppermute(piece, "gz", [(s, (s + hop) % ring) for s in range(ring)]))
        places.append((0, take))
        missing -= take
        hop += 1
    return pieces, places


def axial_matrices(axial_otf, planes):
    wrapped = np.arange(planes)[:, None] * np.arange(planes)[None, :] % planes
    angle = wrapped * (2.0 * math.pi / planes)
    cosine = np.cos(angle).astype(np.float32)
    sine = np.sin(angle).astype(np.float32)
    real = axial_otf[:, 0, :, None]
    imag = axial_otf[:, 1, :, None]
    inner = jnp.concatenate(
        [real * cosine + imag * sine, real * sine - imag * cosine], axis=1
    )
    both = np.concatenate([cosine, sine], axis=1) / planes
    return jnp.einsum(
        "zk,mkw->mzw", both, inner, precision=lax.Precision.HIGHEST,
        preferred_element_type=jnp.float32,
    )


def shards(estimate, frames, phase_index, axial_otf, row_blur, column_taps):
    planes, width, row_count = estimate.shape
    ring = lax.axis_size("gz")
    orients = frames.shape[0]
    bands = row_blur.shape[0]
    span = column_taps.shape[1] - 1
    pad = -(-2 * span // 8) * 8
    table = jnp.asarray(pattern_table(orients, width * ring, row_count, pad))
    sums = data_sums(frames, phase_index, row_blur, column_taps, table, ring)
    received = lax.all_to_all(sums, "gz", 0, 0, tiled=True)
    forward = axial_matrices(axial_otf, planes)
    squared = jnp.einsum("mzw,mzv->mwv", forward, forward, precision=lax.Precision.HIGHEST)
    axial = exact_dot(squared.reshape(bands * planes, planes), estimate.reshape(planes, -1))
    axial = axial.reshape(bands, planes, width, row_count).transpose(0, 2, 1, 3)
    axial = jnp.pad(axial, ((0, 0), (2 * span, 2 * span), (0, 0), (0, 0)))
    begin = lax.axis_index("gz") * width + (pad - 2 * span)
    near = lax.dynamic_slice_in_dim(table, begin, width + 4 * span, axis=1)
    from_estimate = estimate_part(axial, near, row_blur, column_taps)
    pieces, places = spread(from_estimate, span)
    return combine(forward, from_estimate, pieces, places, received)


def solution(mesh):
    placed = (P(None, "gz", "groups"), P(None, None, "gz", None, "groups"), P(), P(), P(), P())
    return jax.shard_map(
        shards, mesh=mesh, in_specs=placed, out_specs=P(None, "gz", "groups"), check_vma=False
    )
```

```python
import functools
import math

import jax
import jax.numpy as jnp
import numpy as np
from jax import lax
from jax.experimental import pallas as pl
from jax.experimental.pallas import tpu as pltpu
from jax.sharding import PartitionSpec as P


pattern_period = 3.7
orient_base = 0.3
data_scale = 1.0 / 1024.0
PAD = 8


def exact_dot(left_side, right_side):
    return jnp.dot(
        left_side, right_side, preferred_element_type=jnp.float32, precision=lax.Precision.HIGHEST
    )


def split(values):
    high = values.astype(jnp.bfloat16)
    low = (values - high.astype(jnp.float32)).astype(jnp.bfloat16)
    return high, low


def wide(values):
    high, low = split(values)
    return jnp.concatenate([high, low], axis=1)


def weights(matrix):
    row = wide(matrix)
    return jnp.concatenate([row, row], axis=0)


def narrow(product):
    half = product.shape[1] // 2
    return product[:, :half] + product[:, half:]


def wide_dot(left_side, right_side):
    return jnp.dot(left_side, right_side, preferred_element_type=jnp.float32)


def pattern_table(orients, loop_width, row_count, pad):
    columns = np.arange(-pad, loop_width + pad) % loop_width
    rows = np.arange(row_count)
    images = []
    for orient in range(orients):
        direction = orient_base + 2.0 * math.pi * orient / 3.0
        phase = (
            columns.astype(np.float32)[:, None] * np.float32(math.cos(direction))
            + rows.astype(np.float32)[None, :] * np.float32(math.sin(direction))
        ) * np.float32(2.0 * math.pi / pattern_period)
        images += [np.cos(phase.astype(np.float64)), np.sin(phase.astype(np.float64))]
    return np.stack(images).astype(np.float32)


def harmonic_of(cos_one, sin_one, harmonic):
    if harmonic == 1:
        return cos_one, sin_one
    return cos_one * cos_one - sin_one * sin_one, 2.0 * (sin_one * cos_one)


def blurred(mixed, image, taps, begin, step):
    reach = (len(taps) - 1) // 2
    acc = None
    for offset in range(-reach, reach + 1):
        term = taps[offset + reach] * mixed[image, pl.ds(begin + PAD - offset, step), :]
        acc = term if acc is None else acc + term
    return acc


def band_rows(mixed, images, taps, table, weight, band, begin, step):
    at = pl.ds(begin + (table.shape[1] - mixed.shape[1]) // 2 + PAD, step)
    parts = [wide(blurred(mixed, image, cut, begin, step)) for image, cut in zip(images, taps)]
    product = narrow(wide_dot(jnp.concatenate(parts, axis=0), weight))
    acc = None
    for orient in range(len(images) // 2):
        cos_pattern, sin_pattern = harmonic_of(
            table[2 * orient, at, :], table[2 * orient + 1, at, :], band
        )
        even = product[2 * orient * step : (2 * orient + 1) * step]
        odd = product[(2 * orient + 1) * step : (2 * orient + 2) * step]
        term = cos_pattern * even - sin_pattern * odd
        acc = term if acc is None else acc + term
    return acc


def put(out, index, band, values):
    width = out.shape[2]
    shares = values.shape[0] // width
    for share in range(shares):
        out[index * shares + share, band] = values[share * width : (share + 1) * width]


def scaled_taps(taps_ref, band, scale):
    return [taps_ref[band, at] * scale for at in range(taps_ref.shape[1])]


def data_kernel(
    phase_hbm, taps_hbm, frames_hbm, blur_hbm, table_hbm, out_hbm,
    raw, summed, mixed, weight, table, blur_rows, out, phase_ref, taps_ref,
    frame_sems, side_sems, out_sems,
):
    orients, phases = raw.shape[0], raw.shape[1]
    loop_width = raw.shape[2]
    bands = out.shape[1]
    phase_copy = pltpu.make_async_copy(phase_hbm, phase_ref, side_sems.at[0])
    phase_copy.start()
    copies = []
    for orient in range(orients):
        row = []
        for index in range(phases):
            copy = pltpu.make_async_copy(
                frames_hbm.at[orient, index, 0],
                raw.at[orient, index],
                frame_sems.at[orient, index],
            )
            copy.start()
            row.append(copy)
        copies.append(row)
    taps_copy = pltpu.make_async_copy(taps_hbm, taps_ref, side_sems.at[1])
    taps_copy.start()
    blur_copy = pltpu.make_async_copy(blur_hbm, blur_rows, side_sems.at[2])
    blur_copy.start()
    table_copy = pltpu.make_async_copy(table_hbm, table, side_sems.at[3])
    table_copy.start()
    step = loop_width // 2
    reach = (taps_ref.shape[1] - 1) // 2
    total = 4 * orients
    count = orients * phases
    first_sine, second_sine = math.sin(2 * math.pi / 5), math.sin(4 * math.pi / 5)
    ratio = second_sine / first_sine
    phase_copy.wait()
    for orient in range(orients):
        holder = []
        for step_index in range(phases):
            at_step = 0
            for index in range(1, phases):
                at_step = jnp.where(phase_ref[orient, index] == step_index, index, at_step)
            holder.append(at_step)
        for copy in copies[orient]:
            copy.wait()

        def mix(index, carry):
            rows = pl.ds(pl.multiple_of(index * step, step), step)
            at = pl.ds(pl.multiple_of(index * step + PAD, 8), step)
            f0, f1, f2, f3, f4 = [raw[orient, k, rows, :] for k in holder]
            near, far, near_odd, far_odd = f1 + f4, f2 + f3, f1 - f4, f2 - f3
            both = near + far
            even = (4 * f0 - both).astype(jnp.float32)
            swing = (near - far).astype(jnp.float32) * math.sqrt(5.0)
            near_odd = near_odd.astype(jnp.float32)
            far_odd = far_odd.astype(jnp.float32)
            mixed[2 * orient, at, :] = even + swing
            mixed[2 * orient + 1, at, :] = near_odd + ratio * far_odd
            mixed[2 * (orients + orient), at, :] = even - swing
            mixed[2 * (orients + orient) + 1, at, :] = ratio * near_odd - far_odd
            plain = f0 + both
            if orient:
                plain = plain + summed[rows, :]
            if orient < orients - 1:
                summed[rows, :] = plain
            else:
                mixed[total, at, :] = plain.astype(jnp.float32) * data_scale - 2.0 * count
            return carry

        lax.fori_loop(0, loop_width // step, mix, 0)
    for image in range(total + 1):
        mixed[image, PAD - reach : PAD, :] = mixed[
            image, loop_width + PAD - reach : loop_width + PAD, :
        ]
        mixed[image, loop_width + PAD : loop_width + PAD + reach, :] = mixed[
            image, PAD : PAD + reach, :
        ]
    taps_copy.wait()
    blur_copy.wait()
    for band in range(bands):
        weight[band] = weights(blur_rows[band])
    even_scale, odd_scale = data_scale / (4.0 * count), data_scale * first_sine / count
    taps = [scaled_taps(taps_ref, 0, 1.0 / count)]
    for band in range(1, bands):
        taps.append(
            [scaled_taps(taps_ref, band, even_scale), scaled_taps(taps_ref, band, odd_scale)]
            * orients
        )

    def plain_out(index, carry):
        begin = pl.multiple_of(index * step, step)
        rows = blurred(mixed, total, taps[0], begin, step)
        put(out, index, 0, narrow(wide_dot(wide(rows), weight[0])))
        return carry

    lax.fori_loop(0, loop_width // step, plain_out, 0)
    out_copies = [pltpu.make_async_copy(out.at[:, 0], out_hbm.at[:, 0], out_sems.at[0])]
    out_copies[0].start()
    table_copy.wait()
    for band in range(1, bands):
        images = list(range(2 * orients * (band - 1), 2 * orients * band))

        def band_out(index, carry):
            begin = pl.multiple_of(index * step, step)
            put(
                out,
                index,
                band,
                band_rows(mixed, images, taps[band], table, weight[band], band, begin, step),
            )
            return carry

        lax.fori_loop(0, loop_width // step, band_out, 0)
        out_copies.append(
            pltpu.make_async_copy(out.at[:, band], out_hbm.at[:, band], out_sems.at[band])
        )
        out_copies[band].start()
    for copy in out_copies:
        copy.wait()


def data_sums(frames, phase_index, row_blur, column_taps, table, chunks):
    orients, phases, _, loop_width, row_count = frames.shape
    bands = row_blur.shape[0]
    width = loop_width // chunks
    anywhere = pl.BlockSpec(memory_space=pltpu.HBM)
    return pl.pallas_call(
        data_kernel,
        out_shape=jax.ShapeDtypeStruct((chunks, bands, width, row_count), jnp.float32),
        in_specs=[anywhere] * 5,
        out_specs=anywhere,
        scratch_shapes=[
            pltpu.VMEM((orients, phases, loop_width, row_count), jnp.int32),
            pltpu.VMEM((loop_width, row_count), jnp.int32),
            pltpu.VMEM((4 * orients + 1, loop_width + 2 * PAD, row_count), jnp.float32),
            pltpu.VMEM((bands, 2 * row_count, 2 * row_count), jnp.bfloat16),
            pltpu.VMEM(table.shape, jnp.float32),
            pltpu.VMEM(row_blur.shape, jnp.float32),
            pltpu.VMEM((chunks, bands, width, row_count), jnp.float32),
            pltpu.SMEM(phase_index.shape, jnp.int32),
            pltpu.SMEM(column_taps.shape, jnp.float32),
            pltpu.SemaphoreType.DMA((orients, phases)),
            pltpu.SemaphoreType.DMA((4,)),
            pltpu.SemaphoreType.DMA((bands,)),
        ],
        cost_estimate=pl.CostEstimate(
            flops=13 * loop_width * 2 * 256 * 256, bytes_accessed=frames.size * 4, transcendentals=0
        ),
        compiler_params=pltpu.CompilerParams(vmem_limit_bytes=63 << 20),
        name="data_sums",
    )(phase_index, column_taps, frames, row_blur, table)


def estimate_kernel(taps_ref, axial_ref, table_ref, blur_ref, out_ref):
    bands, _, planes, _ = axial_ref.shape
    orients = table_ref.shape[0] // 2
    reach = (taps_ref.shape[1] - 1) // 2
    span = 2 * reach
    step = max(d for d in range(1, 23) if out_ref.shape[0] % d == 0 and (d == 1 or d * planes <= 352))

    def lags_of(band, scale):
        return [
            scale
            * sum(
                taps_ref[band, d] * taps_ref[band, d + shift]
                for d in range(0, 2 * reach + 1 - shift)
            )
            for shift in range(span + 1)
        ]

    def filtered(columns, lags):
        rows = []
        for i in range(step):
            acc = lags[0] * columns[i + span]
            for shift in range(1, span + 1):
                acc = acc + lags[shift] * (columns[i + span - shift] + columns[i + span + shift])
            rows.append(wide(acc))
        return rows

    def weight_of(band):
        matrix = blur_ref[band]
        return weights(
            lax.dot_general(
                matrix,
                matrix,
                (((0,), (0,)), ((), ())),
                preferred_element_type=jnp.float32,
                precision=lax.Precision.HIGHEST,
            )
        )

    weight = [weight_of(band) for band in range(bands)]
    lags = [lags_of(0, 1.0)] + [lags_of(band, 0.5 / orients) for band in range(1, bands)]

    def chunk(index, carry):
        begin = index * step
        rows = filtered([axial_ref[0, begin + i] for i in range(step + 2 * span)], lags[0])
        product = narrow(wide_dot(jnp.concatenate(rows, axis=0), weight[0]))
        acc = [product[i * planes : (i + 1) * planes] for i in range(step)]
        for band in range(1, bands):
            rows = []
            patterns = []
            for orient in range(orients):
                pairs = [
                    harmonic_of(
                        table_ref[2 * orient, pl.ds(begin + i, 1), :],
                        table_ref[2 * orient + 1, pl.ds(begin + i, 1), :],
                        band,
                    )
                    for i in range(step + 2 * span)
                ]
                for part in range(2):
                    columns = [
                        pairs[i][part] * axial_ref[band, begin + i]
                        for i in range(step + 2 * span)
                    ]
                    rows += filtered(columns, lags[band])
                    patterns.append([pairs[i + span][part] for i in range(step)])
            product = narrow(wide_dot(jnp.concatenate(rows, axis=0), weight[band]))
            for which, pattern in enumerate(patterns):
                for i in range(step):
                    at = (which * step + i) * planes
                    acc[i] = acc[i] + pattern[i] * product[at : at + planes]
        for i in range(step):
            out_ref[begin + i] = acc[i]
        return carry

    lax.fori_loop(0, out_ref.shape[0] // step, chunk, 0)


def estimate_part(axial, table, row_blur, column_taps):
    _, padded, planes, row_count = axial.shape
    orients = table.shape[0] // 2
    width = padded - 2 * (column_taps.shape[1] - 1)
    smem = pl.BlockSpec(memory_space=pltpu.SMEM)
    vmem = pl.BlockSpec(memory_space=pltpu.VMEM)
    rows = 2 * orients * width * planes
    return pl.pallas_call(
        estimate_kernel,
        out_shape=jax.ShapeDtypeStruct((width, planes, row_count), jnp.float32),
        in_specs=[smem, vmem, vmem, vmem],
        out_specs=vmem,
        cost_estimate=pl.CostEstimate(
            flops=40 * rows * 2 * 256 * 256, bytes_accessed=axial.size * 4, transcendentals=0
        ),
        compiler_params=pltpu.CompilerParams(vmem_limit_bytes=40 << 20),
        name="estimate_part",
    )(column_taps, axial, table, row_blur)


def combine_kernel(adjoint_ref, estimate_ref, received_ref, *refs, places):
    out_ref = refs[-1]
    planes, _ = estimate_ref.shape[1:]
    depth = adjoint_ref.shape[1]
    width = received_ref.shape[0] // depth
    span = (estimate_ref.shape[0] - width) // 2
    high, low = split(adjoint_ref[...])
    left_side = jnp.concatenate([high, high, low], axis=1)
    for index in range(width):
        high, low = split(received_ref[pl.ds(index, depth, stride=width), :])
        right_side = jnp.concatenate([high, low, high], axis=0)
        acc = estimate_ref[span + index]
        for ref, (begin, count) in zip(refs, places):
            if begin <= index < begin + count:
                acc = acc + ref[index - begin]
        out_ref[pl.ds(index, planes, stride=width), :] = acc - wide_dot(left_side, right_side)


def combine(forward, from_estimate, pieces, places, received):
    planes, row_count = from_estimate.shape[1:]
    depth = forward.shape[0] * planes
    width = received.size // (depth * row_count)
    adjoint = forward.transpose(2, 1, 0).reshape(planes, depth)
    vmem = pl.BlockSpec(memory_space=pltpu.VMEM)
    return pl.pallas_call(
        functools.partial(combine_kernel, places=places),
        out_shape=jax.ShapeDtypeStruct((planes * width, row_count), jnp.float32),
        in_specs=[vmem] * (3 + len(pieces)),
        out_specs=vmem,
        cost_estimate=pl.CostEstimate(
            flops=2 * received.size * planes, bytes_accessed=received.size * 4, transcendentals=0
        ),
        compiler_params=pltpu.CompilerParams(vmem_limit_bytes=24 << 20),
        name="combine",
    )(adjoint, from_estimate, received.reshape(depth * width, row_count), *pieces).reshape(
        planes, width, row_count
    )


def spread(from_estimate, span):
    ring = lax.axis_size("gz")
    width = from_estimate.shape[0] - 2 * span
    pieces, places = [], []
    hop, missing = 1, span
    while missing > 0:
        take = min(missing, width)
        piece = from_estimate[missing - take : missing]
        pieces.append(lax.ppermute(piece, "gz", [(s, (s - hop) % ring) for s in range(ring)]))
        places.append((width - take, take))
        begin = span + width * hop
        piece = from_estimate[begin : begin + take]
        pieces.append(lax.ppermute(piece, "gz", [(s, (s + hop) % ring) for s in range(ring)]))
        places.append((0, take))
        missing -= take
        hop += 1
    return pieces, places


def axial_matrices(axial_otf, order):
    planes = order.shape[0]
    wrapped = np.arange(planes)[:, None] * np.arange(planes)[None, :] % planes
    angle = wrapped * (2.0 * math.pi / planes)
    cosine = np.cos(angle).astype(np.float32)
    sine = np.sin(angle).astype(np.float32)
    wrapped = order[:, None] * np.arange(planes, dtype=np.int32)[None, :] % planes
    angle = wrapped.astype(jnp.float32) * (2.0 * math.pi / planes)
    real = axial_otf[:, 0, :, None]
    imag = axial_otf[:, 1, :, None]
    inner = jnp.concatenate(
        [real * cosine + imag * sine, real * sine - imag * cosine], axis=1
    )
    both = jnp.concatenate([jnp.cos(angle), jnp.sin(angle)], axis=1) * (1.0 / planes)
    return jnp.einsum(
        "zk,mkw->mzw", both, inner, precision=lax.Precision.HIGHEST,
        preferred_element_type=jnp.float32,
    )


def by_permutes(ring):
    return ring <= 16 and ring & (ring - 1) == 0 and ring > 2


def exchange(sums):
    ring = lax.axis_size("gz")
    own = lax.axis_index("gz")
    if not by_permutes(ring):
        return lax.all_to_all(sums, "gz", 0, 0, tiled=True)
    core, chip = own % 2, own // 2
    paired = sums.reshape((ring // 2, 2) + sums.shape[1:])
    mine = lax.dynamic_index_in_dim(paired, core, 1, keepdims=False)
    other = lax.dynamic_index_in_dim(paired, 1 - core, 1, keepdims=False)
    other = lax.ppermute(other, "gz", [(s, s ^ 1) for s in range(ring)])
    both = jnp.stack([mine, other], axis=1)
    parts = []
    for bit in range(ring // 2):
        part = lax.dynamic_index_in_dim(both, chip ^ bit, 0, keepdims=False)
        if bit:
            part = lax.ppermute(part, "gz", [(s, s ^ (2 * bit)) for s in range(ring)])
        parts.append(part)
    return jnp.concatenate(parts, axis=0)


def shards(estimate, frames, phase_index, axial_otf, row_blur, column_taps):
    planes, width, row_count = estimate.shape
    ring = lax.axis_size("gz")
    orients = frames.shape[0]
    bands = row_blur.shape[0]
    span = column_taps.shape[1] - 1
    pad = -(-2 * span // 8) * 8
    table = jnp.asarray(pattern_table(orients, width * ring, row_count, pad))
    sums = data_sums(frames, phase_index, row_blur, column_taps, table, ring)
    received = exchange(sums)
    order = jnp.arange(planes, dtype=jnp.int32)
    if by_permutes(ring):
        order = order ^ lax.axis_index("gz")
    forward = axial_matrices(axial_otf, order)
    squared = jnp.einsum("mzw,mzv->mwv", forward, forward, precision=lax.Precision.HIGHEST)
    axial = exact_dot(squared.reshape(bands * planes, planes), estimate.reshape(planes, -1))
    axial = axial.reshape(bands, planes, width, row_count).transpose(0, 2, 1, 3)
    axial = jnp.pad(axial, ((0, 0), (2 * span, 2 * span), (0, 0), (0, 0)))
    begin = lax.axis_index("gz") * width + (pad - 2 * span)
    near = lax.dynamic_slice_in_dim(table, begin, width + 4 * span, axis=1)
    from_estimate = estimate_part(axial, near, row_blur, column_taps)
    pieces, places = spread(from_estimate, span)
    return combine(forward, from_estimate, pieces, places, received)


def solution(mesh):
    placed = (P(None, "gz", "groups"), P(None, None, "gz", None, "groups"), P(), P(), P(), P())
    return jax.shard_map(
        shards, mesh=mesh, in_specs=placed, out_specs=P(None, "gz", "groups"), check_vma=False
    )
```

```python
import math

import jax
import jax.numpy as jnp
import numpy as np
from jax import lax
from jax.experimental import pallas as pl
from jax.experimental.pallas import tpu as pltpu
from jax.sharding import PartitionSpec as P


pattern_period = 3.7
orient_base = 0.3
data_scale = 1.0 / 1024.0
PAD = 8
TABLE_PAD = 16


def exact_dot(left_side, right_side):
    return jnp.dot(
        left_side, right_side, preferred_element_type=jnp.float32, precision=lax.Precision.HIGHEST
    )


def split(values):
    high = values.astype(jnp.bfloat16)
    low = (values - high.astype(jnp.float32)).astype(jnp.bfloat16)
    return high, low


def wide(values):
    high, low = split(values)
    return jnp.concatenate([high, low], axis=1)


def weights(matrix):
    row = wide(matrix)
    return jnp.concatenate([row, row], axis=0)


def narrow(product):
    half = product.shape[1] // 2
    return product[:, :half] + product[:, half:]


def wide_dot(left_side, right_side):
    return jnp.dot(left_side, right_side, preferred_element_type=jnp.float32)


def pattern_table(orients, loop_width, row_count, pad):
    columns = np.arange(-pad, loop_width + pad) % loop_width
    rows = np.arange(row_count)
    images = []
    for orient in range(orients):
        direction = orient_base + 2.0 * math.pi * orient / 3.0
        phase = (
            columns.astype(np.float32)[:, None] * np.float32(math.cos(direction))
            + rows.astype(np.float32)[None, :] * np.float32(math.sin(direction))
        ) * np.float32(2.0 * math.pi / pattern_period)
        images += [np.cos(phase.astype(np.float64)), np.sin(phase.astype(np.float64))]
    return np.stack(images).astype(np.float32)


def harmonic_of(cos_one, sin_one, harmonic):
    if harmonic == 1:
        return cos_one, sin_one
    return cos_one * cos_one - sin_one * sin_one, 2.0 * (sin_one * cos_one)


def blurred(mixed, image, taps, begin, step):
    reach = (len(taps) - 1) // 2
    acc = None
    for offset in range(-reach, reach + 1):
        term = taps[offset + reach] * mixed[image, pl.ds(begin + PAD - offset, step), :]
        acc = term if acc is None else acc + term
    return acc


def band_rows(mixed, images, taps, table, weight, band, begin, step):
    at = pl.ds(begin + (table.shape[1] - mixed.shape[1]) // 2 + PAD, step)
    parts = [wide(blurred(mixed, image, cut, begin, step)) for image, cut in zip(images, taps)]
    product = narrow(wide_dot(jnp.concatenate(parts, axis=0), weight))
    acc = None
    for orient in range(len(images) // 2):
        cos_pattern, sin_pattern = harmonic_of(
            table[2 * orient, at, :], table[2 * orient + 1, at, :], band
        )
        even = product[2 * orient * step : (2 * orient + 1) * step]
        odd = product[(2 * orient + 1) * step : (2 * orient + 2) * step]
        term = cos_pattern * even - sin_pattern * odd
        acc = term if acc is None else acc + term
    return acc


def put(out, index, band, values):
    width = out.shape[3]
    cores = out.shape[1]
    shares = values.shape[0] // width
    for share in range(shares):
        rows = values[share * width : (share + 1) * width]
        out[index * (shares // cores) + share // cores, share % cores, band] = rows


def scaled_taps(taps_ref, band, scale):
    return [taps_ref[band, at] * scale for at in range(taps_ref.shape[1])]


def data_kernel(
    phase_hbm, taps_hbm, frames_hbm, blur_hbm, table_hbm, *refs,
):
    targets, near_hbm, scratch = refs[:-13], refs[-13], refs[-12:]
    raw, summed, mixed, weight, table, blur_rows, out, phase_ref, taps_ref = scratch[:9]
    frame_sems, side_sems, out_sems = scratch[9:]

    orients, phases = raw.shape[0], raw.shape[1]
    loop_width = raw.shape[2]
    bands, width = out.shape[2], out.shape[3]
    core = lax.axis_index("gz") % 2
    phase_copy = pltpu.make_async_copy(phase_hbm, phase_ref, side_sems.at[0])
    phase_copy.start()
    copies = []
    for orient in range(orients):
        row = []
        for index in range(phases):
            copy = pltpu.make_async_copy(
                frames_hbm.at[orient, index, 0],
                raw.at[orient, index],
                frame_sems.at[orient, index],
            )
            copy.start()
            row.append(copy)
        copies.append(row)
    taps_copy = pltpu.make_async_copy(taps_hbm, taps_ref, side_sems.at[1])
    taps_copy.start()
    blur_copy = pltpu.make_async_copy(blur_hbm, blur_rows, side_sems.at[2])
    blur_copy.start()
    table_copy = pltpu.make_async_copy(table_hbm, table, side_sems.at[3])
    table_copy.start()
    step = loop_width // 2
    reach = (taps_ref.shape[1] - 1) // 2
    total = 4 * orients
    count = orients * phases
    first_sine, second_sine = math.sin(2 * math.pi / 5), math.sin(4 * math.pi / 5)
    ratio = second_sine / first_sine
    phase_copy.wait()
    for orient in range(orients):
        holder = []
        for step_index in range(phases):
            at_step = 0
            for index in range(1, phases):
                at_step = jnp.where(phase_ref[orient, index] == step_index, index, at_step)
            holder.append(at_step)
        for copy in copies[orient]:
            copy.wait()

        def mix(index, carry):
            rows = pl.ds(pl.multiple_of(index * step, step), step)
            at = pl.ds(pl.multiple_of(index * step + PAD, 8), step)
            f0, f1, f2, f3, f4 = [raw[orient, k, rows, :] for k in holder]
            near, far, near_odd, far_odd = f1 + f4, f2 + f3, f1 - f4, f2 - f3
            both = near + far
            even = (4 * f0 - both).astype(jnp.float32)
            swing = (near - far).astype(jnp.float32) * math.sqrt(5.0)
            near_odd = near_odd.astype(jnp.float32)
            far_odd = far_odd.astype(jnp.float32)
            mixed[2 * orient, at, :] = even + swing
            mixed[2 * orient + 1, at, :] = near_odd + ratio * far_odd
            mixed[2 * (orients + orient), at, :] = even - swing
            mixed[2 * (orients + orient) + 1, at, :] = ratio * near_odd - far_odd
            plain = f0 + both
            if orient:
                plain = plain + summed[rows, :]
            if orient < orients - 1:
                summed[rows, :] = plain
            else:
                mixed[total, at, :] = plain.astype(jnp.float32) * data_scale - 2.0 * count
            return carry

        lax.fori_loop(0, loop_width // step, mix, 0)
    for image in range(total + 1):
        mixed[image, PAD - reach : PAD, :] = mixed[
            image, loop_width + PAD - reach : loop_width + PAD, :
        ]
        mixed[image, loop_width + PAD : loop_width + PAD + reach, :] = mixed[
            image, PAD : PAD + reach, :
        ]
    taps_copy.wait()
    blur_copy.wait()
    for band in range(bands):
        weight[band] = weights(blur_rows[band])
    even_scale, odd_scale = data_scale / (4.0 * count), data_scale * first_sine / count
    taps = [scaled_taps(taps_ref, 0, 1.0 / count)]
    for band in range(1, bands):
        taps.append(
            [scaled_taps(taps_ref, band, even_scale), scaled_taps(taps_ref, band, odd_scale)]
            * orients
        )

    def plain_out(index, carry):
        begin = pl.multiple_of(index * step, step)
        rows = blurred(mixed, total, taps[0], begin, step)
        put(out, index, 0, narrow(wide_dot(wide(rows), weight[0])))
        return carry

    lax.fori_loop(0, loop_width // step, plain_out, 0)
    out_copies = []

    def ship(band):
        for at, target in enumerate(targets):
            half = (core + at) % 2 if len(targets) > 1 else 0
            copy = pltpu.make_async_copy(
                out.at[:, half, band], target.at[:, band], out_sems.at[at, band]
            )
            copy.start()
            out_copies.append(copy)

    ship(0)
    table_copy.wait()
    begin = 0 if width % 8 else pl.multiple_of(lax.axis_index("gz") * width, 8)
    own_rows = pl.ds(begin, near_hbm.shape[1])
    out_copies.append(pltpu.make_async_copy(table.at[:, own_rows], near_hbm, side_sems.at[4]))
    out_copies[-1].start()
    for band in range(1, bands):
        images = list(range(2 * orients * (band - 1), 2 * orients * band))

        def band_out(index, carry):
            begin = pl.multiple_of(index * step, step)
            put(
                out,
                index,
                band,
                band_rows(mixed, images, taps[band], table, weight[band], band, begin, step),
            )
            return carry

        lax.fori_loop(0, loop_width // step, band_out, 0)
        ship(band)
    for copy in out_copies:
        copy.wait()


def data_sums(frames, phase_index, row_blur, column_taps, table, chunks, cores):
    orients, phases, _, loop_width, row_count = frames.shape
    bands = row_blur.shape[0]
    width = loop_width // chunks
    near = (table.shape[0], -(-width // 8) * 8 + 2 * TABLE_PAD, row_count)
    anywhere = pl.BlockSpec(memory_space=pltpu.HBM)
    return pl.pallas_call(
        data_kernel,
        out_shape=[
            jax.ShapeDtypeStruct((chunks // cores, bands, width, row_count), jnp.float32)
        ]
        * cores
        + [jax.ShapeDtypeStruct(near, jnp.float32)],
        in_specs=[anywhere] * 5,
        out_specs=[anywhere] * (cores + 1),
        scratch_shapes=[
            pltpu.VMEM((orients, phases, loop_width, row_count), jnp.int32),
            pltpu.VMEM((loop_width, row_count), jnp.int32),
            pltpu.VMEM((4 * orients + 1, loop_width + 2 * PAD, row_count), jnp.float32),
            pltpu.VMEM((bands, 2 * row_count, 2 * row_count), jnp.bfloat16),
            pltpu.VMEM(table.shape, jnp.float32),
            pltpu.VMEM(row_blur.shape, jnp.float32),
            pltpu.VMEM((chunks // cores, cores, bands, width, row_count), jnp.float32),
            pltpu.SMEM(phase_index.shape, jnp.int32),
            pltpu.SMEM(column_taps.shape, jnp.float32),
            pltpu.SemaphoreType.DMA((orients, phases)),
            pltpu.SemaphoreType.DMA((5,)),
            pltpu.SemaphoreType.DMA((cores, bands)),
        ],
        cost_estimate=pl.CostEstimate(
            flops=13 * loop_width * 2 * 256 * 256, bytes_accessed=frames.size * 4, transcendentals=0
        ),
        compiler_params=pltpu.CompilerParams(vmem_limit_bytes=63 << 20),
        name="data_sums",
    )(phase_index, column_taps, frames, row_blur, table)


def ends():
    own = lax.axis_index("gz")
    return own == 0, own == lax.axis_size("gz") - 1


def estimate_kernel(taps_ref, axial_ref, table_ref, blur_ref, out_ref, *refs):
    edge_ref = refs[0] if refs else None
    width = out_ref.shape[0]
    bands, extended, planes, _ = axial_ref.shape
    orients = table_ref.shape[0] // 2
    reach = (taps_ref.shape[1] - 1) // 2
    span = 2 * reach

    def lags_of(band, scale):
        return [
            scale
            * sum(
                taps_ref[band, d] * taps_ref[band, d + shift]
                for d in range(0, 2 * reach + 1 - shift)
            )
            for shift in range(span + 1)
        ]

    def filtered(columns, lags, step):
        rows = []
        for i in range(step):
            acc = lags[0] * columns[i + span]
            for shift in range(1, span + 1):
                acc = acc + lags[shift] * (columns[i + span - shift] + columns[i + span + shift])
            rows.append(wide(acc))
        return rows

    def weight_of(band):
        matrix = blur_ref[band]
        return weights(
            lax.dot_general(
                matrix,
                matrix,
                (((0,), (0,)), ((), ())),
                preferred_element_type=jnp.float32,
                precision=lax.Precision.HIGHEST,
            )
        )

    weight = [weight_of(band) for band in range(bands)]
    extra = (extended - width) // 2 - span
    lags = [lags_of(0, 1.0)] + [lags_of(band, 0.5 / orients) for band in range(1, bands)]

    def columns_from(begin, step, target, place):
        reads = range(step + 2 * span)
        rows = filtered([axial_ref[0, begin + i + extra] for i in reads], lags[0], step)
        product = narrow(wide_dot(jnp.concatenate(rows, axis=0), weight[0]))
        acc = [product[i * planes : (i + 1) * planes] for i in range(step)]
        for band in range(1, bands):
            rows = []
            patterns = []
            for orient in range(orients):
                pairs = [
                    harmonic_of(
                        table_ref[2 * orient, pl.ds(begin + i + TABLE_PAD - span, 1), :],
                        table_ref[2 * orient + 1, pl.ds(begin + i + TABLE_PAD - span, 1), :],
                        band,
                    )
                    for i in reads
                ]
                for part in range(2):
                    columns = [pairs[i][part] * axial_ref[band, begin + i + extra] for i in reads]
                    rows += filtered(columns, lags[band], step)
                    patterns.append([pairs[i + span][part] for i in range(step)])
            product = narrow(wide_dot(jnp.concatenate(rows, axis=0), weight[band]))
            for which, pattern in enumerate(patterns):
                for i in range(step):
                    at = (which * step + i) * planes
                    acc[i] = acc[i] + pattern[i] * product[at : at + planes]
        for i in range(step):
            target[place + i] = acc[i]

    step = max(d for d in range(1, 23) if width % d == 0 and (d == 1 or d * planes <= 352))

    def chunk(index, carry):
        columns_from(index * step, step, out_ref, index * step)
        return carry

    lax.fori_loop(0, width // step, chunk, 0)
    if edge_ref is not None:
        first, last = ends()

        @pl.when(first | last)
        def _():
            columns_from(jnp.where(first, -span, width), span, edge_ref, 0)

        @pl.when(~(first | last))
        def _():
            edge_ref[...] = jnp.zeros_like(edge_ref)


def estimate_part(axial, table, row_blur, column_taps, width):
    _, extended, planes, row_count = axial.shape
    span = column_taps.shape[1] - 1
    shapes = [(width, planes, row_count)]
    if extended > width + 2 * span:
        shapes.append((span, planes, row_count))
    smem = pl.BlockSpec(memory_space=pltpu.SMEM)
    vmem = pl.BlockSpec(memory_space=pltpu.VMEM)
    rows = table.shape[0] * width * planes
    return pl.pallas_call(
        estimate_kernel,
        out_shape=[jax.ShapeDtypeStruct(shape, jnp.float32) for shape in shapes],
        in_specs=[smem, vmem, vmem, vmem],
        out_specs=[vmem] * len(shapes),
        cost_estimate=pl.CostEstimate(
            flops=40 * rows * 2 * 256 * 256, bytes_accessed=axial.size * 4, transcendentals=0
        ),
        compiler_params=pltpu.CompilerParams(vmem_limit_bytes=40 << 20),
        name="estimate_part",
    )(column_taps, axial, table, row_blur)


def combine_kernel(adjoint_ref, estimate_ref, received_ref, *refs):
    out_ref = refs[-1]
    width, planes, row_count = estimate_ref.shape
    depth = adjoint_ref.shape[1]
    high, low = split(adjoint_ref[...])
    left_side = jnp.concatenate([high, high, low], axis=1)
    for index in range(0, width, 2):
        columns = [received_ref[pl.ds(index + i, depth, stride=width), :] for i in range(2)]
        high, low = split(jnp.concatenate(columns, axis=1))
        right_side = jnp.concatenate([high, low, high], axis=0)
        product = wide_dot(left_side, right_side)
        for i in range(2):
            acc = estimate_ref[index + i] - product[:, i * row_count : (i + 1) * row_count]
            if len(refs) > 1:
                edge_ref = refs[0]
                span = edge_ref.shape[0]
                for end, begin in zip(ends(), (0, width - span)):
                    at = index + i - begin
                    if 0 <= at < span:
                        acc = acc + jnp.where(end, edge_ref[at], 0.0)
            out_ref[pl.ds(index + i, planes, stride=width), :] = acc


def combine(forward, from_estimate, received, edge):
    width, planes, row_count = from_estimate.shape
    depth = forward.shape[0] * planes
    adjoint = forward.transpose(2, 1, 0).reshape(planes, depth)
    vmem = pl.BlockSpec(memory_space=pltpu.VMEM)
    return pl.pallas_call(
        combine_kernel,
        out_shape=jax.ShapeDtypeStruct((planes * width, row_count), jnp.float32),
        in_specs=[vmem] * (3 + len(edge)),
        out_specs=vmem,
        cost_estimate=pl.CostEstimate(
            flops=2 * received.size * planes, bytes_accessed=received.size * 4, transcendentals=0
        ),
        compiler_params=pltpu.CompilerParams(vmem_limit_bytes=24 << 20),
        name="combine",
    )(adjoint, from_estimate, received.reshape(depth * width, row_count), *edge).reshape(
        planes, width, row_count
    )


def halo(estimate, span, closed):
    ring = lax.axis_size("gz")
    width = estimate.shape[1]
    lefts, rights = [], []
    hop, missing = 1, span
    while missing > 0:
        take = min(missing, width)
        forth = [(s, (s + hop) % ring) for s in range(ring if closed else ring - hop)]
        back = [(t, s) for s, t in forth]
        lefts.insert(0, lax.ppermute(estimate[:, width - take :], "gz", forth))
        rights.append(lax.ppermute(estimate[:, :take], "gz", back))
        missing -= take
        hop += 1
    return lefts + [estimate] + rights


def axial_matrices(axial_otf, order):
    planes = order.shape[0]
    wrapped = np.arange(planes)[:, None] * np.arange(planes)[None, :] % planes
    angle = wrapped * (2.0 * math.pi / planes)
    cosine = np.cos(angle).astype(np.float32)
    sine = np.sin(angle).astype(np.float32)
    wrapped = order[:, None] * np.arange(planes, dtype=np.int32)[None, :] % planes
    angle = wrapped.astype(jnp.float32) * (2.0 * math.pi / planes)
    real = axial_otf[:, 0, :, None]
    imag = axial_otf[:, 1, :, None]
    inner = jnp.concatenate(
        [real * cosine + imag * sine, real * sine - imag * cosine], axis=1
    )
    both = jnp.concatenate([jnp.cos(angle), jnp.sin(angle)], axis=1) * (1.0 / planes)
    return jnp.einsum(
        "zk,mkw->mzw", both, inner, precision=lax.Precision.HIGHEST,
        preferred_element_type=jnp.float32,
    )


def by_permutes(ring):
    return ring <= 16 and ring & (ring - 1) == 0 and ring > 2


def exchange(sums):
    ring = lax.axis_size("gz")
    if len(sums) == 1:
        return lax.all_to_all(sums[0], "gz", 0, 0, tiled=True)
    chip = lax.axis_index("gz") // 2
    mine, other = sums
    other = lax.ppermute(other, "gz", [(s, s ^ 1) for s in range(ring)])
    both = jnp.stack([mine, other], axis=1)
    parts = []
    for bit in range(ring // 2):
        part = lax.dynamic_index_in_dim(both, chip ^ bit, 0, keepdims=False)
        if bit:
            part = lax.ppermute(part, "gz", [(s, s ^ (2 * bit)) for s in range(ring)])
        parts.append(part)
    return jnp.concatenate(parts, axis=0)


def shards(estimate, frames, phase_index, axial_otf, row_blur, column_taps):
    planes, width, row_count = estimate.shape
    ring = lax.axis_size("gz")
    orients = frames.shape[0]
    bands = row_blur.shape[0]
    span = column_taps.shape[1] - 1
    table = jnp.asarray(pattern_table(orients, width * ring, row_count, TABLE_PAD))
    cores = 2 if by_permutes(ring) else 1
    open_loop = by_permutes(ring) and width >= span
    *sums, near = data_sums(frames, phase_index, row_blur, column_taps, table, ring, cores)
    if width % 8:
        begin = lax.axis_index("gz") * width
        near = lax.dynamic_slice_in_dim(table, begin, width + 2 * TABLE_PAD, axis=1)
    estimate, *sums = lax.optimization_barrier((estimate, *sums))
    pieces = halo(estimate, span, not open_loop)
    received = exchange(sums)
    order = jnp.arange(planes, dtype=jnp.int32)
    if by_permutes(ring):
        order = order ^ lax.axis_index("gz")
    forward = axial_matrices(axial_otf, order)
    squared = jnp.einsum("mzw,mzv->mwv", forward, forward, precision=lax.Precision.HIGHEST)
    extended = jnp.concatenate(pieces, axis=1)
    axial = exact_dot(squared.reshape(bands * planes, planes), extended.reshape(planes, -1))
    axial = axial.reshape(bands, planes, width + 2 * span, row_count)
    axial = axial.transpose(0, 2, 1, 3)
    if open_loop:
        axial = jnp.pad(axial, ((0, 0), (span, span), (0, 0), (0, 0)))
    from_estimate, *edge = estimate_part(axial, near, row_blur, column_taps, width)
    edge = [lax.ppermute(piece, "gz", [(0, ring - 1), (ring - 1, 0)]) for piece in edge]
    return combine(forward, from_estimate, received, edge)


def solution(mesh):
    placed = (P(None, "gz", "groups"), P(None, None, "gz", None, "groups"), P(), P(), P(), P())
    return jax.shard_map(
        shards, mesh=mesh, in_specs=placed, out_specs=P(None, "gz", "groups"), check_vma=False
    )
```

```python
import math

import jax
import jax.numpy as jnp
import numpy as np
from jax import lax
from jax.experimental import pallas as pl
from jax.experimental.pallas import tpu as pltpu
from jax.sharding import PartitionSpec as P


pattern_period = 3.7
orient_base = 0.3
data_scale = 1.0 / 1024.0
PAD = 8


def exact_dot(left_side, right_side):
    return jnp.dot(
        left_side, right_side, preferred_element_type=jnp.float32, precision=lax.Precision.HIGHEST
    )


def split(values):
    high = values.astype(jnp.bfloat16)
    low = (values - high.astype(jnp.float32)).astype(jnp.bfloat16)
    return high, low


def wide(values):
    high, low = split(values)
    return jnp.concatenate([high, low], axis=1)


def weights(matrix):
    row = wide(matrix)
    return jnp.concatenate([row, row], axis=0)


def narrow(product):
    half = product.shape[1] // 2
    return product[:, :half] + product[:, half:]


def wide_dot(left_side, right_side):
    return jnp.dot(left_side, right_side, preferred_element_type=jnp.float32)


def pattern_table(orients, loop_width, row_count, pad):
    columns = np.arange(-pad, loop_width + pad) % loop_width
    rows = np.arange(row_count)
    images = []
    for orient in range(orients):
        direction = orient_base + 2.0 * math.pi * orient / 3.0
        phase = (
            columns.astype(np.float32)[:, None] * np.float32(math.cos(direction))
            + rows.astype(np.float32)[None, :] * np.float32(math.sin(direction))
        ) * np.float32(2.0 * math.pi / pattern_period)
        images += [np.cos(phase.astype(np.float64)), np.sin(phase.astype(np.float64))]
    return np.stack(images).astype(np.float32)


def harmonic_of(cos_one, sin_one, harmonic):
    if harmonic == 1:
        return cos_one, sin_one
    return cos_one * cos_one - sin_one * sin_one, 2.0 * (sin_one * cos_one)


def blurred(mixed, image, taps, begin, step):
    reach = (len(taps) - 1) // 2
    acc = None
    for offset in range(-reach, reach + 1):
        term = taps[offset + reach] * mixed[image, pl.ds(begin + PAD - offset, step), :]
        acc = term if acc is None else acc + term
    return acc


def band_rows(mixed, images, taps, table, weight, band, begin, step):
    at = pl.ds(begin + (table.shape[1] - mixed.shape[1]) // 2 + PAD, step)
    parts = [wide(blurred(mixed, image, cut, begin, step)) for image, cut in zip(images, taps)]
    product = narrow(wide_dot(jnp.concatenate(parts, axis=0), weight))
    acc = None
    for orient in range(len(images) // 2):
        cos_pattern, sin_pattern = harmonic_of(
            table[2 * orient, at, :], table[2 * orient + 1, at, :], band
        )
        even = product[2 * orient * step : (2 * orient + 1) * step]
        odd = product[(2 * orient + 1) * step : (2 * orient + 2) * step]
        term = cos_pattern * even - sin_pattern * odd
        acc = term if acc is None else acc + term
    return acc


def put(out, index, band, values):
    width = out.shape[3]
    cores = out.shape[1]
    shares = values.shape[0] // width
    for share in range(shares):
        rows = values[share * width : (share + 1) * width]
        out[index * (shares // cores) + share // cores, share % cores, band] = rows


def scaled_taps(taps_ref, band, scale):
    return [taps_ref[band, at] * scale for at in range(taps_ref.shape[1])]


def data_kernel(
    phase_hbm, taps_hbm, frames_hbm, blur_hbm, table_hbm, *refs,
):
    targets, scratch = refs[:-12], refs[-12:]
    raw, summed, mixed, weight, table, blur_rows, out, phase_ref, taps_ref = scratch[:9]
    frame_sems, side_sems, out_sems = scratch[9:]

    orients, phases = raw.shape[0], raw.shape[1]
    loop_width = raw.shape[2]
    bands = out.shape[2]
    core = lax.axis_index("gz") % 2
    phase_copy = pltpu.make_async_copy(phase_hbm, phase_ref, side_sems.at[0])
    phase_copy.start()
    copies = []
    for orient in range(orients):
        row = []
        for index in range(phases):
            copy = pltpu.make_async_copy(
                frames_hbm.at[orient, index, 0],
                raw.at[orient, index],
                frame_sems.at[orient, index],
            )
            copy.start()
            row.append(copy)
        copies.append(row)
    taps_copy = pltpu.make_async_copy(taps_hbm, taps_ref, side_sems.at[1])
    taps_copy.start()
    blur_copy = pltpu.make_async_copy(blur_hbm, blur_rows, side_sems.at[2])
    blur_copy.start()
    table_copy = pltpu.make_async_copy(table_hbm, table, side_sems.at[3])
    table_copy.start()
    step = loop_width // 2
    reach = (taps_ref.shape[1] - 1) // 2
    total = 4 * orients
    count = orients * phases
    first_sine, second_sine = math.sin(2 * math.pi / 5), math.sin(4 * math.pi / 5)
    ratio = second_sine / first_sine
    phase_copy.wait()
    for orient in range(orients):
        holder = []
        for step_index in range(phases):
            at_step = 0
            for index in range(1, phases):
                at_step = jnp.where(phase_ref[orient, index] == step_index, index, at_step)
            holder.append(at_step)
        for copy in copies[orient]:
            copy.wait()

        def mix(index, carry):
            rows = pl.ds(pl.multiple_of(index * step, step), step)
            at = pl.ds(pl.multiple_of(index * step + PAD, 8), step)
            f0, f1, f2, f3, f4 = [raw[orient, k, rows, :] for k in holder]
            near, far, near_odd, far_odd = f1 + f4, f2 + f3, f1 - f4, f2 - f3
            both = near + far
            even = (4 * f0 - both).astype(jnp.float32)
            swing = (near - far).astype(jnp.float32) * math.sqrt(5.0)
            near_odd = near_odd.astype(jnp.float32)
            far_odd = far_odd.astype(jnp.float32)
            mixed[2 * orient, at, :] = even + swing
            mixed[2 * orient + 1, at, :] = near_odd + ratio * far_odd
            mixed[2 * (orients + orient), at, :] = even - swing
            mixed[2 * (orients + orient) + 1, at, :] = ratio * near_odd - far_odd
            plain = f0 + both
            if orient:
                plain = plain + summed[rows, :]
            if orient < orients - 1:
                summed[rows, :] = plain
            else:
                mixed[total, at, :] = plain.astype(jnp.float32) * data_scale - 2.0 * count
            return carry

        lax.fori_loop(0, loop_width // step, mix, 0)
    for image in range(total + 1):
        mixed[image, PAD - reach : PAD, :] = mixed[
            image, loop_width + PAD - reach : loop_width + PAD, :
        ]
        mixed[image, loop_width + PAD : loop_width + PAD + reach, :] = mixed[
            image, PAD : PAD + reach, :
        ]
    taps_copy.wait()
    blur_copy.wait()
    for band in range(bands):
        weight[band] = weights(blur_rows[band])
    even_scale, odd_scale = data_scale / (4.0 * count), data_scale * first_sine / count
    taps = [scaled_taps(taps_ref, 0, 1.0 / count)]
    for band in range(1, bands):
        taps.append(
            [scaled_taps(taps_ref, band, even_scale), scaled_taps(taps_ref, band, odd_scale)]
            * orients
        )

    def plain_out(index, carry):
        begin = pl.multiple_of(index * step, step)
        rows = blurred(mixed, total, taps[0], begin, step)
        put(out, index, 0, narrow(wide_dot(wide(rows), weight[0])))
        return carry

    lax.fori_loop(0, loop_width // step, plain_out, 0)
    out_copies = []

    def ship(band):
        for at, target in enumerate(targets):
            half = (core + at) % 2 if len(targets) > 1 else 0
            copy = pltpu.make_async_copy(
                out.at[:, half, band], target.at[:, band], out_sems.at[at, band]
            )
            copy.start()
            out_copies.append(copy)

    ship(0)
    table_copy.wait()
    for band in range(1, bands):
        images = list(range(2 * orients * (band - 1), 2 * orients * band))

        def band_out(index, carry):
            begin = pl.multiple_of(index * step, step)
            put(
                out,
                index,
                band,
                band_rows(mixed, images, taps[band], table, weight[band], band, begin, step),
            )
            return carry

        lax.fori_loop(0, loop_width // step, band_out, 0)
        ship(band)
    for copy in out_copies:
        copy.wait()


def data_sums(frames, phase_index, row_blur, column_taps, table, chunks, cores):
    orients, phases, _, loop_width, row_count = frames.shape
    bands = row_blur.shape[0]
    width = loop_width // chunks
    anywhere = pl.BlockSpec(memory_space=pltpu.HBM)
    return pl.pallas_call(
        data_kernel,
        out_shape=[
            jax.ShapeDtypeStruct((chunks // cores, bands, width, row_count), jnp.float32)
        ]
        * cores,
        in_specs=[anywhere] * 5,
        out_specs=[anywhere] * cores,
        scratch_shapes=[
            pltpu.VMEM((orients, phases, loop_width, row_count), jnp.int32),
            pltpu.VMEM((loop_width, row_count), jnp.int32),
            pltpu.VMEM((4 * orients + 1, loop_width + 2 * PAD, row_count), jnp.float32),
            pltpu.VMEM((bands, 2 * row_count, 2 * row_count), jnp.bfloat16),
            pltpu.VMEM(table.shape, jnp.float32),
            pltpu.VMEM(row_blur.shape, jnp.float32),
            pltpu.VMEM((chunks // cores, cores, bands, width, row_count), jnp.float32),
            pltpu.SMEM(phase_index.shape, jnp.int32),
            pltpu.SMEM(column_taps.shape, jnp.float32),
            pltpu.SemaphoreType.DMA((orients, phases)),
            pltpu.SemaphoreType.DMA((4,)),
            pltpu.SemaphoreType.DMA((cores, bands)),
        ],
        cost_estimate=pl.CostEstimate(
            flops=13 * loop_width * 2 * 256 * 256, bytes_accessed=frames.size * 4, transcendentals=0
        ),
        compiler_params=pltpu.CompilerParams(vmem_limit_bytes=63 << 20),
        name="data_sums",
    )(phase_index, column_taps, frames, row_blur, table)


def estimate_kernel(taps_ref, axial_ref, table_hbm, blur_ref, out_ref, table_ref, sem):
    width = out_ref.shape[0]
    source = table_hbm
    if table_hbm.shape != table_ref.shape:
        begin = pl.multiple_of(lax.axis_index("gz") * width, 8)
        source = table_hbm.at[:, pl.ds(begin, table_ref.shape[1]), :]
    table_copy = pltpu.make_async_copy(source, table_ref, sem)
    table_copy.start()
    bands, _, planes, _ = axial_ref.shape
    orients = table_ref.shape[0] // 2
    reach = (taps_ref.shape[1] - 1) // 2
    span = 2 * reach
    step = max(d for d in range(1, 23) if out_ref.shape[0] % d == 0 and (d == 1 or d * planes <= 352))

    def lags_of(band, scale):
        return [
            scale
            * sum(
                taps_ref[band, d] * taps_ref[band, d + shift]
                for d in range(0, 2 * reach + 1 - shift)
            )
            for shift in range(span + 1)
        ]

    def filtered(columns, lags):
        rows = []
        for i in range(step):
            acc = lags[0] * columns[i + span]
            for shift in range(1, span + 1):
                acc = acc + lags[shift] * (columns[i + span - shift] + columns[i + span + shift])
            rows.append(wide(acc))
        return rows

    def weight_of(band):
        matrix = blur_ref[band]
        return weights(
            lax.dot_general(
                matrix,
                matrix,
                (((0,), (0,)), ((), ())),
                preferred_element_type=jnp.float32,
                precision=lax.Precision.HIGHEST,
            )
        )

    weight = [weight_of(band) for band in range(bands)]
    shift = PAD - span
    table_copy.wait()
    lags = [lags_of(0, 1.0)] + [lags_of(band, 0.5 / orients) for band in range(1, bands)]

    def chunk(index, carry):
        begin = index * step
        rows = filtered([axial_ref[0, begin + i] for i in range(step + 2 * span)], lags[0])
        product = narrow(wide_dot(jnp.concatenate(rows, axis=0), weight[0]))
        acc = [product[i * planes : (i + 1) * planes] for i in range(step)]
        for band in range(1, bands):
            rows = []
            patterns = []
            for orient in range(orients):
                pairs = [
                    harmonic_of(
                        table_ref[2 * orient, pl.ds(begin + i + shift, 1), :],
                        table_ref[2 * orient + 1, pl.ds(begin + i + shift, 1), :],
                        band,
                    )
                    for i in range(step + 2 * span)
                ]
                for part in range(2):
                    columns = [
                        pairs[i][part] * axial_ref[band, begin + i]
                        for i in range(step + 2 * span)
                    ]
                    rows += filtered(columns, lags[band])
                    patterns.append([pairs[i + span][part] for i in range(step)])
            product = narrow(wide_dot(jnp.concatenate(rows, axis=0), weight[band]))
            for which, pattern in enumerate(patterns):
                for i in range(step):
                    at = (which * step + i) * planes
                    acc[i] = acc[i] + pattern[i] * product[at : at + planes]
        for i in range(step):
            out_ref[begin + i] = acc[i]
        return carry

    lax.fori_loop(0, out_ref.shape[0] // step, chunk, 0)


def estimate_part(axial, table, row_blur, column_taps):
    _, extended, planes, row_count = axial.shape
    width = extended - 2 * (column_taps.shape[1] - 1)
    near = (table.shape[0], width + 2 * PAD, row_count)
    if width % 8:
        table = lax.dynamic_slice_in_dim(table, lax.axis_index("gz") * width, near[1], axis=1)
    smem = pl.BlockSpec(memory_space=pltpu.SMEM)
    vmem = pl.BlockSpec(memory_space=pltpu.VMEM)
    anywhere = pl.BlockSpec(memory_space=pltpu.HBM)
    rows = table.shape[0] * width * planes
    return pl.pallas_call(
        estimate_kernel,
        out_shape=jax.ShapeDtypeStruct((width, planes, row_count), jnp.float32),
        in_specs=[smem, vmem, anywhere, vmem],
        out_specs=vmem,
        scratch_shapes=[pltpu.VMEM(near, jnp.float32), pltpu.SemaphoreType.DMA],
        cost_estimate=pl.CostEstimate(
            flops=40 * rows * 2 * 256 * 256, bytes_accessed=axial.size * 4, transcendentals=0
        ),
        compiler_params=pltpu.CompilerParams(vmem_limit_bytes=40 << 20),
        name="estimate_part",
    )(column_taps, axial, table, row_blur)


def combine_kernel(adjoint_ref, estimate_ref, received_ref, out_ref):
    width, planes, row_count = estimate_ref.shape
    depth = adjoint_ref.shape[1]
    high, low = split(adjoint_ref[...])
    left_side = jnp.concatenate([high, high, low], axis=1)
    for index in range(0, width, 2):
        columns = [received_ref[pl.ds(index + i, depth, stride=width), :] for i in range(2)]
        high, low = split(jnp.concatenate(columns, axis=1))
        right_side = jnp.concatenate([high, low, high], axis=0)
        product = wide_dot(left_side, right_side)
        for i in range(2):
            out_ref[pl.ds(index + i, planes, stride=width), :] = (
                estimate_ref[index + i] - product[:, i * row_count : (i + 1) * row_count]
            )


def combine(forward, from_estimate, received):
    width, planes, row_count = from_estimate.shape
    depth = forward.shape[0] * planes
    adjoint = forward.transpose(2, 1, 0).reshape(planes, depth)
    vmem = pl.BlockSpec(memory_space=pltpu.VMEM)
    return pl.pallas_call(
        combine_kernel,
        out_shape=jax.ShapeDtypeStruct((planes * width, row_count), jnp.float32),
        in_specs=[vmem] * 3,
        out_specs=vmem,
        cost_estimate=pl.CostEstimate(
            flops=2 * received.size * planes, bytes_accessed=received.size * 4, transcendentals=0
        ),
        compiler_params=pltpu.CompilerParams(vmem_limit_bytes=24 << 20),
        name="combine",
    )(adjoint, from_estimate, received.reshape(depth * width, row_count)).reshape(
        planes, width, row_count
    )


def halo(estimate, span):
    ring = lax.axis_size("gz")
    width = estimate.shape[1]
    lefts, rights = [], []
    hop, missing = 1, span
    while missing > 0:
        take = min(missing, width)
        forth = [(s, (s + hop) % ring) for s in range(ring)]
        back = [(s, (s - hop) % ring) for s in range(ring)]
        lefts.insert(0, lax.ppermute(estimate[:, width - take :], "gz", forth))
        rights.append(lax.ppermute(estimate[:, :take], "gz", back))
        missing -= take
        hop += 1
    return lefts + [estimate] + rights


def axial_matrices(axial_otf, order):
    planes = order.shape[0]
    wrapped = np.arange(planes)[:, None] * np.arange(planes)[None, :] % planes
    angle = wrapped * (2.0 * math.pi / planes)
    cosine = np.cos(angle).astype(np.float32)
    sine = np.sin(angle).astype(np.float32)
    wrapped = order[:, None] * np.arange(planes, dtype=np.int32)[None, :] % planes
    angle = wrapped.astype(jnp.float32) * (2.0 * math.pi / planes)
    real = axial_otf[:, 0, :, None]
    imag = axial_otf[:, 1, :, None]
    inner = jnp.concatenate(
        [real * cosine + imag * sine, real * sine - imag * cosine], axis=1
    )
    both = jnp.concatenate([jnp.cos(angle), jnp.sin(angle)], axis=1) * (1.0 / planes)
    return jnp.einsum(
        "zk,mkw->mzw", both, inner, precision=lax.Precision.HIGHEST,
        preferred_element_type=jnp.float32,
    )


def by_permutes(ring):
    return ring <= 16 and ring & (ring - 1) == 0 and ring > 4


def exchange(sums):
    ring = lax.axis_size("gz")
    if len(sums) == 1:
        return lax.all_to_all(sums[0], "gz", 0, 0, tiled=True)
    chip = lax.axis_index("gz") // 2
    mine, other = sums
    other = lax.ppermute(other, "gz", [(s, s ^ 1) for s in range(ring)])
    both = jnp.stack([mine, other], axis=1)
    parts = []
    for bit in range(ring // 2):
        part = lax.dynamic_index_in_dim(both, chip ^ bit, 0, keepdims=False)
        if bit:
            part = lax.ppermute(part, "gz", [(s, s ^ (2 * bit)) for s in range(ring)])
        parts.append(part)
    return jnp.concatenate(parts, axis=0)


def shards(estimate, frames, phase_index, axial_otf, row_blur, column_taps):
    planes, width, row_count = estimate.shape
    ring = lax.axis_size("gz")
    orients = frames.shape[0]
    bands = row_blur.shape[0]
    span = column_taps.shape[1] - 1
    table = jnp.asarray(pattern_table(orients, width * ring, row_count, PAD))
    cores = 2 if by_permutes(ring) else 1
    sums = data_sums(frames, phase_index, row_blur, column_taps, table, ring, cores)
    estimate, *sums = lax.optimization_barrier((estimate, *sums))
    pieces = halo(estimate, span)
    received = exchange(sums)
    order = jnp.arange(planes, dtype=jnp.int32)
    if by_permutes(ring):
        order = order ^ lax.axis_index("gz")
    forward = axial_matrices(axial_otf, order)
    squared = jnp.einsum("mzw,mzv->mwv", forward, forward, precision=lax.Precision.HIGHEST)
    extended = jnp.concatenate(pieces, axis=1)
    axial = exact_dot(squared.reshape(bands * planes, planes), extended.reshape(planes, -1))
    axial = axial.reshape(bands, planes, width + 2 * span, row_count)
    axial = axial.transpose(0, 2, 1, 3)
    from_estimate = estimate_part(axial, table, row_blur, column_taps)
    return combine(forward, from_estimate, received)


def solution(mesh):
    placed = (P(None, "gz", "groups"), P(None, None, "gz", None, "groups"), P(), P(), P(), P())
    return jax.shard_map(
        shards, mesh=mesh, in_specs=placed, out_specs=P(None, "gz", "groups"), check_vma=False
    )
```

```python
import math

import jax
import jax.numpy as jnp
import numpy as np
from jax import lax
from jax.experimental import pallas as pl
from jax.experimental.pallas import tpu as pltpu
from jax.sharding import PartitionSpec as P


pattern_period = 3.7
orient_base = 0.3
data_scale = 1.0 / 1024.0
PAD = 8


def exact_dot(left_side, right_side):
    return jnp.dot(
        left_side, right_side, preferred_element_type=jnp.float32, precision=lax.Precision.HIGHEST
    )


def split(values):
    high = values.astype(jnp.bfloat16)
    low = (values - high.astype(jnp.float32)).astype(jnp.bfloat16)
    return high, low


def wide(values):
    high, low = split(values)
    return jnp.concatenate([high, low], axis=1)


def weights(matrix):
    row = wide(matrix)
    return jnp.concatenate([row, row], axis=0)


def narrow(product):
    half = product.shape[1] // 2
    return product[:, :half] + product[:, half:]


def wide_dot(left_side, right_side):
    return jnp.dot(left_side, right_side, preferred_element_type=jnp.float32)


def pattern_table(orients, loop_width, row_count, pad):
    columns = np.arange(-pad, loop_width + pad) % loop_width
    rows = np.arange(row_count)
    images = []
    for orient in range(orients):
        direction = orient_base + 2.0 * math.pi * orient / 3.0
        phase = (
            columns.astype(np.float32)[:, None] * np.float32(math.cos(direction))
            + rows.astype(np.float32)[None, :] * np.float32(math.sin(direction))
        ) * np.float32(2.0 * math.pi / pattern_period)
        images += [np.cos(phase.astype(np.float64)), np.sin(phase.astype(np.float64))]
    return np.stack(images).astype(np.float32)


def harmonic_of(cos_one, sin_one, harmonic):
    if harmonic == 1:
        return cos_one, sin_one
    return cos_one * cos_one - sin_one * sin_one, 2.0 * (sin_one * cos_one)


def blurred(mixed, image, taps, begin, step):
    reach = (len(taps) - 1) // 2
    acc = None
    for offset in range(-reach, reach + 1):
        term = taps[offset + reach] * mixed[image, pl.ds(begin + PAD - offset, step), :]
        acc = term if acc is None else acc + term
    return acc


def band_rows(mixed, images, taps, table, weight, band, begin, step):
    at = pl.ds(begin + (table.shape[1] - mixed.shape[1]) // 2 + PAD, step)
    parts = [wide(blurred(mixed, image, cut, begin, step)) for image, cut in zip(images, taps)]
    product = narrow(wide_dot(jnp.concatenate(parts, axis=0), weight))
    acc = None
    for orient in range(len(images) // 2):
        cos_pattern, sin_pattern = harmonic_of(
            table[2 * orient, at, :], table[2 * orient + 1, at, :], band
        )
        even = product[2 * orient * step : (2 * orient + 1) * step]
        odd = product[(2 * orient + 1) * step : (2 * orient + 2) * step]
        term = cos_pattern * even - sin_pattern * odd
        acc = term if acc is None else acc + term
    return acc


def put(out, index, band, values):
    width = out.shape[3]
    cores = out.shape[1]
    shares = values.shape[0] // width
    for share in range(shares):
        rows = values[share * width : (share + 1) * width]
        out[index * (shares // cores) + share // cores, share % cores, band] = rows


def scaled_taps(taps_ref, band, scale):
    return [taps_ref[band, at] * scale for at in range(taps_ref.shape[1])]


def data_kernel(
    phase_hbm, taps_hbm, frames_hbm, blur_hbm, table_hbm, *refs,
):
    targets, scratch = refs[:-12], refs[-12:]
    raw, summed, mixed, weight, table, blur_rows, out, phase_ref, taps_ref = scratch[:9]
    frame_sems, side_sems, out_sems = scratch[9:]

    orients, phases = raw.shape[0], raw.shape[1]
    loop_width = raw.shape[2]
    bands = out.shape[2]
    core = lax.axis_index("gz") % 2
    phase_copy = pltpu.make_async_copy(phase_hbm, phase_ref, side_sems.at[0])
    phase_copy.start()
    copies = []
    for orient in range(orients):
        row = []
        for index in range(phases):
            copy = pltpu.make_async_copy(
                frames_hbm.at[orient, index, 0],
                raw.at[orient, index],
                frame_sems.at[orient, index],
            )
            copy.start()
            row.append(copy)
        copies.append(row)
    taps_copy = pltpu.make_async_copy(taps_hbm, taps_ref, side_sems.at[1])
    taps_copy.start()
    blur_copy = pltpu.make_async_copy(blur_hbm, blur_rows, side_sems.at[2])
    blur_copy.start()
    table_copy = pltpu.make_async_copy(table_hbm, table, side_sems.at[3])
    table_copy.start()
    step = loop_width // 2
    reach = (taps_ref.shape[1] - 1) // 2
    total = 4 * orients
    count = orients * phases
    first_sine, second_sine = math.sin(2 * math.pi / 5), math.sin(4 * math.pi / 5)
    ratio = second_sine / first_sine
    phase_copy.wait()
    for orient in range(orients):
        holder = []
        for step_index in range(phases):
            at_step = 0
            for index in range(1, phases):
                at_step = jnp.where(phase_ref[orient, index] == step_index, index, at_step)
            holder.append(at_step)
        for copy in copies[orient]:
            copy.wait()

        def mix(index, carry):
            rows = pl.ds(pl.multiple_of(index * step, step), step)
            at = pl.ds(pl.multiple_of(index * step + PAD, 8), step)
            f0, f1, f2, f3, f4 = [raw[orient, k, rows, :] for k in holder]
            near, far, near_odd, far_odd = f1 + f4, f2 + f3, f1 - f4, f2 - f3
            both = near + far
            even = (4 * f0 - both).astype(jnp.float32)
            swing = (near - far).astype(jnp.float32) * math.sqrt(5.0)
            near_odd = near_odd.astype(jnp.float32)
            far_odd = far_odd.astype(jnp.float32)
            mixed[2 * orient, at, :] = even + swing
            mixed[2 * orient + 1, at, :] = near_odd + ratio * far_odd
            mixed[2 * (orients + orient), at, :] = even - swing
            mixed[2 * (orients + orient) + 1, at, :] = ratio * near_odd - far_odd
            plain = f0 + both
            if orient:
                plain = plain + summed[rows, :]
            if orient < orients - 1:
                summed[rows, :] = plain
            else:
                mixed[total, at, :] = plain.astype(jnp.float32) * data_scale - 2.0 * count
            return carry

        lax.fori_loop(0, loop_width // step, mix, 0)
    for image in range(total + 1):
        mixed[image, PAD - reach : PAD, :] = mixed[
            image, loop_width + PAD - reach : loop_width + PAD, :
        ]
        mixed[image, loop_width + PAD : loop_width + PAD + reach, :] = mixed[
            image, PAD : PAD + reach, :
        ]
    taps_copy.wait()
    blur_copy.wait()
    for band in range(bands):
        weight[band] = weights(blur_rows[band])
    even_scale, odd_scale = data_scale / (4.0 * count), data_scale * first_sine / count
    taps = [scaled_taps(taps_ref, 0, 1.0 / count)]
    for band in range(1, bands):
        taps.append(
            [scaled_taps(taps_ref, band, even_scale), scaled_taps(taps_ref, band, odd_scale)]
            * orients
        )

    def plain_out(index, carry):
        begin = pl.multiple_of(index * step, step)
        rows = blurred(mixed, total, taps[0], begin, step)
        put(out, index, 0, narrow(wide_dot(wide(rows), weight[0])))
        return carry

    lax.fori_loop(0, loop_width // step, plain_out, 0)
    out_copies = []

    def ship(band):
        for at, target in enumerate(targets):
            half = (core + at) % 2 if len(targets) > 1 else 0
            copy = pltpu.make_async_copy(
                out.at[:, half, band], target.at[:, band], out_sems.at[at, band]
            )
            copy.start()
            out_copies.append(copy)

    ship(0)
    table_copy.wait()
    for band in range(1, bands):
        images = list(range(2 * orients * (band - 1), 2 * orients * band))

        def band_out(index, carry):
            begin = pl.multiple_of(index * step, step)
            put(
                out,
                index,
                band,
                band_rows(mixed, images, taps[band], table, weight[band], band, begin, step),
            )
            return carry

        lax.fori_loop(0, loop_width // step, band_out, 0)
        ship(band)
    for copy in out_copies:
        copy.wait()


def data_sums(frames, phase_index, row_blur, column_taps, table, chunks, cores):
    orients, phases, _, loop_width, row_count = frames.shape
    bands = row_blur.shape[0]
    width = loop_width // chunks
    anywhere = pl.BlockSpec(memory_space=pltpu.HBM)
    return pl.pallas_call(
        data_kernel,
        out_shape=[
            jax.ShapeDtypeStruct((chunks // cores, bands, width, row_count), jnp.float32)
        ]
        * cores,
        in_specs=[anywhere] * 5,
        out_specs=[anywhere] * cores,
        scratch_shapes=[
            pltpu.VMEM((orients, phases, loop_width, row_count), jnp.int32),
            pltpu.VMEM((loop_width, row_count), jnp.int32),
            pltpu.VMEM((4 * orients + 1, loop_width + 2 * PAD, row_count), jnp.float32),
            pltpu.VMEM((bands, 2 * row_count, 2 * row_count), jnp.bfloat16),
            pltpu.VMEM(table.shape, jnp.float32),
            pltpu.VMEM(row_blur.shape, jnp.float32),
            pltpu.VMEM((chunks // cores, cores, bands, width, row_count), jnp.float32),
            pltpu.SMEM(phase_index.shape, jnp.int32),
            pltpu.SMEM(column_taps.shape, jnp.float32),
            pltpu.SemaphoreType.DMA((orients, phases)),
            pltpu.SemaphoreType.DMA((4,)),
            pltpu.SemaphoreType.DMA((cores, bands)),
        ],
        cost_estimate=pl.CostEstimate(
            flops=13 * loop_width * 2 * 256 * 256, bytes_accessed=frames.size * 4, transcendentals=0
        ),
        compiler_params=pltpu.CompilerParams(vmem_limit_bytes=63 << 20),
        name="data_sums",
    )(phase_index, column_taps, frames, row_blur, table)


def estimate_kernel(taps_ref, axial_ref, table_hbm, blur_ref, out_ref, table_ref, sem):
    width = out_ref.shape[0]
    source = table_hbm
    if table_hbm.shape != table_ref.shape:
        begin = pl.multiple_of(lax.axis_index("gz") * width, 8)
        source = table_hbm.at[:, pl.ds(begin, table_ref.shape[1]), :]
    table_copy = pltpu.make_async_copy(source, table_ref, sem)
    table_copy.start()
    bands, _, planes, _ = axial_ref.shape
    orients = table_ref.shape[0] // 2
    reach = (taps_ref.shape[1] - 1) // 2
    span = 2 * reach
    step = max(d for d in range(1, 23) if out_ref.shape[0] % d == 0 and (d == 1 or d * planes <= 352))

    def lags_of(band, scale):
        return [
            scale
            * sum(
                taps_ref[band, d] * taps_ref[band, d + shift]
                for d in range(0, 2 * reach + 1 - shift)
            )
            for shift in range(span + 1)
        ]

    def filtered(columns, lags):
        rows = []
        for i in range(step):
            acc = lags[0] * columns[i + span]
            for shift in range(1, span + 1):
                acc = acc + lags[shift] * (columns[i + span - shift] + columns[i + span + shift])
            rows.append(wide(acc))
        return rows

    def weight_of(band):
        matrix = blur_ref[band]
        return weights(
            lax.dot_general(
                matrix,
                matrix,
                (((0,), (0,)), ((), ())),
                preferred_element_type=jnp.float32,
                precision=lax.Precision.HIGHEST,
            )
        )

    weight = [weight_of(band) for band in range(bands)]
    shift = PAD - span
    table_copy.wait()
    lags = [lags_of(0, 1.0)] + [lags_of(band, 0.5 / orients) for band in range(1, bands)]

    def chunk(index, carry):
        begin = index * step
        rows = filtered([axial_ref[0, begin + i] for i in range(step + 2 * span)], lags[0])
        product = narrow(wide_dot(jnp.concatenate(rows, axis=0), weight[0]))
        acc = [product[i * planes : (i + 1) * planes] for i in range(step)]
        for band in range(1, bands):
            rows = []
            patterns = []
            for orient in range(orients):
                pairs = [
                    harmonic_of(
                        table_ref[2 * orient, pl.ds(begin + i + shift, 1), :],
                        table_ref[2 * orient + 1, pl.ds(begin + i + shift, 1), :],
                        band,
                    )
                    for i in range(step + 2 * span)
                ]
                for part in range(2):
                    columns = [
                        pairs[i][part] * axial_ref[band, begin + i]
                        for i in range(step + 2 * span)
                    ]
                    rows += filtered(columns, lags[band])
                    patterns.append([pairs[i + span][part] for i in range(step)])
            product = narrow(wide_dot(jnp.concatenate(rows, axis=0), weight[band]))
            for which, pattern in enumerate(patterns):
                for i in range(step):
                    at = (which * step + i) * planes
                    acc[i] = acc[i] + pattern[i] * product[at : at + planes]
        for i in range(step):
            out_ref[begin + i] = acc[i]
        return carry

    lax.fori_loop(0, out_ref.shape[0] // step, chunk, 0)


def estimate_part(axial, table, row_blur, column_taps):
    _, extended, planes, row_count = axial.shape
    width = extended - 2 * (column_taps.shape[1] - 1)
    near = (table.shape[0], width + 2 * PAD, row_count)
    if width % 8:
        table = lax.dynamic_slice_in_dim(table, lax.axis_index("gz") * width, near[1], axis=1)
    smem = pl.BlockSpec(memory_space=pltpu.SMEM)
    vmem = pl.BlockSpec(memory_space=pltpu.VMEM)
    anywhere = pl.BlockSpec(memory_space=pltpu.HBM)
    rows = table.shape[0] * width * planes
    return pl.pallas_call(
        estimate_kernel,
        out_shape=jax.ShapeDtypeStruct((width, planes, row_count), jnp.float32),
        in_specs=[smem, vmem, anywhere, vmem],
        out_specs=vmem,
        scratch_shapes=[pltpu.VMEM(near, jnp.float32), pltpu.SemaphoreType.DMA],
        cost_estimate=pl.CostEstimate(
            flops=40 * rows * 2 * 256 * 256, bytes_accessed=axial.size * 4, transcendentals=0
        ),
        compiler_params=pltpu.CompilerParams(vmem_limit_bytes=40 << 20),
        name="estimate_part",
    )(column_taps, axial, table, row_blur)


def combine_kernel(adjoint_ref, estimate_ref, received_ref, out_ref):
    width, planes, row_count = estimate_ref.shape
    depth = adjoint_ref.shape[1]
    high, low = split(adjoint_ref[...])
    left_side = jnp.concatenate([high, high, low], axis=1)
    for index in range(0, width, 2):
        columns = [received_ref[pl.ds(index + i, depth, stride=width), :] for i in range(2)]
        high, low = split(jnp.concatenate(columns, axis=1))
        right_side = jnp.concatenate([high, low, high], axis=0)
        product = wide_dot(left_side, right_side)
        for i in range(2):
            out_ref[pl.ds(index + i, planes, stride=width), :] = (
                estimate_ref[index + i] + product[:, i * row_count : (i + 1) * row_count]
            )


def combine(forward, from_estimate, received):
    width, planes, row_count = from_estimate.shape
    depth = forward.shape[0] * planes
    adjoint = forward.transpose(2, 1, 0).reshape(planes, depth)
    vmem = pl.BlockSpec(memory_space=pltpu.VMEM)
    return pl.pallas_call(
        combine_kernel,
        out_shape=jax.ShapeDtypeStruct((planes * width, row_count), jnp.float32),
        in_specs=[vmem] * 3,
        out_specs=vmem,
        cost_estimate=pl.CostEstimate(
            flops=2 * received.size * planes, bytes_accessed=received.size * 4, transcendentals=0
        ),
        compiler_params=pltpu.CompilerParams(vmem_limit_bytes=24 << 20),
        name="combine",
    )(adjoint, from_estimate, received.reshape(depth * width, row_count)).reshape(
        planes, width, row_count
    )


def halo(estimate, span):
    ring = lax.axis_size("gz")
    width = estimate.shape[1]
    lefts, rights = [], []
    hop, missing = 1, span
    while missing > 0:
        take = min(missing, width)
        forth = [(s, (s + hop) % ring) for s in range(ring)]
        back = [(s, (s - hop) % ring) for s in range(ring)]
        lefts.insert(0, lax.ppermute(estimate[:, width - take :], "gz", forth))
        rights.append(lax.ppermute(estimate[:, :take], "gz", back))
        missing -= take
        hop += 1
    return lefts + [estimate] + rights


def axial_matrices(axial_otf, order):
    planes = order.shape[0]
    wrapped = np.arange(planes)[:, None] * np.arange(planes)[None, :] % planes
    angle = wrapped * (2.0 * math.pi / planes)
    cosine = np.cos(angle).astype(np.float32)
    sine = np.sin(angle).astype(np.float32)
    wrapped = order[:, None] * np.arange(planes, dtype=np.int32)[None, :] % planes
    angle = wrapped.astype(jnp.float32) * (2.0 * math.pi / planes)
    real = axial_otf[:, 0, :, None]
    imag = axial_otf[:, 1, :, None]
    inner = jnp.concatenate(
        [real * cosine + imag * sine, real * sine - imag * cosine], axis=1
    )
    both = jnp.concatenate([jnp.cos(angle), jnp.sin(angle)], axis=1) * (1.0 / planes)
    return jnp.einsum(
        "zk,mkw->mzw", both, inner, precision=lax.Precision.HIGHEST,
        preferred_element_type=jnp.float32,
    )


def by_permutes(ring):
    return ring <= 16 and ring & (ring - 1) == 0 and ring > 4


def exchange(sums):
    ring = lax.axis_size("gz")
    if len(sums) == 1:
        return lax.all_to_all(-sums[0], "gz", 0, 0, tiled=True)
    chip = lax.axis_index("gz") // 2
    mine, other = sums
    other = lax.ppermute(other, "gz", [(s, s ^ 1) for s in range(ring)])
    mine = lax.optimization_barrier(-mine)
    both = jnp.stack([mine, -other], axis=1)
    parts = []
    for bit in range(ring // 2):
        part = lax.dynamic_index_in_dim(both, chip ^ bit, 0, keepdims=False)
        if bit:
            part = lax.ppermute(part, "gz", [(s, s ^ (2 * bit)) for s in range(ring)])
        parts.append(part)
    return jnp.concatenate(parts, axis=0)


def shards(estimate, frames, phase_index, axial_otf, row_blur, column_taps):
    planes, width, row_count = estimate.shape
    ring = lax.axis_size("gz")
    orients = frames.shape[0]
    bands = row_blur.shape[0]
    span = column_taps.shape[1] - 1
    table = jnp.asarray(pattern_table(orients, width * ring, row_count, PAD))
    cores = 2 if by_permutes(ring) else 1
    sums = data_sums(frames, phase_index, row_blur, column_taps, table, ring, cores)
    estimate, *sums = lax.optimization_barrier((estimate, *sums))
    pieces = halo(estimate, span)
    received = exchange(sums)
    order = jnp.arange(planes, dtype=jnp.int32)
    if by_permutes(ring):
        order = order ^ lax.axis_index("gz")
    forward = axial_matrices(axial_otf, order)
    squared = jnp.einsum("mzw,mzv->mwv", forward, forward, precision=lax.Precision.HIGHEST)
    extended = jnp.concatenate(pieces, axis=1)
    axial = exact_dot(squared.reshape(bands * planes, planes), extended.reshape(planes, -1))
    axial = axial.reshape(bands, planes, width + 2 * span, row_count)
    axial = axial.transpose(0, 2, 1, 3)
    from_estimate = estimate_part(axial, table, row_blur, column_taps)
    return combine(forward, from_estimate, received)


def solution(mesh):
    placed = (P(None, "gz", "groups"), P(None, None, "gz", None, "groups"), P(), P(), P(), P())
    return jax.shard_map(
        shards, mesh=mesh, in_specs=placed, out_specs=P(None, "gz", "groups"), check_vma=False
    )
```

```python
import math

import jax
import jax.numpy as jnp
import numpy as np
from jax import lax
from jax.experimental import pallas as pl
from jax.experimental.pallas import tpu as pltpu
from jax.sharding import PartitionSpec as P


pattern_period = 3.7
orient_base = 0.3
data_scale = 1.0 / 1024.0
PAD = 8


def exact_dot(left_side, right_side):
    return jnp.dot(
        left_side, right_side, preferred_element_type=jnp.float32, precision=lax.Precision.HIGHEST
    )


def split(values):
    high = values.astype(jnp.bfloat16)
    low = (values - high.astype(jnp.float32)).astype(jnp.bfloat16)
    return high, low


def wide(values):
    high, low = split(values)
    return jnp.concatenate([high, low], axis=1)


def weights(matrix):
    row = wide(matrix)
    return jnp.concatenate([row, row], axis=0)


def narrow(product):
    half = product.shape[1] // 2
    return product[:, :half] + product[:, half:]


def wide_dot(left_side, right_side):
    return jnp.dot(left_side, right_side, preferred_element_type=jnp.float32)


def pattern_table(orients, loop_width, row_count, pad):
    columns = np.arange(-pad, loop_width + pad) % loop_width
    rows = np.arange(row_count)
    images = []
    for orient in range(orients):
        direction = orient_base + 2.0 * math.pi * orient / 3.0
        phase = (
            columns.astype(np.float32)[:, None] * np.float32(math.cos(direction))
            + rows.astype(np.float32)[None, :] * np.float32(math.sin(direction))
        ) * np.float32(2.0 * math.pi / pattern_period)
        images += [np.cos(phase.astype(np.float64)), np.sin(phase.astype(np.float64))]
    return np.stack(images).astype(np.float32)


def harmonic_of(cos_one, sin_one, harmonic):
    if harmonic == 1:
        return cos_one, sin_one
    return cos_one * cos_one - sin_one * sin_one, 2.0 * (sin_one * cos_one)


def blurred(mixed, image, taps, begin, step):
    reach = (len(taps) - 1) // 2
    acc = None
    for offset in range(-reach, reach + 1):
        term = taps[offset + reach] * mixed[image, pl.ds(begin + PAD - offset, step), :]
        acc = term if acc is None else acc + term
    return acc


def band_rows(mixed, images, taps, patterns, weight, band, begin, step):
    parts = [wide(blurred(mixed, image, cut, begin, step)) for image, cut in zip(images, taps)]
    product = narrow(wide_dot(jnp.concatenate(parts, axis=0), weight))
    cos_pattern, sin_pattern = harmonic_of(*patterns, band)
    return cos_pattern * product[:step] - sin_pattern * product[step:]


def put(out, index, band, values, add):
    width = out.shape[3]
    cores = out.shape[1]
    shares = values.shape[0] // width
    for share in range(shares):
        rows = values[share * width : (share + 1) * width]
        at = index * (shares // cores) + share // cores, share % cores, band
        out[at] = out[at] + rows if add else rows


def scaled_taps(taps_ref, band, scale):
    return [taps_ref[band, at] * scale for at in range(taps_ref.shape[1])]


def data_kernel(
    phase_hbm, taps_hbm, frames_hbm, blur_hbm, table_hbm, *refs,
):
    targets, scratch = refs[:-12], refs[-12:]
    raw, summed, mixed, weight, table, blur_rows, out, phase_ref, taps_ref = scratch[:9]
    frame_sems, side_sems, out_sems = scratch[9:]

    orients, phases = raw.shape[0], raw.shape[1]
    loop_width = raw.shape[2]
    bands, width = out.shape[2], out.shape[3]
    core = lax.axis_index("gz") % 2
    phase_copy = pltpu.make_async_copy(phase_hbm, phase_ref, side_sems.at[0])
    phase_copy.start()
    taps_copy = pltpu.make_async_copy(taps_hbm, taps_ref, side_sems.at[1])
    taps_copy.start()
    copies = []
    table_copies = []
    for orient in range(orients):
        row = []
        for index in range(phases):
            copy = pltpu.make_async_copy(
                frames_hbm.at[orient, index, 0],
                raw.at[orient, index],
                frame_sems.at[orient, index],
            )
            copy.start()
            row.append(copy)
        copies.append(row)
        if not orient:
            blur_copy = pltpu.make_async_copy(blur_hbm, blur_rows, side_sems.at[2])
            blur_copy.start()
        pair = pl.ds(2 * orient, 2)
        copy = pltpu.make_async_copy(table_hbm.at[pair], table.at[pair], side_sems.at[3 + orient])
        copy.start()
        table_copies.append(copy)
    step = loop_width // 2
    reach = (taps_ref.shape[1] - 1) // 2
    total = 4 * orients
    count = orients * phases
    first_sine, second_sine = math.sin(2 * math.pi / 5), math.sin(4 * math.pi / 5)
    ratio = second_sine / first_sine
    step_chips = step // width // out.shape[1]

    def half_of(at):
        return (core + at) % 2 if len(targets) > 1 else 0

    def ship(index, band):
        chips = pl.ds(index * step_chips, step_chips)
        for at, target in enumerate(targets):
            pltpu.make_async_copy(
                out.at[chips, half_of(at), band], target.at[chips, band], out_sems.at[at, band]
            ).start()

    phase_copy.wait()
    for orient in range(orients):
        holder = []
        for step_index in range(phases):
            at_step = 0
            for index in range(1, phases):
                at_step = jnp.where(phase_ref[orient, index] == step_index, index, at_step)
            holder.append(at_step)
        for copy in copies[orient]:
            copy.wait()

        def mix(index, carry):
            rows = pl.ds(pl.multiple_of(index * step, step), step)
            at = pl.ds(pl.multiple_of(index * step + PAD, 8), step)
            f0, f1, f2, f3, f4 = [raw[orient, k, rows, :] for k in holder]
            near, far, near_odd, far_odd = f1 + f4, f2 + f3, f1 - f4, f2 - f3
            both = near + far
            even = (4 * f0 - both).astype(jnp.float32)
            swing = (near - far).astype(jnp.float32) * math.sqrt(5.0)
            near_odd = near_odd.astype(jnp.float32)
            far_odd = far_odd.astype(jnp.float32)
            mixed[2 * orient, at, :] = even + swing
            mixed[2 * orient + 1, at, :] = near_odd + ratio * far_odd
            mixed[2 * (orients + orient), at, :] = even - swing
            mixed[2 * (orients + orient) + 1, at, :] = ratio * near_odd - far_odd
            plain = f0 + both
            if orient:
                plain = plain + summed[rows, :]
            if orient < orients - 1:
                summed[rows, :] = plain
            else:
                mixed[total, at, :] = plain.astype(jnp.float32) * data_scale - 2.0 * count
            return carry

        lax.fori_loop(0, loop_width // step, mix, 0)
        ring_images = [2 * orient, 2 * orient + 1]
        ring_images += [2 * orients + image for image in ring_images]
        if orient == orients - 1:
            ring_images.append(total)
        for image in ring_images:
            mixed[image, PAD - reach : PAD, :] = mixed[
                image, loop_width + PAD - reach : loop_width + PAD, :
            ]
            mixed[image, loop_width + PAD : loop_width + PAD + reach, :] = mixed[
                image, PAD : PAD + reach, :
            ]
        if not orient:
            taps_copy.wait()
            blur_copy.wait()
            for band in range(bands):
                weight[band] = weights(blur_rows[band])
            plain_taps = scaled_taps(taps_ref, 0, 1.0 / count)
            even_scale = data_scale / (4.0 * count)
            odd_scale = data_scale * first_sine / count
        if orient == orients - 1:

            def plain_out(index, carry):
                begin = pl.multiple_of(index * step, step)
                rows = blurred(mixed, total, plain_taps, begin, step)
                put(out, index, 0, narrow(wide_dot(wide(rows), weight[0])), False)
                ship(index, 0)
                return carry

            lax.fori_loop(0, loop_width // step, plain_out, 0)
        table_copies[orient].wait()
        taps = [
            [scaled_taps(taps_ref, band, even_scale), scaled_taps(taps_ref, band, odd_scale)]
            for band in range(1, bands)
        ]

        def band_out(index, carry):
            begin = pl.multiple_of(index * step, step)
            at = pl.ds(begin + (table.shape[1] - loop_width) // 2, step)
            patterns = table[2 * orient, at, :], table[2 * orient + 1, at, :]
            for band in range(1, bands):
                base = 2 * (orients * (band - 1) + orient)
                images = base, base + 1
                rows = band_rows(
                    mixed, images, taps[band - 1], patterns, weight[band], band, begin, step
                )
                put(out, index, band, rows, orient > 0)
                if orient == orients - 1:
                    ship(index, band)
            return carry

        lax.fori_loop(0, loop_width // step, band_out, 0)
    for band in range(bands):
        for at, target in enumerate(targets):
            half = half_of(at)
            pltpu.make_async_copy(
                out.at[:, half, band], target.at[:, band], out_sems.at[at, band]
            ).wait()


def data_sums(frames, phase_index, row_blur, column_taps, table, chunks, cores):
    orients, phases, _, loop_width, row_count = frames.shape
    bands = row_blur.shape[0]
    width = loop_width // chunks
    anywhere = pl.BlockSpec(memory_space=pltpu.HBM)
    return pl.pallas_call(
        data_kernel,
        out_shape=[
            jax.ShapeDtypeStruct((chunks // cores, bands, width, row_count), jnp.float32)
        ]
        * cores,
        in_specs=[anywhere] * 5,
        out_specs=[anywhere] * cores,
        scratch_shapes=[
            pltpu.VMEM((orients, phases, loop_width, row_count), jnp.int32),
            pltpu.VMEM((loop_width, row_count), jnp.int32),
            pltpu.VMEM((4 * orients + 1, loop_width + 2 * PAD, row_count), jnp.float32),
            pltpu.VMEM((bands, 2 * row_count, 2 * row_count), jnp.bfloat16),
            pltpu.VMEM(table.shape, jnp.float32),
            pltpu.VMEM(row_blur.shape, jnp.float32),
            pltpu.VMEM((chunks // cores, cores, bands, width, row_count), jnp.float32),
            pltpu.SMEM(phase_index.shape, jnp.int32),
            pltpu.SMEM(column_taps.shape, jnp.float32),
            pltpu.SemaphoreType.DMA((orients, phases)),
            pltpu.SemaphoreType.DMA((3 + orients,)),
            pltpu.SemaphoreType.DMA((cores, bands)),
        ],
        cost_estimate=pl.CostEstimate(
            flops=13 * loop_width * 2 * 256 * 256, bytes_accessed=frames.size * 4, transcendentals=0
        ),
        compiler_params=pltpu.CompilerParams(vmem_limit_bytes=63 << 20),
        name="data_sums",
    )(phase_index, column_taps, frames, row_blur, table)


def estimate_kernel(taps_ref, axial_ref, table_hbm, blur_ref, out_ref, table_ref, sem):
    width = out_ref.shape[0]
    source = table_hbm
    if table_hbm.shape != table_ref.shape:
        begin = pl.multiple_of(lax.axis_index("gz") * width, 8)
        source = table_hbm.at[:, pl.ds(begin, table_ref.shape[1]), :]
    table_copy = pltpu.make_async_copy(source, table_ref, sem)
    table_copy.start()
    bands, _, planes, _ = axial_ref.shape
    orients = table_ref.shape[0] // 2
    reach = (taps_ref.shape[1] - 1) // 2
    span = 2 * reach
    step = max(d for d in range(1, 23) if out_ref.shape[0] % d == 0 and (d == 1 or d * planes <= 352))

    def lags_of(band, scale):
        return [
            scale
            * sum(
                taps_ref[band, d] * taps_ref[band, d + shift]
                for d in range(0, 2 * reach + 1 - shift)
            )
            for shift in range(span + 1)
        ]

    def filtered(columns, lags):
        rows = []
        for i in range(step):
            acc = lags[0] * columns[i + span]
            for shift in range(1, span + 1):
                acc = acc + lags[shift] * (columns[i + span - shift] + columns[i + span + shift])
            rows.append(wide(acc))
        return rows

    def weight_of(band):
        matrix = blur_ref[band]
        return weights(
            lax.dot_general(
                matrix,
                matrix,
                (((0,), (0,)), ((), ())),
                preferred_element_type=jnp.float32,
                precision=lax.Precision.HIGHEST,
            )
        )

    weight = [weight_of(band) for band in range(bands)]
    shift = PAD - span
    table_copy.wait()
    lags = [lags_of(0, 1.0)] + [lags_of(band, 0.5 / orients) for band in range(1, bands)]

    def chunk(index, carry):
        begin = index * step
        rows = filtered([axial_ref[0, begin + i] for i in range(step + 2 * span)], lags[0])
        product = narrow(wide_dot(jnp.concatenate(rows, axis=0), weight[0]))
        acc = [product[i * planes : (i + 1) * planes] for i in range(step)]
        for band in range(1, bands):
            rows = []
            patterns = []
            for orient in range(orients):
                pairs = [
                    harmonic_of(
                        table_ref[2 * orient, pl.ds(begin + i + shift, 1), :],
                        table_ref[2 * orient + 1, pl.ds(begin + i + shift, 1), :],
                        band,
                    )
                    for i in range(step + 2 * span)
                ]
                for part in range(2):
                    columns = [
                        pairs[i][part] * axial_ref[band, begin + i]
                        for i in range(step + 2 * span)
                    ]
                    rows += filtered(columns, lags[band])
                    patterns.append([pairs[i + span][part] for i in range(step)])
            product = narrow(wide_dot(jnp.concatenate(rows, axis=0), weight[band]))
            for which, pattern in enumerate(patterns):
                for i in range(step):
                    at = (which * step + i) * planes
                    acc[i] = acc[i] + pattern[i] * product[at : at + planes]
        for i in range(step):
            out_ref[begin + i] = acc[i]
        return carry

    lax.fori_loop(0, out_ref.shape[0] // step, chunk, 0)


def estimate_part(axial, table, row_blur, column_taps):
    _, extended, planes, row_count = axial.shape
    width = extended - 2 * (column_taps.shape[1] - 1)
    near = (table.shape[0], width + 2 * PAD, row_count)
    if width % 8:
        table = lax.dynamic_slice_in_dim(table, lax.axis_index("gz") * width, near[1], axis=1)
    smem = pl.BlockSpec(memory_space=pltpu.SMEM)
    vmem = pl.BlockSpec(memory_space=pltpu.VMEM)
    anywhere = pl.BlockSpec(memory_space=pltpu.HBM)
    rows = table.shape[0] * width * planes
    return pl.pallas_call(
        estimate_kernel,
        out_shape=jax.ShapeDtypeStruct((width, planes, row_count), jnp.float32),
        in_specs=[smem, vmem, anywhere, vmem],
        out_specs=vmem,
        scratch_shapes=[pltpu.VMEM(near, jnp.float32), pltpu.SemaphoreType.DMA],
        cost_estimate=pl.CostEstimate(
            flops=40 * rows * 2 * 256 * 256, bytes_accessed=axial.size * 4, transcendentals=0
        ),
        compiler_params=pltpu.CompilerParams(vmem_limit_bytes=40 << 20),
        name="estimate_part",
    )(column_taps, axial, table, row_blur)


def combine_kernel(adjoint_ref, estimate_ref, received_ref, out_ref):
    width, planes, row_count = estimate_ref.shape
    depth = adjoint_ref.shape[1]
    high, low = split(adjoint_ref[...])
    left_side = jnp.concatenate([high, high, low], axis=1)
    for index in range(0, width, 2):
        columns = [received_ref[pl.ds(index + i, depth, stride=width), :] for i in range(2)]
        high, low = split(jnp.concatenate(columns, axis=1))
        right_side = jnp.concatenate([high, low, high], axis=0)
        product = wide_dot(left_side, right_side)
        for i in range(2):
            out_ref[pl.ds(index + i, planes, stride=width), :] = (
                estimate_ref[index + i] + product[:, i * row_count : (i + 1) * row_count]
            )


def combine(forward, from_estimate, received):
    width, planes, row_count = from_estimate.shape
    depth = forward.shape[0] * planes
    adjoint = forward.transpose(2, 1, 0).reshape(planes, depth)
    vmem = pl.BlockSpec(memory_space=pltpu.VMEM)
    return pl.pallas_call(
        combine_kernel,
        out_shape=jax.ShapeDtypeStruct((planes * width, row_count), jnp.float32),
        in_specs=[vmem] * 3,
        out_specs=vmem,
        cost_estimate=pl.CostEstimate(
            flops=2 * received.size * planes, bytes_accessed=received.size * 4, transcendentals=0
        ),
        compiler_params=pltpu.CompilerParams(vmem_limit_bytes=24 << 20),
        name="combine",
    )(adjoint, from_estimate, received.reshape(depth * width, row_count)).reshape(
        planes, width, row_count
    )


def halo(estimate, span):
    ring = lax.axis_size("gz")
    width = estimate.shape[1]
    lefts, rights = [], []
    hop, missing = 1, span
    while missing > 0:
        take = min(missing, width)
        forth = [(s, (s + hop) % ring) for s in range(ring)]
        back = [(s, (s - hop) % ring) for s in range(ring)]
        lefts.insert(0, lax.ppermute(estimate[:, width - take :], "gz", forth))
        rights.append(lax.ppermute(estimate[:, :take], "gz", back))
        missing -= take
        hop += 1
    return lefts + [estimate] + rights


def axial_matrices(axial_otf, order):
    planes = order.shape[0]
    wrapped = np.arange(planes)[:, None] * np.arange(planes)[None, :] % planes
    angle = wrapped * (2.0 * math.pi / planes)
    cosine = np.cos(angle).astype(np.float32)
    sine = np.sin(angle).astype(np.float32)
    wrapped = order[:, None] * np.arange(planes, dtype=np.int32)[None, :] % planes
    angle = wrapped.astype(jnp.float32) * (2.0 * math.pi / planes)
    real = axial_otf[:, 0, :, None]
    imag = axial_otf[:, 1, :, None]
    inner = jnp.concatenate(
        [real * cosine + imag * sine, real * sine - imag * cosine], axis=1
    )
    both = jnp.concatenate([jnp.cos(angle), jnp.sin(angle)], axis=1) * (1.0 / planes)
    return jnp.einsum(
        "zk,mkw->mzw", both, inner, precision=lax.Precision.HIGHEST,
        preferred_element_type=jnp.float32,
    )


def by_permutes(ring):
    return ring <= 16 and ring & (ring - 1) == 0 and ring > 4


def exchange(sums):
    ring = lax.axis_size("gz")
    if len(sums) == 1:
        return lax.all_to_all(-sums[0], "gz", 0, 0, tiled=True)
    chip = lax.axis_index("gz") // 2
    mine, other = sums
    other = lax.ppermute(other, "gz", [(s, s ^ 1) for s in range(ring)])
    mine = lax.optimization_barrier(-mine)
    both = jnp.stack([mine, -other], axis=1)
    parts = []
    for bit in range(ring // 2):
        part = lax.dynamic_index_in_dim(both, chip ^ bit, 0, keepdims=False)
        if bit:
            part = lax.ppermute(part, "gz", [(s, s ^ (2 * bit)) for s in range(ring)])
        parts.append(part)
    return jnp.concatenate(parts, axis=0)


def shards(estimate, frames, phase_index, axial_otf, row_blur, column_taps):
    planes, width, row_count = estimate.shape
    ring = lax.axis_size("gz")
    orients = frames.shape[0]
    bands = row_blur.shape[0]
    span = column_taps.shape[1] - 1
    table = jnp.asarray(pattern_table(orients, width * ring, row_count, PAD))
    cores = 2 if by_permutes(ring) else 1
    sums = data_sums(frames, phase_index, row_blur, column_taps, table, ring, cores)
    estimate, *sums = lax.optimization_barrier((estimate, *sums))
    pieces = halo(estimate, span)
    received = exchange(sums)
    order = jnp.arange(planes, dtype=jnp.int32)
    if by_permutes(ring):
        order = order ^ lax.axis_index("gz")
    forward = axial_matrices(axial_otf, order)
    squared = jnp.einsum("mzw,mzv->mwv", forward, forward, precision=lax.Precision.HIGHEST)
    extended = jnp.concatenate(pieces, axis=1)
    axial = exact_dot(squared.reshape(bands * planes, planes), extended.reshape(planes, -1))
    axial = axial.reshape(bands, planes, width + 2 * span, row_count)
    axial = axial.transpose(0, 2, 1, 3)
    from_estimate = estimate_part(axial, table, row_blur, column_taps)
    return combine(forward, from_estimate, received)


def solution(mesh):
    placed = (P(None, "gz", "groups"), P(None, None, "gz", None, "groups"), P(), P(), P(), P())
    return jax.shard_map(
        shards, mesh=mesh, in_specs=placed, out_specs=P(None, "gz", "groups"), check_vma=False
    )
```

```python
import math

import jax
import jax.numpy as jnp
import numpy as np
from jax import lax
from jax.experimental import pallas as pl
from jax.experimental.pallas import tpu as pltpu
from jax.sharding import PartitionSpec as P


pattern_period = 3.7
orient_base = 0.3
data_scale = 1.0 / 1024.0
PAD = 8


def exact_dot(left_side, right_side):
    return jnp.dot(
        left_side, right_side, preferred_element_type=jnp.float32, precision=lax.Precision.HIGHEST
    )


def split(values):
    high = values.astype(jnp.bfloat16)
    low = (values - high.astype(jnp.float32)).astype(jnp.bfloat16)
    return high, low


def wide(values):
    high, low = split(values)
    return jnp.concatenate([high, low], axis=1)


def weights(matrix):
    row = wide(matrix)
    return jnp.concatenate([row, row], axis=0)


def narrow(product):
    half = product.shape[1] // 2
    return product[:, :half] + product[:, half:]


def wide_dot(left_side, right_side):
    return jnp.dot(left_side, right_side, preferred_element_type=jnp.float32)


def pattern_table(orients, loop_width, row_count, pad):
    columns = np.arange(-pad, loop_width + pad) % loop_width
    rows = np.arange(row_count)
    images = []
    for orient in range(orients):
        direction = orient_base + 2.0 * math.pi * orient / 3.0
        phase = (
            columns.astype(np.float32)[:, None] * np.float32(math.cos(direction))
            + rows.astype(np.float32)[None, :] * np.float32(math.sin(direction))
        ) * np.float32(2.0 * math.pi / pattern_period)
        images += [np.cos(phase.astype(np.float64)), np.sin(phase.astype(np.float64))]
    return np.stack(images).astype(np.float32)


def harmonic_of(cos_one, sin_one, harmonic):
    if harmonic == 1:
        return cos_one, sin_one
    return cos_one * cos_one - sin_one * sin_one, 2.0 * (sin_one * cos_one)


def blurred(mixed, image, taps, begin, step):
    reach = (len(taps) - 1) // 2
    acc = None
    for offset in range(-reach, reach + 1):
        term = taps[offset + reach] * mixed[image, pl.ds(begin + PAD - offset, step), :]
        acc = term if acc is None else acc + term
    return acc


def band_rows(mixed, images, taps, table, weight, band, begin, step):
    at = pl.ds(begin + (table.shape[1] - mixed.shape[1]) // 2 + PAD, step)
    parts = [wide(blurred(mixed, image, cut, begin, step)) for image, cut in zip(images, taps)]
    product = narrow(wide_dot(jnp.concatenate(parts, axis=0), weight))
    acc = None
    for orient in range(len(images) // 2):
        cos_pattern, sin_pattern = harmonic_of(
            table[2 * orient, at, :], table[2 * orient + 1, at, :], band
        )
        even = product[2 * orient * step : (2 * orient + 1) * step]
        odd = product[(2 * orient + 1) * step : (2 * orient + 2) * step]
        term = cos_pattern * even - sin_pattern * odd
        acc = term if acc is None else acc + term
    return acc


def put(out, index, band, values):
    width = out.shape[3]
    cores = out.shape[1]
    shares = values.shape[0] // width
    for share in range(shares):
        rows = values[share * width : (share + 1) * width]
        out[index * (shares // cores) + share // cores, share % cores, band] = rows


def scaled_taps(taps_ref, band, scale):
    return [taps_ref[band, at] * scale for at in range(taps_ref.shape[1])]


def data_kernel(
    phase_hbm, taps_hbm, frames_hbm, blur_hbm, table_hbm, *refs,
):
    targets, scratch = refs[:-12], refs[-12:]
    raw, summed, mixed, weight, table, blur_rows, out, phase_ref, taps_ref = scratch[:9]
    frame_sems, side_sems, out_sems = scratch[9:]

    orients, phases = raw.shape[0], raw.shape[1]
    loop_width = raw.shape[2]
    bands = out.shape[2]
    core = lax.axis_index("gz") % 2
    phase_copy = pltpu.make_async_copy(phase_hbm, phase_ref, side_sems.at[0])
    phase_copy.start()
    copies = []
    for orient in range(orients):
        row = []
        for index in range(phases):
            copy = pltpu.make_async_copy(
                frames_hbm.at[orient, index, 0],
                raw.at[orient, index],
                frame_sems.at[orient, index],
            )
            copy.start()
            row.append(copy)
        copies.append(row)
    taps_copy = pltpu.make_async_copy(taps_hbm, taps_ref, side_sems.at[1])
    taps_copy.start()
    blur_copy = pltpu.make_async_copy(blur_hbm, blur_rows, side_sems.at[2])
    blur_copy.start()
    table_copy = pltpu.make_async_copy(table_hbm, table, side_sems.at[3])
    table_copy.start()
    step = loop_width
    reach = (taps_ref.shape[1] - 1) // 2
    total = 4 * orients
    count = orients * phases
    first_sine, second_sine = math.sin(2 * math.pi / 5), math.sin(4 * math.pi / 5)
    ratio = second_sine / first_sine
    phase_copy.wait()
    for orient in range(orients):
        holder = []
        for step_index in range(phases):
            at_step = 0
            for index in range(1, phases):
                at_step = jnp.where(phase_ref[orient, index] == step_index, index, at_step)
            holder.append(at_step)
        for copy in copies[orient]:
            copy.wait()

        def mix(index, carry):
            rows = pl.ds(pl.multiple_of(index * step, step), step)
            at = pl.ds(pl.multiple_of(index * step + PAD, 8), step)
            f0, f1, f2, f3, f4 = [raw[orient, k, rows, :] for k in holder]
            near, far, near_odd, far_odd = f1 + f4, f2 + f3, f1 - f4, f2 - f3
            both = near + far
            even = (4 * f0 - both).astype(jnp.float32)
            swing = (near - far).astype(jnp.float32) * math.sqrt(5.0)
            near_odd = near_odd.astype(jnp.float32)
            far_odd = far_odd.astype(jnp.float32)
            mixed[2 * orient, at, :] = even + swing
            mixed[2 * orient + 1, at, :] = near_odd + ratio * far_odd
            mixed[2 * (orients + orient), at, :] = even - swing
            mixed[2 * (orients + orient) + 1, at, :] = ratio * near_odd - far_odd
            plain = f0 + both
            if orient:
                plain = plain + summed[rows, :]
            if orient < orients - 1:
                summed[rows, :] = plain
            else:
                mixed[total, at, :] = plain.astype(jnp.float32) * data_scale - 2.0 * count
            return carry

        lax.fori_loop(0, loop_width // step, mix, 0)
    for image in range(total + 1):
        mixed[image, PAD - reach : PAD, :] = mixed[
            image, loop_width + PAD - reach : loop_width + PAD, :
        ]
        mixed[image, loop_width + PAD : loop_width + PAD + reach, :] = mixed[
            image, PAD : PAD + reach, :
        ]
    taps_copy.wait()
    blur_copy.wait()
    for band in range(bands):
        weight[band] = weights(blur_rows[band])
    even_scale, odd_scale = data_scale / (4.0 * count), data_scale * first_sine / count
    taps = [scaled_taps(taps_ref, 0, 1.0 / count)]
    for band in range(1, bands):
        taps.append(
            [scaled_taps(taps_ref, band, even_scale), scaled_taps(taps_ref, band, odd_scale)]
            * orients
        )

    def plain_out(index, carry):
        begin = pl.multiple_of(index * step, step)
        rows = blurred(mixed, total, taps[0], begin, step)
        put(out, index, 0, narrow(wide_dot(wide(rows), weight[0])))
        return carry

    lax.fori_loop(0, loop_width // step, plain_out, 0)
    out_copies = []

    def ship(band):
        for at, target in enumerate(targets):
            half = (core + at) % 2 if len(targets) > 1 else 0
            copy = pltpu.make_async_copy(
                out.at[:, half, band], target.at[:, band], out_sems.at[at, band]
            )
            copy.start()
            out_copies.append(copy)

    ship(0)
    table_copy.wait()
    for band in range(1, bands):
        images = list(range(2 * orients * (band - 1), 2 * orients * band))

        def band_out(index, carry):
            begin = pl.multiple_of(index * step, step)
            put(
                out,
                index,
                band,
                band_rows(mixed, images, taps[band], table, weight[band], band, begin, step),
            )
            return carry

        lax.fori_loop(0, loop_width // step, band_out, 0)
        ship(band)
    for copy in out_copies:
        copy.wait()


def data_sums(frames, phase_index, row_blur, column_taps, table, chunks, cores):
    orients, phases, _, loop_width, row_count = frames.shape
    bands = row_blur.shape[0]
    width = loop_width // chunks
    anywhere = pl.BlockSpec(memory_space=pltpu.HBM)
    return pl.pallas_call(
        data_kernel,
        out_shape=[
            jax.ShapeDtypeStruct((chunks // cores, bands, width, row_count), jnp.float32)
        ]
        * cores,
        in_specs=[anywhere] * 5,
        out_specs=[anywhere] * cores,
        scratch_shapes=[
            pltpu.VMEM((orients, phases, loop_width, row_count), jnp.int32),
            pltpu.VMEM((loop_width, row_count), jnp.int32),
            pltpu.VMEM((4 * orients + 1, loop_width + 2 * PAD, row_count), jnp.float32),
            pltpu.VMEM((bands, 2 * row_count, 2 * row_count), jnp.bfloat16),
            pltpu.VMEM(table.shape, jnp.float32),
            pltpu.VMEM(row_blur.shape, jnp.float32),
            pltpu.VMEM((chunks // cores, cores, bands, width, row_count), jnp.float32),
            pltpu.SMEM(phase_index.shape, jnp.int32),
            pltpu.SMEM(column_taps.shape, jnp.float32),
            pltpu.SemaphoreType.DMA((orients, phases)),
            pltpu.SemaphoreType.DMA((4,)),
            pltpu.SemaphoreType.DMA((cores, bands)),
        ],
        cost_estimate=pl.CostEstimate(
            flops=13 * loop_width * 2 * 256 * 256, bytes_accessed=frames.size * 4, transcendentals=0
        ),
        compiler_params=pltpu.CompilerParams(vmem_limit_bytes=63 << 20),
        name="data_sums",
    )(phase_index, column_taps, frames, row_blur, table)


def estimate_kernel(taps_ref, axial_ref, table_hbm, blur_ref, out_ref, table_ref, sem):
    width = out_ref.shape[0]
    source = table_hbm
    if table_hbm.shape != table_ref.shape:
        begin = pl.multiple_of(lax.axis_index("gz") * width, 8)
        source = table_hbm.at[:, pl.ds(begin, table_ref.shape[1]), :]
    table_copy = pltpu.make_async_copy(source, table_ref, sem)
    table_copy.start()
    bands, _, planes, _ = axial_ref.shape
    orients = table_ref.shape[0] // 2
    reach = (taps_ref.shape[1] - 1) // 2
    span = 2 * reach
    step = max(d for d in range(1, 23) if out_ref.shape[0] % d == 0 and (d == 1 or d * planes <= 352))

    def lags_of(band, scale):
        return [
            scale
            * sum(
                taps_ref[band, d] * taps_ref[band, d + shift]
                for d in range(0, 2 * reach + 1 - shift)
            )
            for shift in range(span + 1)
        ]

    def filtered(columns, lags):
        rows = []
        for i in range(step):
            acc = lags[0] * columns[i + span]
            for shift in range(1, span + 1):
                acc = acc + lags[shift] * (columns[i + span - shift] + columns[i + span + shift])
            rows.append(wide(acc))
        return rows

    def weight_of(band):
        matrix = blur_ref[band]
        return weights(
            lax.dot_general(
                matrix,
                matrix,
                (((0,), (0,)), ((), ())),
                preferred_element_type=jnp.float32,
                precision=lax.Precision.HIGHEST,
            )
        )

    weight = [weight_of(band) for band in range(bands)]
    shift = PAD - span
    table_copy.wait()
    lags = [lags_of(0, 1.0)] + [lags_of(band, 0.5 / orients) for band in range(1, bands)]

    def chunk(index, carry):
        begin = index * step
        rows = filtered([axial_ref[0, begin + i] for i in range(step + 2 * span)], lags[0])
        product = narrow(wide_dot(jnp.concatenate(rows, axis=0), weight[0]))
        acc = [product[i * planes : (i + 1) * planes] for i in range(step)]
        for band in range(1, bands):
            rows = []
            patterns = []
            for orient in range(orients):
                pairs = [
                    harmonic_of(
                        table_ref[2 * orient, pl.ds(begin + i + shift, 1), :],
                        table_ref[2 * orient + 1, pl.ds(begin + i + shift, 1), :],
                        band,
                    )
                    for i in range(step + 2 * span)
                ]
                for part in range(2):
                    columns = [
                        pairs[i][part] * axial_ref[band, begin + i]
                        for i in range(step + 2 * span)
                    ]
                    rows += filtered(columns, lags[band])
                    patterns.append([pairs[i + span][part] for i in range(step)])
            product = narrow(wide_dot(jnp.concatenate(rows, axis=0), weight[band]))
            for which, pattern in enumerate(patterns):
                for i in range(step):
                    at = (which * step + i) * planes
                    acc[i] = acc[i] + pattern[i] * product[at : at + planes]
        for i in range(step):
            out_ref[begin + i] = acc[i]
        return carry

    lax.fori_loop(0, out_ref.shape[0] // step, chunk, 0)


def estimate_part(axial, table, row_blur, column_taps):
    _, extended, planes, row_count = axial.shape
    width = extended - 2 * (column_taps.shape[1] - 1)
    near = (table.shape[0], width + 2 * PAD, row_count)
    if width % 8:
        table = lax.dynamic_slice_in_dim(table, lax.axis_index("gz") * width, near[1], axis=1)
    smem = pl.BlockSpec(memory_space=pltpu.SMEM)
    vmem = pl.BlockSpec(memory_space=pltpu.VMEM)
    anywhere = pl.BlockSpec(memory_space=pltpu.HBM)
    rows = table.shape[0] * width * planes
    return pl.pallas_call(
        estimate_kernel,
        out_shape=jax.ShapeDtypeStruct((width, planes, row_count), jnp.float32),
        in_specs=[smem, vmem, anywhere, vmem],
        out_specs=vmem,
        scratch_shapes=[pltpu.VMEM(near, jnp.float32), pltpu.SemaphoreType.DMA],
        cost_estimate=pl.CostEstimate(
            flops=40 * rows * 2 * 256 * 256, bytes_accessed=axial.size * 4, transcendentals=0
        ),
        compiler_params=pltpu.CompilerParams(vmem_limit_bytes=40 << 20),
        name="estimate_part",
    )(column_taps, axial, table, row_blur)


def combine_kernel(adjoint_ref, estimate_ref, received_ref, out_ref):
    width, planes, row_count = estimate_ref.shape
    depth = adjoint_ref.shape[1]
    high, low = split(adjoint_ref[...])
    left_side = jnp.concatenate([high, high, low], axis=1)
    for index in range(0, width, 2):
        columns = [received_ref[pl.ds(index + i, depth, stride=width), :] for i in range(2)]
        high, low = split(jnp.concatenate(columns, axis=1))
        right_side = jnp.concatenate([high, low, high], axis=0)
        product = wide_dot(left_side, right_side)
        for i in range(2):
            out_ref[pl.ds(index + i, planes, stride=width), :] = (
                estimate_ref[index + i] + product[:, i * row_count : (i + 1) * row_count]
            )


def combine(forward, from_estimate, received):
    width, planes, row_count = from_estimate.shape
    depth = forward.shape[0] * planes
    adjoint = forward.transpose(2, 1, 0).reshape(planes, depth)
    vmem = pl.BlockSpec(memory_space=pltpu.VMEM)
    return pl.pallas_call(
        combine_kernel,
        out_shape=jax.ShapeDtypeStruct((planes * width, row_count), jnp.float32),
        in_specs=[vmem] * 3,
        out_specs=vmem,
        cost_estimate=pl.CostEstimate(
            flops=2 * received.size * planes, bytes_accessed=received.size * 4, transcendentals=0
        ),
        compiler_params=pltpu.CompilerParams(vmem_limit_bytes=24 << 20),
        name="combine",
    )(adjoint, from_estimate, received.reshape(depth * width, row_count)).reshape(
        planes, width, row_count
    )


def halo(estimate, span):
    ring = lax.axis_size("gz")
    width = estimate.shape[1]
    lefts, rights = [], []
    hop, missing = 1, span
    while missing > 0:
        take = min(missing, width)
        forth = [(s, (s + hop) % ring) for s in range(ring)]
        back = [(s, (s - hop) % ring) for s in range(ring)]
        lefts.insert(0, lax.ppermute(estimate[:, width - take :], "gz", forth))
        rights.append(lax.ppermute(estimate[:, :take], "gz", back))
        missing -= take
        hop += 1
    return lefts + [estimate] + rights


def axial_matrices(axial_otf, order):
    planes = order.shape[0]
    wrapped = np.arange(planes)[:, None] * np.arange(planes)[None, :] % planes
    angle = wrapped * (2.0 * math.pi / planes)
    cosine = np.cos(angle).astype(np.float32)
    sine = np.sin(angle).astype(np.float32)
    wrapped = order[:, None] * np.arange(planes, dtype=np.int32)[None, :] % planes
    angle = wrapped.astype(jnp.float32) * (2.0 * math.pi / planes)
    real = axial_otf[:, 0, :, None]
    imag = axial_otf[:, 1, :, None]
    inner = jnp.concatenate(
        [real * cosine + imag * sine, real * sine - imag * cosine], axis=1
    )
    both = jnp.concatenate([jnp.cos(angle), jnp.sin(angle)], axis=1) * (1.0 / planes)
    return jnp.einsum(
        "zk,mkw->mzw", both, inner, precision=lax.Precision.HIGHEST,
        preferred_element_type=jnp.float32,
    )


def by_permutes(ring):
    return ring <= 16 and ring & (ring - 1) == 0 and ring > 4


def exchange(sums):
    ring = lax.axis_size("gz")
    if len(sums) == 1:
        return lax.all_to_all(-sums[0], "gz", 0, 0, tiled=True)
    chip = lax.axis_index("gz") // 2
    mine, other = sums
    other = lax.ppermute(other, "gz", [(s, s ^ 1) for s in range(ring)])
    early = ring // 4
    first = lax.dynamic_index_in_dim(mine, chip ^ early, 0, keepdims=False)
    first = lax.optimization_barrier(-first)
    parts = []
    for bit in range(ring // 2):
        own = first
        if bit != early:
            own = -lax.dynamic_index_in_dim(mine, chip ^ bit, 0, keepdims=False)
        got = -lax.dynamic_index_in_dim(other, chip ^ bit, 0, keepdims=False)
        part = jnp.stack([own, got])
        if bit:
            part = lax.ppermute(part, "gz", [(s, s ^ (2 * bit)) for s in range(ring)])
        parts.append(part)
    return jnp.concatenate(parts, axis=0)


def shards(estimate, frames, phase_index, axial_otf, row_blur, column_taps):
    planes, width, row_count = estimate.shape
    ring = lax.axis_size("gz")
    orients = frames.shape[0]
    bands = row_blur.shape[0]
    span = column_taps.shape[1] - 1
    table = jnp.asarray(pattern_table(orients, width * ring, row_count, PAD))
    cores = 2 if by_permutes(ring) else 1
    sums = data_sums(frames, phase_index, row_blur, column_taps, table, ring, cores)
    estimate, *sums = lax.optimization_barrier((estimate, *sums))
    pieces = halo(estimate, span)
    received = exchange(sums)
    order = jnp.arange(planes, dtype=jnp.int32)
    if by_permutes(ring):
        order = order ^ lax.axis_index("gz")
    forward = axial_matrices(axial_otf, order)
    squared = jnp.einsum("mzw,mzv->mwv", forward, forward, precision=lax.Precision.HIGHEST)
    extended = jnp.concatenate(pieces, axis=1)
    axial = exact_dot(squared.reshape(bands * planes, planes), extended.reshape(planes, -1))
    axial = axial.reshape(bands, planes, width + 2 * span, row_count)
    axial = axial.transpose(0, 2, 1, 3)
    from_estimate = estimate_part(axial, table, row_blur, column_taps)
    return combine(forward, from_estimate, received)


def solution(mesh):
    placed = (P(None, "gz", "groups"), P(None, None, "gz", None, "groups"), P(), P(), P(), P())
    return jax.shard_map(
        shards, mesh=mesh, in_specs=placed, out_specs=P(None, "gz", "groups"), check_vma=False
    )
```

```python
import math

import jax
import jax.numpy as jnp
import numpy as np
from jax import lax
from jax.experimental import pallas as pl
from jax.experimental.pallas import tpu as pltpu
from jax.sharding import PartitionSpec as P


pattern_period = 3.7
orient_base = 0.3
data_scale = 1.0 / 1024.0
PAD = 8


def exact_dot(left_side, right_side):
    return jnp.dot(
        left_side, right_side, preferred_element_type=jnp.float32, precision=lax.Precision.HIGHEST
    )


def split(values):
    high = values.astype(jnp.bfloat16)
    low = (values - high.astype(jnp.float32)).astype(jnp.bfloat16)
    return high, low


def wide(values):
    high, low = split(values)
    return jnp.concatenate([high, low], axis=1)


def weights(matrix):
    row = wide(matrix)
    return jnp.concatenate([row, row], axis=0)


def narrow(product):
    half = product.shape[1] // 2
    return product[:, :half] + product[:, half:]


def wide_dot(left_side, right_side):
    return jnp.dot(left_side, right_side, preferred_element_type=jnp.float32)


def pattern_table(orients, loop_width, row_count, pad):
    columns = np.arange(-pad, loop_width + pad) % loop_width
    rows = np.arange(row_count)
    images = []
    for orient in range(orients):
        direction = orient_base + 2.0 * math.pi * orient / 3.0
        phase = (
            columns.astype(np.float32)[:, None] * np.float32(math.cos(direction))
            + rows.astype(np.float32)[None, :] * np.float32(math.sin(direction))
        ) * np.float32(2.0 * math.pi / pattern_period)
        images += [np.cos(phase.astype(np.float64)), np.sin(phase.astype(np.float64))]
    return np.stack(images).astype(np.float32)


def harmonic_of(cos_one, sin_one, harmonic):
    if harmonic == 1:
        return cos_one, sin_one
    return cos_one * cos_one - sin_one * sin_one, 2.0 * (sin_one * cos_one)


def blurred(mixed, image, taps, begin, step):
    reach = (len(taps) - 1) // 2
    acc = None
    for offset in range(-reach, reach + 1):
        term = taps[offset + reach] * mixed[image, pl.ds(begin + PAD - offset, step), :]
        acc = term if acc is None else acc + term
    return acc


def band_rows(mixed, images, taps, table, weight, band, begin, step):
    at = pl.ds(begin + (table.shape[1] - mixed.shape[1]) // 2 + PAD, step)
    parts = [wide(blurred(mixed, image, cut, begin, step)) for image, cut in zip(images, taps)]
    product = narrow(wide_dot(jnp.concatenate(parts, axis=0), weight))
    acc = None
    for orient in range(len(images) // 2):
        cos_pattern, sin_pattern = harmonic_of(
            table[2 * orient, at, :], table[2 * orient + 1, at, :], band
        )
        even = product[2 * orient * step : (2 * orient + 1) * step]
        odd = product[(2 * orient + 1) * step : (2 * orient + 2) * step]
        term = cos_pattern * even - sin_pattern * odd
        acc = term if acc is None else acc + term
    return acc


def put(out, index, band, values):
    width = out.shape[3]
    cores = out.shape[1]
    shares = values.shape[0] // width
    for share in range(shares):
        rows = values[share * width : (share + 1) * width]
        out[index * (shares // cores) + share // cores, share % cores, band] = rows


def scaled_taps(taps_ref, band, scale):
    return [taps_ref[band, at] * scale for at in range(taps_ref.shape[1])]


def data_kernel(
    phase_hbm, taps_hbm, frames_hbm, blur_hbm, table_hbm, *refs,
):
    targets, scratch = refs[:-12], refs[-12:]
    raw, summed, mixed, weight, table, blur_rows, out, phase_ref, taps_ref = scratch[:9]
    frame_sems, side_sems, out_sems = scratch[9:]

    orients, phases = raw.shape[0], raw.shape[1]
    loop_width = raw.shape[2]
    bands = out.shape[2]
    core = lax.axis_index("gz") % 2
    phase_copy = pltpu.make_async_copy(phase_hbm, phase_ref, side_sems.at[0])
    phase_copy.start()
    copies = []
    for orient in range(orients):
        row = []
        for index in range(phases):
            copy = pltpu.make_async_copy(
                frames_hbm.at[orient, index, 0],
                raw.at[orient, index],
                frame_sems.at[orient, index],
            )
            copy.start()
            row.append(copy)
        copies.append(row)
    taps_copy = pltpu.make_async_copy(taps_hbm, taps_ref, side_sems.at[1])
    taps_copy.start()
    blur_copy = pltpu.make_async_copy(blur_hbm, blur_rows, side_sems.at[2])
    blur_copy.start()
    table_copy = pltpu.make_async_copy(table_hbm, table, side_sems.at[3])
    table_copy.start()
    step = loop_width
    reach = (taps_ref.shape[1] - 1) // 2
    total = 4 * orients
    count = orients * phases
    first_sine, second_sine = math.sin(2 * math.pi / 5), math.sin(4 * math.pi / 5)
    ratio = second_sine / first_sine
    phase_copy.wait()
    for orient in range(orients):
        holder = []
        for step_index in range(phases):
            at_step = 0
            for index in range(1, phases):
                at_step = jnp.where(phase_ref[orient, index] == step_index, index, at_step)
            holder.append(at_step)
        for copy in copies[orient]:
            copy.wait()

        def mix(index, carry):
            rows = pl.ds(pl.multiple_of(index * step, step), step)
            at = pl.ds(pl.multiple_of(index * step + PAD, 8), step)
            f0, f1, f2, f3, f4 = [raw[orient, k, rows, :] for k in holder]
            near, far, near_odd, far_odd = f1 + f4, f2 + f3, f1 - f4, f2 - f3
            both = near + far
            even = (4 * f0 - both).astype(jnp.float32)
            swing = (near - far).astype(jnp.float32) * math.sqrt(5.0)
            near_odd = near_odd.astype(jnp.float32)
            far_odd = far_odd.astype(jnp.float32)
            mixed[2 * orient, at, :] = even + swing
            mixed[2 * orient + 1, at, :] = near_odd + ratio * far_odd
            mixed[2 * (orients + orient), at, :] = even - swing
            mixed[2 * (orients + orient) + 1, at, :] = ratio * near_odd - far_odd
            plain = f0 + both
            if orient:
                plain = plain + summed[rows, :]
            if orient < orients - 1:
                summed[rows, :] = plain
            else:
                mixed[total, at, :] = plain.astype(jnp.float32) * data_scale - 2.0 * count
            return carry

        lax.fori_loop(0, loop_width // step, mix, 0)
    for image in range(total + 1):
        mixed[image, PAD - reach : PAD, :] = mixed[
            image, loop_width + PAD - reach : loop_width + PAD, :
        ]
        mixed[image, loop_width + PAD : loop_width + PAD + reach, :] = mixed[
            image, PAD : PAD + reach, :
        ]
    taps_copy.wait()
    blur_copy.wait()
    for band in range(bands):
        weight[band] = weights(blur_rows[band])
    even_scale, odd_scale = data_scale / (4.0 * count), data_scale * first_sine / count
    taps = [scaled_taps(taps_ref, 0, 1.0 / count)]
    for band in range(1, bands):
        taps.append(
            [scaled_taps(taps_ref, band, even_scale), scaled_taps(taps_ref, band, odd_scale)]
            * orients
        )

    def plain_out(index, carry):
        begin = pl.multiple_of(index * step, step)
        rows = blurred(mixed, total, taps[0], begin, step)
        put(out, index, 0, narrow(wide_dot(wide(rows), weight[0])))
        return carry

    lax.fori_loop(0, loop_width // step, plain_out, 0)
    out_copies = []

    def ship(band):
        for at, target in enumerate(targets):
            half = (core + at) % 2 if len(targets) > 1 else 0
            copy = pltpu.make_async_copy(
                out.at[:, half, band], target.at[:, band], out_sems.at[at, band]
            )
            copy.start()
            out_copies.append(copy)

    ship(0)
    table_copy.wait()
    for band in range(1, bands):
        images = list(range(2 * orients * (band - 1), 2 * orients * band))

        def band_out(index, carry):
            begin = pl.multiple_of(index * step, step)
            put(
                out,
                index,
                band,
                band_rows(mixed, images, taps[band], table, weight[band], band, begin, step),
            )
            return carry

        lax.fori_loop(0, loop_width // step, band_out, 0)
        ship(band)
    for copy in out_copies:
        copy.wait()


def data_sums(frames, phase_index, row_blur, column_taps, table, chunks, cores):
    orients, phases, _, loop_width, row_count = frames.shape
    bands = row_blur.shape[0]
    width = loop_width // chunks
    anywhere = pl.BlockSpec(memory_space=pltpu.HBM)
    return pl.pallas_call(
        data_kernel,
        out_shape=[
            jax.ShapeDtypeStruct((chunks // cores, bands, width, row_count), jnp.float32)
        ]
        * cores,
        in_specs=[anywhere] * 5,
        out_specs=[anywhere] * cores,
        scratch_shapes=[
            pltpu.VMEM((orients, phases, loop_width, row_count), jnp.int32),
            pltpu.VMEM((loop_width, row_count), jnp.int32),
            pltpu.VMEM((4 * orients + 1, loop_width + 2 * PAD, row_count), jnp.float32),
            pltpu.VMEM((bands, 2 * row_count, 2 * row_count), jnp.bfloat16),
            pltpu.VMEM(table.shape, jnp.float32),
            pltpu.VMEM(row_blur.shape, jnp.float32),
            pltpu.VMEM((chunks // cores, cores, bands, width, row_count), jnp.float32),
            pltpu.SMEM(phase_index.shape, jnp.int32),
            pltpu.SMEM(column_taps.shape, jnp.float32),
            pltpu.SemaphoreType.DMA((orients, phases)),
            pltpu.SemaphoreType.DMA((4,)),
            pltpu.SemaphoreType.DMA((cores, bands)),
        ],
        cost_estimate=pl.CostEstimate(
            flops=13 * loop_width * 2 * 256 * 256, bytes_accessed=frames.size * 4, transcendentals=0
        ),
        compiler_params=pltpu.CompilerParams(vmem_limit_bytes=63 << 20),
        name="data_sums",
    )(phase_index, column_taps, frames, row_blur, table)


def estimate_kernel(taps_ref, axial_ref, table_hbm, blur_ref, out_ref, table_ref, sem):
    width = out_ref.shape[0]
    source = table_hbm
    if table_hbm.shape != table_ref.shape:
        begin = pl.multiple_of(lax.axis_index("gz") * width, 8)
        source = table_hbm.at[:, pl.ds(begin, table_ref.shape[1]), :]
    table_copy = pltpu.make_async_copy(source, table_ref, sem)
    table_copy.start()
    bands, _, planes, _ = axial_ref.shape
    orients = table_ref.shape[0] // 2
    reach = (taps_ref.shape[1] - 1) // 2
    span = 2 * reach
    step = max(d for d in range(1, 33) if out_ref.shape[0] % d == 0 and (d == 1 or d * planes <= 512))

    def lags_of(band, scale):
        return [
            scale
            * sum(
                taps_ref[band, d] * taps_ref[band, d + shift]
                for d in range(0, 2 * reach + 1 - shift)
            )
            for shift in range(span + 1)
        ]

    def filtered(columns, lags):
        rows = []
        for i in range(step):
            acc = lags[0] * columns[i + span]
            for shift in range(1, span + 1):
                acc = acc + lags[shift] * (columns[i + span - shift] + columns[i + span + shift])
            rows.append(wide(acc))
        return rows

    def weight_of(band):
        high, low = split(blur_ref[band])
        return weights(
            lax.dot_general(
                jnp.concatenate([high, high, low], axis=0),
                jnp.concatenate([high, low, high], axis=0),
                (((0,), (0,)), ((), ())),
                preferred_element_type=jnp.float32,
            )
        )

    weight = [weight_of(band) for band in range(bands)]
    shift = PAD - span
    table_copy.wait()
    lags = [lags_of(0, 1.0)] + [lags_of(band, 0.5 / orients) for band in range(1, bands)]

    def chunk(index, carry):
        begin = index * step
        rows = filtered([axial_ref[0, begin + i] for i in range(step + 2 * span)], lags[0])
        product = narrow(wide_dot(jnp.concatenate(rows, axis=0), weight[0]))
        acc = [product[i * planes : (i + 1) * planes] for i in range(step)]
        for band in range(1, bands):
            rows = []
            patterns = []
            for orient in range(orients):
                pairs = [
                    harmonic_of(
                        table_ref[2 * orient, pl.ds(begin + i + shift, 1), :],
                        table_ref[2 * orient + 1, pl.ds(begin + i + shift, 1), :],
                        band,
                    )
                    for i in range(step + 2 * span)
                ]
                for part in range(2):
                    columns = [
                        pairs[i][part] * axial_ref[band, begin + i]
                        for i in range(step + 2 * span)
                    ]
                    rows += filtered(columns, lags[band])
                    patterns.append([pairs[i + span][part] for i in range(step)])
            product = narrow(wide_dot(jnp.concatenate(rows, axis=0), weight[band]))
            for which, pattern in enumerate(patterns):
                for i in range(step):
                    at = (which * step + i) * planes
                    acc[i] = acc[i] + pattern[i] * product[at : at + planes]
        for i in range(step):
            out_ref[begin + i] = acc[i]
        return carry

    lax.fori_loop(0, out_ref.shape[0] // step, chunk, 0)


def estimate_part(axial, table, row_blur, column_taps):
    _, extended, planes, row_count = axial.shape
    width = extended - 2 * (column_taps.shape[1] - 1)
    near = (table.shape[0], width + 2 * PAD, row_count)
    if width % 8:
        table = lax.dynamic_slice_in_dim(table, lax.axis_index("gz") * width, near[1], axis=1)
    smem = pl.BlockSpec(memory_space=pltpu.SMEM)
    vmem = pl.BlockSpec(memory_space=pltpu.VMEM)
    anywhere = pl.BlockSpec(memory_space=pltpu.HBM)
    rows = table.shape[0] * width * planes
    return pl.pallas_call(
        estimate_kernel,
        out_shape=jax.ShapeDtypeStruct((width, planes, row_count), jnp.float32),
        in_specs=[smem, vmem, anywhere, vmem],
        out_specs=vmem,
        scratch_shapes=[pltpu.VMEM(near, jnp.float32), pltpu.SemaphoreType.DMA],
        cost_estimate=pl.CostEstimate(
            flops=40 * rows * 2 * 256 * 256, bytes_accessed=axial.size * 4, transcendentals=0
        ),
        compiler_params=pltpu.CompilerParams(vmem_limit_bytes=40 << 20),
        name="estimate_part",
    )(column_taps, axial, table, row_blur)


def combine_kernel(adjoint_ref, estimate_ref, received_ref, out_ref):
    width, planes, row_count = estimate_ref.shape
    depth = adjoint_ref.shape[1]
    high, low = split(adjoint_ref[...])
    left_side = jnp.concatenate(
        [jnp.concatenate([high, high], axis=1), jnp.concatenate([low, low], axis=1)], axis=0
    )
    for index in range(0, width, 2):
        columns = [received_ref[pl.ds(index + i, depth, stride=width), :] for i in range(2)]
        high, low = split(jnp.concatenate(columns, axis=1))
        product = wide_dot(left_side, jnp.concatenate([high, low], axis=0))
        product = product[:planes] + product[planes:]
        for i in range(2):
            out_ref[pl.ds(index + i, planes, stride=width), :] = (
                estimate_ref[index + i] + product[:, i * row_count : (i + 1) * row_count]
            )


def combine(forward, from_estimate, received):
    width, planes, row_count = from_estimate.shape
    depth = forward.shape[0] * planes
    adjoint = forward.transpose(2, 1, 0).reshape(planes, depth)
    vmem = pl.BlockSpec(memory_space=pltpu.VMEM)
    return pl.pallas_call(
        combine_kernel,
        out_shape=jax.ShapeDtypeStruct((planes * width, row_count), jnp.float32),
        in_specs=[vmem] * 3,
        out_specs=vmem,
        cost_estimate=pl.CostEstimate(
            flops=2 * received.size * planes, bytes_accessed=received.size * 4, transcendentals=0
        ),
        compiler_params=pltpu.CompilerParams(vmem_limit_bytes=24 << 20),
        name="combine",
    )(adjoint, from_estimate, received.reshape(depth * width, row_count)).reshape(
        planes, width, row_count
    )


def halo(estimate, span):
    ring = lax.axis_size("gz")
    width = estimate.shape[1]
    lefts, rights = [], []
    hop, missing = 1, span
    while missing > 0:
        take = min(missing, width)
        forth = [(s, (s + hop) % ring) for s in range(ring)]
        back = [(s, (s - hop) % ring) for s in range(ring)]
        lefts.insert(0, lax.ppermute(estimate[:, width - take :], "gz", forth))
        rights.append(lax.ppermute(estimate[:, :take], "gz", back))
        missing -= take
        hop += 1
    return lefts + [estimate] + rights


def axial_matrices(axial_otf, order):
    planes = order.shape[0]
    wrapped = np.arange(planes)[:, None] * np.arange(planes)[None, :] % planes
    angle = wrapped * (2.0 * math.pi / planes)
    cosine = np.cos(angle).astype(np.float32)
    sine = np.sin(angle).astype(np.float32)
    wrapped = order[:, None] * np.arange(planes, dtype=np.int32)[None, :] % planes
    angle = wrapped.astype(jnp.float32) * (2.0 * math.pi / planes)
    real = axial_otf[:, 0, :, None]
    imag = axial_otf[:, 1, :, None]
    inner = jnp.concatenate(
        [real * cosine + imag * sine, real * sine - imag * cosine], axis=1
    )
    both = jnp.concatenate([jnp.cos(angle), jnp.sin(angle)], axis=1) * (1.0 / planes)
    return jnp.einsum(
        "zk,mkw->mzw", both, inner, precision=lax.Precision.HIGHEST,
        preferred_element_type=jnp.float32,
    )


def by_permutes(ring):
    return ring <= 16 and ring & (ring - 1) == 0 and ring > 4


def exchange(sums):
    ring = lax.axis_size("gz")
    if len(sums) == 1:
        return lax.all_to_all(-sums[0], "gz", 0, 0, tiled=True)
    chip = lax.axis_index("gz") // 2
    mine, other = sums
    other = lax.ppermute(other, "gz", [(s, s ^ 1) for s in range(ring)])
    early = ring // 4
    first = lax.dynamic_index_in_dim(mine, chip ^ early, 0, keepdims=False)
    first = lax.optimization_barrier(-first)
    parts = []
    for bit in range(ring // 2):
        own = first
        if bit != early:
            own = -lax.dynamic_index_in_dim(mine, chip ^ bit, 0, keepdims=False)
        got = -lax.dynamic_index_in_dim(other, chip ^ bit, 0, keepdims=False)
        part = jnp.stack([own, got])
        if bit:
            part = lax.ppermute(part, "gz", [(s, s ^ (2 * bit)) for s in range(ring)])
        parts.append(part)
    return jnp.concatenate(parts, axis=0)


def shards(estimate, frames, phase_index, axial_otf, row_blur, column_taps):
    planes, width, row_count = estimate.shape
    ring = lax.axis_size("gz")
    orients = frames.shape[0]
    bands = row_blur.shape[0]
    span = column_taps.shape[1] - 1
    table = jnp.asarray(pattern_table(orients, width * ring, row_count, PAD))
    cores = 2 if by_permutes(ring) else 1
    sums = data_sums(frames, phase_index, row_blur, column_taps, table, ring, cores)
    estimate, *sums = lax.optimization_barrier((estimate, *sums))
    pieces = halo(estimate, span)
    received = exchange(sums)
    order = jnp.arange(planes, dtype=jnp.int32)
    if by_permutes(ring):
        order = order ^ lax.axis_index("gz")
    forward = axial_matrices(axial_otf, order)
    squared = jnp.einsum("mzw,mzv->mwv", forward, forward, precision=lax.Precision.HIGHEST)
    extended = jnp.concatenate(pieces, axis=1)
    axial = exact_dot(squared.reshape(bands * planes, planes), extended.reshape(planes, -1))
    axial = axial.reshape(bands, planes, width + 2 * span, row_count)
    axial = axial.transpose(0, 2, 1, 3)
    from_estimate = estimate_part(axial, table, row_blur, column_taps)
    return combine(forward, from_estimate, received)


def solution(mesh):
    placed = (P(None, "gz", "groups"), P(None, None, "gz", None, "groups"), P(), P(), P(), P())
    return jax.shard_map(
        shards, mesh=mesh, in_specs=placed, out_specs=P(None, "gz", "groups"), check_vma=False
    )
```

```python
import math

import jax
import jax.numpy as jnp
import numpy as np
from jax import lax
from jax.experimental import pallas as pl
from jax.experimental.pallas import tpu as pltpu
from jax.sharding import PartitionSpec as P


pattern_period = 3.7
orient_base = 0.3
data_scale = 1.0 / 1024.0
PAD = 8


def exact_dot(left_side, right_side):
    return jnp.dot(
        left_side, right_side, preferred_element_type=jnp.float32, precision=lax.Precision.HIGHEST
    )


def split(values):
    high = values.astype(jnp.bfloat16)
    low = (values - high.astype(jnp.float32)).astype(jnp.bfloat16)
    return high, low


def wide(values):
    high, low = split(values)
    return jnp.concatenate([high, low], axis=1)


def weights(matrix):
    row = wide(matrix)
    return jnp.concatenate([row, row], axis=0)


def narrow(product):
    half = product.shape[1] // 2
    return product[:, :half] + product[:, half:]


def wide_dot(left_side, right_side):
    return jnp.dot(left_side, right_side, preferred_element_type=jnp.float32)


def pattern_table(orients, loop_width, row_count, pad):
    columns = np.arange(-pad, loop_width + pad) % loop_width
    rows = np.arange(row_count)
    images = []
    for orient in range(orients):
        direction = orient_base + 2.0 * math.pi * orient / 3.0
        phase = (
            columns.astype(np.float32)[:, None] * np.float32(math.cos(direction))
            + rows.astype(np.float32)[None, :] * np.float32(math.sin(direction))
        ) * np.float32(2.0 * math.pi / pattern_period)
        images += [np.cos(phase.astype(np.float64)), np.sin(phase.astype(np.float64))]
    return np.stack(images).astype(np.float32)


def harmonic_of(cos_one, sin_one, harmonic):
    if harmonic == 1:
        return cos_one, sin_one
    return cos_one * cos_one - sin_one * sin_one, 2.0 * (sin_one * cos_one)


def blurred(mixed, image, taps, begin, step):
    reach = (len(taps) - 1) // 2
    acc = None
    for offset in range(-reach, reach + 1):
        term = taps[offset + reach] * mixed[image, pl.ds(begin + PAD - offset, step), :]
        acc = term if acc is None else acc + term
    return acc


def band_rows(mixed, images, taps, table, weight, band, begin, step):
    at = pl.ds(begin + (table.shape[1] - mixed.shape[1]) // 2 + PAD, step)
    parts = [wide(blurred(mixed, image, cut, begin, step)) for image, cut in zip(images, taps)]
    product = narrow(wide_dot(jnp.concatenate(parts, axis=0), weight))
    acc = None
    for orient in range(len(images) // 2):
        cos_pattern, sin_pattern = harmonic_of(
            table[2 * orient, at, :], table[2 * orient + 1, at, :], band
        )
        even = product[2 * orient * step : (2 * orient + 1) * step]
        odd = product[(2 * orient + 1) * step : (2 * orient + 2) * step]
        term = cos_pattern * even - sin_pattern * odd
        acc = term if acc is None else acc + term
    return acc


def put(out, index, band, values):
    width = out.shape[3]
    cores = out.shape[1]
    shares = values.shape[0] // width
    for share in range(shares):
        rows = values[share * width : (share + 1) * width]
        out[index * (shares // cores) + share // cores, share % cores, band] = rows


def scaled_taps(taps_ref, band, scale):
    return [taps_ref[band, at] * scale for at in range(taps_ref.shape[1])]


def data_kernel(
    phase_hbm, taps_hbm, frames_hbm, blur_hbm, table_hbm, *refs,
):
    targets, scratch = refs[:-12], refs[-12:]
    raw, summed, mixed, weight, table, blur_rows, out, phase_ref, taps_ref = scratch[:9]
    frame_sems, side_sems, out_sems = scratch[9:]

    orients, phases = raw.shape[0], raw.shape[1]
    loop_width = raw.shape[2]
    bands = out.shape[2]
    core = lax.axis_index("gz") % 2
    phase_copy = pltpu.make_async_copy(phase_hbm, phase_ref, side_sems.at[0])
    phase_copy.start()
    copies = []
    for orient in range(orients):
        row = []
        for index in range(phases):
            copy = pltpu.make_async_copy(
                frames_hbm.at[orient, index, 0],
                raw.at[orient, index],
                frame_sems.at[orient, index],
            )
            copy.start()
            row.append(copy)
        copies.append(row)
    taps_copy = pltpu.make_async_copy(taps_hbm, taps_ref, side_sems.at[1])
    taps_copy.start()
    blur_copy = pltpu.make_async_copy(blur_hbm, blur_rows, side_sems.at[2])
    blur_copy.start()
    table_copy = pltpu.make_async_copy(table_hbm, table, side_sems.at[3])
    table_copy.start()
    step = loop_width
    reach = (taps_ref.shape[1] - 1) // 2
    total = 4 * orients
    count = orients * phases
    first_sine, second_sine = math.sin(2 * math.pi / 5), math.sin(4 * math.pi / 5)
    ratio = second_sine / first_sine
    phase_copy.wait()
    for orient in range(orients):
        holder = []
        for step_index in range(phases):
            at_step = 0
            for index in range(1, phases):
                at_step = jnp.where(phase_ref[orient, index] == step_index, index, at_step)
            holder.append(at_step)
        for copy in copies[orient]:
            copy.wait()

        def mix(index, carry):
            rows = pl.ds(pl.multiple_of(index * step, step), step)
            at = pl.ds(pl.multiple_of(index * step + PAD, 8), step)
            f0, f1, f2, f3, f4 = [raw[orient, k, rows, :] for k in holder]
            near, far, near_odd, far_odd = f1 + f4, f2 + f3, f1 - f4, f2 - f3
            both = near + far
            even = (4 * f0 - both).astype(jnp.float32)
            swing = (near - far).astype(jnp.float32) * math.sqrt(5.0)
            near_odd = near_odd.astype(jnp.float32)
            far_odd = far_odd.astype(jnp.float32)
            mixed[2 * orient, at, :] = even + swing
            mixed[2 * orient + 1, at, :] = near_odd + ratio * far_odd
            mixed[2 * (orients + orient), at, :] = even - swing
            mixed[2 * (orients + orient) + 1, at, :] = ratio * near_odd - far_odd
            plain = f0 + both
            if orient:
                plain = plain + summed[rows, :]
            if orient < orients - 1:
                summed[rows, :] = plain
            else:
                mixed[total, at, :] = plain.astype(jnp.float32) * data_scale - 2.0 * count
            return carry

        lax.fori_loop(0, loop_width // step, mix, 0)
    for image in range(total + 1):
        mixed[image, PAD - reach : PAD, :] = mixed[
            image, loop_width + PAD - reach : loop_width + PAD, :
        ]
        mixed[image, loop_width + PAD : loop_width + PAD + reach, :] = mixed[
            image, PAD : PAD + reach, :
        ]
    taps_copy.wait()
    blur_copy.wait()
    for band in range(bands):
        weight[band] = weights(blur_rows[band])
    even_scale, odd_scale = data_scale / (4.0 * count), data_scale * first_sine / count
    taps = [scaled_taps(taps_ref, 0, 1.0 / count)]
    for band in range(1, bands):
        taps.append(
            [scaled_taps(taps_ref, band, even_scale), scaled_taps(taps_ref, band, odd_scale)]
            * orients
        )

    def plain_out(index, carry):
        begin = pl.multiple_of(index * step, step)
        rows = blurred(mixed, total, taps[0], begin, step)
        put(out, index, 0, narrow(wide_dot(wide(rows), weight[0])))
        return carry

    lax.fori_loop(0, loop_width // step, plain_out, 0)
    out_copies = []

    def ship(band):
        for at, target in enumerate(targets):
            half = (core + at) % 2 if len(targets) > 1 else 0
            copy = pltpu.make_async_copy(
                out.at[:, half, band], target.at[:, band], out_sems.at[at, band]
            )
            copy.start()
            out_copies.append(copy)

    ship(0)
    table_copy.wait()
    for band in range(1, bands):
        images = list(range(2 * orients * (band - 1), 2 * orients * band))

        def band_out(index, carry):
            begin = pl.multiple_of(index * step, step)
            put(
                out,
                index,
                band,
                band_rows(mixed, images, taps[band], table, weight[band], band, begin, step),
            )
            return carry

        lax.fori_loop(0, loop_width // step, band_out, 0)
        ship(band)
    for copy in out_copies:
        copy.wait()


def data_sums(frames, phase_index, row_blur, column_taps, table, chunks, cores):
    orients, phases, _, loop_width, row_count = frames.shape
    bands = row_blur.shape[0]
    width = loop_width // chunks
    anywhere = pl.BlockSpec(memory_space=pltpu.HBM)
    return pl.pallas_call(
        data_kernel,
        out_shape=[
            jax.ShapeDtypeStruct((chunks // cores, bands, width, row_count), jnp.float32)
        ]
        * cores,
        in_specs=[anywhere] * 5,
        out_specs=[anywhere] * cores,
        scratch_shapes=[
            pltpu.VMEM((orients, phases, loop_width, row_count), jnp.int32),
            pltpu.VMEM((loop_width, row_count), jnp.int32),
            pltpu.VMEM((4 * orients + 1, loop_width + 2 * PAD, row_count), jnp.float32),
            pltpu.VMEM((bands, 2 * row_count, 2 * row_count), jnp.bfloat16),
            pltpu.VMEM(table.shape, jnp.float32),
            pltpu.VMEM(row_blur.shape, jnp.float32),
            pltpu.VMEM((chunks // cores, cores, bands, width, row_count), jnp.float32),
            pltpu.SMEM(phase_index.shape, jnp.int32),
            pltpu.SMEM(column_taps.shape, jnp.float32),
            pltpu.SemaphoreType.DMA((orients, phases)),
            pltpu.SemaphoreType.DMA((4,)),
            pltpu.SemaphoreType.DMA((cores, bands)),
        ],
        cost_estimate=pl.CostEstimate(
            flops=13 * loop_width * 2 * 256 * 256, bytes_accessed=frames.size * 4, transcendentals=0
        ),
        compiler_params=pltpu.CompilerParams(vmem_limit_bytes=63 << 20),
        name="data_sums",
    )(phase_index, column_taps, frames, row_blur, table)


def estimate_kernel(taps_ref, axial_ref, table_hbm, blur_ref, out_ref, table_ref, sem):
    width = out_ref.shape[0]
    source = table_hbm
    if table_hbm.shape != table_ref.shape:
        begin = pl.multiple_of(lax.axis_index("gz") * width, 8)
        source = table_hbm.at[:, pl.ds(begin, table_ref.shape[1]), :]
    table_copy = pltpu.make_async_copy(source, table_ref, sem)
    table_copy.start()
    bands, _, planes, _ = axial_ref.shape
    orients = table_ref.shape[0] // 2
    reach = (taps_ref.shape[1] - 1) // 2
    span = 2 * reach
    step = max(d for d in range(1, 33) if out_ref.shape[0] % d == 0 and (d == 1 or d * planes <= 512))

    def lags_of(band, scale):
        return [
            scale
            * sum(
                taps_ref[band, d] * taps_ref[band, d + shift]
                for d in range(0, 2 * reach + 1 - shift)
            )
            for shift in range(span + 1)
        ]

    def filtered(columns, lags):
        rows = []
        for i in range(step):
            acc = lags[0] * columns[i + span]
            for shift in range(1, span + 1):
                acc = acc + lags[shift] * (columns[i + span - shift] + columns[i + span + shift])
            rows.append(wide(acc))
        return rows

    def weight_of(band):
        high, low = split(blur_ref[band])
        return weights(
            lax.dot_general(
                jnp.concatenate([high, high, low], axis=0),
                jnp.concatenate([high, low, high], axis=0),
                (((0,), (0,)), ((), ())),
                preferred_element_type=jnp.float32,
            )
        )

    weight = [weight_of(band) for band in range(bands)]
    shift = PAD - span
    table_copy.wait()
    lags = [lags_of(0, 1.0)] + [lags_of(band, 0.5 / orients) for band in range(1, bands)]

    def chunk(index, carry):
        begin = index * step
        rows = filtered([axial_ref[0, begin + i] for i in range(step + 2 * span)], lags[0])
        product = narrow(wide_dot(jnp.concatenate(rows, axis=0), weight[0]))
        acc = [product[i * planes : (i + 1) * planes] for i in range(step)]
        for band in range(1, bands):
            rows = []
            patterns = []
            for orient in range(orients):
                pairs = [
                    harmonic_of(
                        table_ref[2 * orient, pl.ds(begin + i + shift, 1), :],
                        table_ref[2 * orient + 1, pl.ds(begin + i + shift, 1), :],
                        band,
                    )
                    for i in range(step + 2 * span)
                ]
                for part in range(2):
                    columns = [
                        pairs[i][part] * axial_ref[band, begin + i]
                        for i in range(step + 2 * span)
                    ]
                    rows += filtered(columns, lags[band])
                    patterns.append([pairs[i + span][part] for i in range(step)])
            product = narrow(wide_dot(jnp.concatenate(rows, axis=0), weight[band]))
            for which, pattern in enumerate(patterns):
                for i in range(step):
                    at = (which * step + i) * planes
                    acc[i] = acc[i] + pattern[i] * product[at : at + planes]
        for i in range(step):
            out_ref[begin + i] = acc[i]
        return carry

    lax.fori_loop(0, out_ref.shape[0] // step, chunk, 0)


def estimate_part(axial, table, row_blur, column_taps):
    _, extended, planes, row_count = axial.shape
    width = extended - 2 * (column_taps.shape[1] - 1)
    near = (table.shape[0], width + 2 * PAD, row_count)
    if width % 8:
        table = lax.dynamic_slice_in_dim(table, lax.axis_index("gz") * width, near[1], axis=1)
    smem = pl.BlockSpec(memory_space=pltpu.SMEM)
    vmem = pl.BlockSpec(memory_space=pltpu.VMEM)
    anywhere = pl.BlockSpec(memory_space=pltpu.HBM)
    rows = table.shape[0] * width * planes
    return pl.pallas_call(
        estimate_kernel,
        out_shape=jax.ShapeDtypeStruct((width, planes, row_count), jnp.float32),
        in_specs=[smem, vmem, anywhere, vmem],
        out_specs=vmem,
        scratch_shapes=[pltpu.VMEM(near, jnp.float32), pltpu.SemaphoreType.DMA],
        cost_estimate=pl.CostEstimate(
            flops=40 * rows * 2 * 256 * 256, bytes_accessed=axial.size * 4, transcendentals=0
        ),
        compiler_params=pltpu.CompilerParams(vmem_limit_bytes=40 << 20),
        name="estimate_part",
    )(column_taps, axial, table, row_blur)


def combine_kernel(adjoint_ref, estimate_ref, received_ref, out_ref):
    width, planes, row_count = estimate_ref.shape
    depth = adjoint_ref.shape[1]
    high, low = split(adjoint_ref[...])
    left_side = jnp.concatenate([high, high, low], axis=1)
    for index in range(0, width, 2):
        columns = [received_ref[pl.ds(index + i, depth, stride=width), :] for i in range(2)]
        high, low = split(jnp.concatenate(columns, axis=1))
        right_side = jnp.concatenate([high, low, high], axis=0)
        product = wide_dot(left_side, right_side)
        for i in range(2):
            out_ref[pl.ds(index + i, planes, stride=width), :] = (
                estimate_ref[index + i] + product[:, i * row_count : (i + 1) * row_count]
            )


def combine(forward, from_estimate, received):
    width, planes, row_count = from_estimate.shape
    depth = forward.shape[0] * planes
    adjoint = forward.transpose(2, 1, 0).reshape(planes, depth)
    vmem = pl.BlockSpec(memory_space=pltpu.VMEM)
    return pl.pallas_call(
        combine_kernel,
        out_shape=jax.ShapeDtypeStruct((planes * width, row_count), jnp.float32),
        in_specs=[vmem] * 3,
        out_specs=vmem,
        cost_estimate=pl.CostEstimate(
            flops=2 * received.size * planes, bytes_accessed=received.size * 4, transcendentals=0
        ),
        compiler_params=pltpu.CompilerParams(vmem_limit_bytes=24 << 20),
        name="combine",
    )(adjoint, from_estimate, received.reshape(depth * width, row_count)).reshape(
        planes, width, row_count
    )


def halo(estimate, span):
    ring = lax.axis_size("gz")
    width = estimate.shape[1]
    lefts, rights = [], []
    hop, missing = 1, span
    while missing > 0:
        take = min(missing, width)
        forth = [(s, (s + hop) % ring) for s in range(ring)]
        back = [(s, (s - hop) % ring) for s in range(ring)]
        lefts.insert(0, lax.ppermute(estimate[:, width - take :], "gz", forth))
        rights.append(lax.ppermute(estimate[:, :take], "gz", back))
        missing -= take
        hop += 1
    return lefts + [estimate] + rights


def axial_matrices(axial_otf, order):
    planes = order.shape[0]
    wrapped = np.arange(planes)[:, None] * np.arange(planes)[None, :] % planes
    angle = wrapped * (2.0 * math.pi / planes)
    cosine = np.cos(angle).astype(np.float32)
    sine = np.sin(angle).astype(np.float32)
    wrapped = order[:, None] * np.arange(planes, dtype=np.int32)[None, :] % planes
    angle = wrapped.astype(jnp.float32) * (2.0 * math.pi / planes)
    real = axial_otf[:, 0, :, None]
    imag = axial_otf[:, 1, :, None]
    inner = jnp.concatenate(
        [real * cosine + imag * sine, real * sine - imag * cosine], axis=1
    )
    both = jnp.concatenate([jnp.cos(angle), jnp.sin(angle)], axis=1) * (1.0 / planes)
    return jnp.einsum(
        "zk,mkw->mzw", both, inner, precision=lax.Precision.HIGHEST,
        preferred_element_type=jnp.float32,
    )


def by_permutes(ring):
    return ring <= 16 and ring & (ring - 1) == 0 and ring > 4


def exchange(sums):
    ring = lax.axis_size("gz")
    if len(sums) == 1:
        return lax.all_to_all(-sums[0], "gz", 0, 0, tiled=True)
    chip = lax.axis_index("gz") // 2
    mine, other = sums
    other = lax.ppermute(other, "gz", [(s, s ^ 1) for s in range(ring)])
    early = ring // 4
    first = lax.dynamic_index_in_dim(mine, chip ^ early, 0, keepdims=False)
    first = lax.optimization_barrier(-first)
    parts = []
    for bit in range(ring // 2):
        own = first
        if bit != early:
            own = -lax.dynamic_index_in_dim(mine, chip ^ bit, 0, keepdims=False)
        got = -lax.dynamic_index_in_dim(other, chip ^ bit, 0, keepdims=False)
        part = jnp.stack([own, got])
        if bit:
            part = lax.ppermute(part, "gz", [(s, s ^ (2 * bit)) for s in range(ring)])
        parts.append(part)
    return jnp.concatenate(parts, axis=0)


def shards(estimate, frames, phase_index, axial_otf, row_blur, column_taps):
    planes, width, row_count = estimate.shape
    ring = lax.axis_size("gz")
    orients = frames.shape[0]
    bands = row_blur.shape[0]
    span = column_taps.shape[1] - 1
    table = jnp.asarray(pattern_table(orients, width * ring, row_count, PAD))
    cores = 2 if by_permutes(ring) else 1
    sums = data_sums(frames, phase_index, row_blur, column_taps, table, ring, cores)
    estimate, *sums = lax.optimization_barrier((estimate, *sums))
    pieces = halo(estimate, span)
    received = exchange(sums)
    order = jnp.arange(planes, dtype=jnp.int32)
    if by_permutes(ring):
        order = order ^ lax.axis_index("gz")
    forward = axial_matrices(axial_otf, order)
    squared = jnp.einsum("mzw,mzv->mwv", forward, forward, precision=lax.Precision.HIGHEST)
    extended = jnp.concatenate(pieces, axis=1)
    axial = exact_dot(squared.reshape(bands * planes, planes), extended.reshape(planes, -1))
    axial = axial.reshape(bands, planes, width + 2 * span, row_count)
    axial = axial.transpose(0, 2, 1, 3)
    from_estimate = estimate_part(axial, table, row_blur, column_taps)
    return combine(forward, from_estimate, received)


def solution(mesh):
    placed = (P(None, "gz", "groups"), P(None, None, "gz", None, "groups"), P(), P(), P(), P())
    return jax.shard_map(
        shards, mesh=mesh, in_specs=placed, out_specs=P(None, "gz", "groups"), check_vma=False
    )
```
